32 devices in a mesh: gx: 8 (over z, y), ha: 4 (over x, core).
Axes of the slice: x: 2, y: 2, z: 4, core: 2. Of those that a mesh axis runs over, the one named last changes fastest.
Arguments:
- value_field: float32 [8, 32, 16, 16], P('ha', None, 'gx'), may hold values from -6 to 6
- avoid_field: float32 [8, 32, 16, 16], P('ha', None, 'gx'), may hold values from -6 to 6
- sample_adjoint: float32 [8, 4, 8, 128], P('gx', 'ha'), may hold values from -6 to 6
- offset_y: float32 [8, 4, 8, 128], P('gx', 'ha'), may hold values from 0 to 1
- offset_s: float32 [8, 4, 8, 128], P('gx', 'ha'), may hold values from 0 to 1
- start_xy: int32 [8, 4, 8, 128], P('gx', 'ha'), may hold values from 0 to 30, as said below
- start_hs: int32 [8, 4, 8, 128], P('gx', 'ha'), may hold values from 0 to 62, as said below
- send_counts: int32 [8, 4, 8], P('gx', 'ha'), may hold values from 16 to 128, as said below
Outputs:
- next_value: float32 [8, 32, 16, 16], P('ha', None, 'gx')
- value_grad: float32 [8, 32, 16, 16], P('ha', None, 'gx')
- avoid_grad: float32 [8, 32, 16, 16], P('ha', None, 'gx')
The draws below stay inside these ranges and needn't reach their ends.
Inputs may be any that keep to these rules, and one draw needn't show every extreme that they name: `start_xy`: the y cell of a start is at most 14. `start_hs`: the speed cell of a start is at most 30. `send_counts`: the live slots of a row are its first ones. For each index along ha, one owner drawn from the seed gets all 128 slots live from every sender.
All inputs are finite; a program needn't handle non-finite values.
Results may differ from the reference program's by a relative error of at most 0.00002.
Values sent between devices are 32-bit elements; how exact they have to be, the bound alone decides.
A program may use at most 64 MiB of HBM per device.

```python
import math
import jax
import jax.numpy as jnp
from jax import lax

CX = 2
CH = 2
NS = 32
CAP = 128
ROWGROUPS = 8
HEADGROUPS = 4
NX = 16
NY = 16
NH = 8


def draw_start_xy(key, part):
    first_key, second_key = jax.random.split(jax.random.fold_in(key, 11))
    shape_all = (ROWGROUPS, HEADGROUPS, ROWGROUPS, CAP)
    row_cells = jax.random.randint(first_key, shape_all, 0, CX)
    col_cells = jax.random.randint(second_key, shape_all, 0, NY - 1)
    return (row_cells * NY + col_cells).astype(jnp.int32)


def draw_start_hs(key, part):
    first_key, second_key = jax.random.split(jax.random.fold_in(key, 23))
    shape_all = (ROWGROUPS, HEADGROUPS, ROWGROUPS, CAP)
    head_cells = jax.random.randint(first_key, shape_all, 0, CH)
    speed_cells = jax.random.randint(second_key, shape_all, 0, NS - 1)
    return (head_cells * NS + speed_cells).astype(jnp.int32)


def draw_send_counts(key, part):
    first_key, second_key = jax.random.split(jax.random.fold_in(key, 37))
    shape_all = (ROWGROUPS, HEADGROUPS, ROWGROUPS)
    counts = jax.random.randint(first_key, shape_all, CAP // 8, 3 * CAP // 4 + 1)
    busiest = jax.random.randint(second_key, (HEADGROUPS,), 0, ROWGROUPS)
    owner_index = jnp.arange(ROWGROUPS, dtype=jnp.int32)[None, None, :]
    filled = owner_index == busiest[None, :, None]
    return jnp.where(filled, CAP, counts).astype(jnp.int32)


def shard_levels(stream_key, extent, cuts, least, high):
    def one(dim, shards_of):
        steps = jax.random.uniform(jax.random.fold_in(jax.random.fold_in(stream_key, 6), dim), (shards_of,), jnp.float32, least / len(cuts), high / len(cuts))
        return jnp.repeat(jnp.exp(steps), extent[dim] // shards_of).reshape((-1,) + (1,) * (len(extent) - dim - 1))

    factor_of = one(*cuts[0])
    for cut in cuts[1:]:
        factor_of = factor_of * one(*cut)
    return factor_of


def noise(key, shape, scale, reach, cuts=(), held_as=jnp.bfloat16):
    loudness = shard_levels(key, shape, cuts, -0.22, 0.18) if cuts else 1.0
    array = jax.random.normal(key, shape, jnp.float32) * scale * loudness
    return jnp.minimum(jnp.maximum(array, -reach), reach).astype(held_as)


def setup_inputs(seed: int = 0) -> dict:
    streams_of = jax.random.split(jax.random.key(seed), 9)
    value_field = noise(streams_of[0], (NH, NS, NX, NY), 1.0, 6.0, ((0, 4), (2, 8)), jnp.float32)
    avoid_field = noise(streams_of[1], (NH, NS, NX, NY), 1.0, 6.0, ((0, 4), (2, 8)), jnp.float32)
    sample_adjoint = noise(streams_of[2], (ROWGROUPS, HEADGROUPS, ROWGROUPS, CAP), 1.0, 6.0, ((0, 8), (1, 4)), jnp.float32)
    offset_y = jnp.clip(1.0 * jax.random.uniform(streams_of[3], (ROWGROUPS, HEADGROUPS, ROWGROUPS, CAP), jnp.float32) ** shard_levels(streams_of[3], (ROWGROUPS, HEADGROUPS, ROWGROUPS, CAP), ((0, 8), (1, 4)), -0.2, 0.2), 0.0, 1.0)
    offset_s = jnp.clip(1.0 * jax.random.uniform(streams_of[4], (ROWGROUPS, HEADGROUPS, ROWGROUPS, CAP), jnp.float32) ** shard_levels(streams_of[4], (ROWGROUPS, HEADGROUPS, ROWGROUPS, CAP), ((0, 8), (1, 4)), -0.2, 0.2), 0.0, 1.0)
    start_xy = draw_start_xy(jax.random.fold_in(streams_of[8], 71), 0)
    start_hs = draw_start_hs(jax.random.fold_in(streams_of[8], 71), 0)
    send_counts = draw_send_counts(jax.random.fold_in(streams_of[8], 71), 0)
    return dict(value_field=value_field, avoid_field=avoid_field, sample_adjoint=sample_adjoint, offset_y=offset_y, offset_s=offset_s, start_xy=start_xy, start_hs=start_hs, send_counts=send_counts)


TIME_STEP = 0.3
SHARPNESS = 2.0
SOFTENING = 0.1
TURN_RATE = 0.5
ACCELERATION = 0.3
SLOWEST = 0.2
SPEED_RANGE = 0.8
FASTEST = 1.0

def smooth_abs(slope_value):
    return jnp.sqrt(slope_value * slope_value + SOFTENING * SOFTENING)

def edge_neighbours(grid_field, along_dim):
    length = grid_field.shape[along_dim]
    first_plane = lax.slice_in_dim(grid_field, 0, 1, axis=along_dim)
    last_plane = lax.slice_in_dim(grid_field, length - 1, length, axis=along_dim)
    upper_cells = jnp.concatenate([lax.slice_in_dim(grid_field, 1, length, axis=along_dim), last_plane], along_dim)
    lower_cells = jnp.concatenate([first_plane, lax.slice_in_dim(grid_field, 0, length - 1, axis=along_dim)], along_dim)
    return (upper_cells, lower_cells)

def linear_term(grid_field, upper_cells, lower_cells, factor):
    return factor * (upper_cells - lower_cells) * 0.5 - FASTEST * (upper_cells - 2.0 * grid_field + lower_cells) * 0.5

def turn_term(grid_field, upper_cells, lower_cells, turn_rate):
    return turn_rate * smooth_abs(0.5 * (upper_cells - lower_cells)) - turn_rate * 0.5 * (upper_cells - 2.0 * grid_field + lower_cells)

def coefficients(head_index, total_heads):
    heading_angle = 2.0 * math.pi / total_heads * head_index.astype(jnp.float32)
    speed_cell = SLOWEST + SPEED_RANGE * jnp.arange(NS, dtype=jnp.int32).astype(jnp.float32) / (NS - 1)
    along_x = jnp.cos(heading_angle)[:, None, None, None] * speed_cell[None, :, None, None]
    along_y = jnp.sin(heading_angle)[:, None, None, None] * speed_cell[None, :, None, None]
    return (along_x, along_y)

def hamilton_of(grid_field):
    along_x, along_y = coefficients(jnp.arange(NH, dtype=jnp.int32), NH)
    upper_cells, lower_cells = edge_neighbours(grid_field, 2)
    summed = linear_term(grid_field, upper_cells, lower_cells, along_x)
    upper_cells, lower_cells = edge_neighbours(grid_field, 3)
    summed = summed + linear_term(grid_field, upper_cells, lower_cells, along_y)
    upper_cells = jnp.roll(grid_field, -1, 0)
    lower_cells = jnp.roll(grid_field, 1, 0)
    summed = summed + turn_term(grid_field, upper_cells, lower_cells, TURN_RATE)
    upper_cells, lower_cells = edge_neighbours(grid_field, 1)
    return summed + turn_term(grid_field, upper_cells, lower_cells, ACCELERATION)

def step_map(value_field, avoid_field):
    relaxed = value_field - TIME_STEP * hamilton_of(value_field)
    return avoid_field + jax.nn.softplus(SHARPNESS * (relaxed - avoid_field)) / SHARPNESS

def reference(value_field, avoid_field, sample_adjoint, offset_y, offset_s, start_xy, start_hs, send_counts):
    slot_index = jnp.arange(CAP, dtype=jnp.int32)
    live_slot = slot_index[None, None, None, :] < send_counts[..., None]
    weight = jnp.where(live_slot, sample_adjoint, jnp.zeros_like(sample_adjoint))
    owner_index = jnp.arange(ROWGROUPS, dtype=jnp.int32)[None, None, :, None]
    block_index = jnp.arange(HEADGROUPS, dtype=jnp.int32)[None, :, None, None]
    x_cell = (owner_index * CX + start_xy // NY).astype(jnp.int32)
    y_cell = (start_xy % NY).astype(jnp.int32)
    h_cell = (block_index * CH + start_hs // NS).astype(jnp.int32)
    s_cell = (start_hs % NS).astype(jnp.int32)
    flat_index = (((h_cell * NS + s_cell) * NX + x_cell) * NY + y_cell).astype(jnp.int32).reshape(-1)
    plane = NX * NY
    deposited = jnp.zeros((NH * NS * NX * NY,), jnp.float32)
    deposited = deposited.at[flat_index].add((weight * (1.0 - offset_y) * (1.0 - offset_s)).reshape(-1))
    deposited = deposited.at[flat_index + 1].add((weight * offset_y * (1.0 - offset_s)).reshape(-1))
    deposited = deposited.at[flat_index + plane].add((weight * (1.0 - offset_y) * offset_s).reshape(-1))
    deposited = deposited.at[flat_index + plane + 1].add((weight * offset_y * offset_s).reshape(-1))
    deposited = deposited.reshape(NH, NS, NX, NY)
    next_value, pullback = jax.vjp(step_map, value_field, avoid_field)
    value_grad, avoid_grad = pullback(deposited)
    return (next_value, value_grad, avoid_grad)
```

```python
import functools
import math

import jax
import jax.numpy as jnp
import numpy as np
from jax import lax
from jax.experimental import pallas as pl
from jax.experimental.pallas import tpu as pltpu
from jax.sharding import PartitionSpec as P

TIME_STEP = 0.3
SHARPNESS = 2.0
SOFTENING = 0.1
TURN_RATE = 0.5
ACCELERATION = 0.3
SLOWEST = 0.2
SPEED_RANGE = 0.8
ROWS = 8
MESH = pl.DeviceIdType.MESH


def smooth_abs(slope):
    return jnp.sqrt(slope * slope + SOFTENING * SOFTENING)


def upper(plane, axis):
    n = plane.shape[axis]
    return jnp.concatenate(
        [lax.slice_in_dim(plane, 1, n, axis=axis), lax.slice_in_dim(plane, n - 1, n, axis=axis)], axis
    )


def lower(plane, axis):
    n = plane.shape[axis]
    return jnp.concatenate(
        [lax.slice_in_dim(plane, 0, 1, axis=axis), lax.slice_in_dim(plane, 0, n - 1, axis=axis)], axis
    )


def spread(up, down, axis):
    n = up.shape[axis]
    from_lower = jnp.concatenate(
        [lax.slice_in_dim(down, 0, 1, axis=axis), lax.slice_in_dim(up, 0, n - 1, axis=axis)], axis
    )
    from_upper = jnp.concatenate(
        [lax.slice_in_dim(down, 1, n, axis=axis), lax.slice_in_dim(up, n - 1, n, axis=axis)], axis
    )
    return from_lower + from_upper


def pick(table, index):
    chosen = jnp.float32(table[0])
    for i in range(1, len(table)):
        chosen = jnp.where(index == i, jnp.float32(table[i]), chosen)
    return chosen


def kernel(
    groups, blocks,
    value_h, avoid_h, weight_h, offy_h, offs_h, xy_h, hs_h, count_h,
    next_o, vgrad_o, agrad_o,
    value, avoid, weight, offy, offs, xy, hs, count,
    pay, got, xhalo, hhalo, carried, turned, cxhalo, chhalo,
    in_sem, pay_send, pay_recv, x_send, x_recv, h_send, h_recv,
    cx_send, cx_recv, ch_send, ch_recv, self_sem,
):
    heads, cells, lines, speeds = value.shape
    slots = weight.shape[1]
    me = lax.axis_index("gx")
    hb = lax.axis_index("ha")
    h_next = lax.rem(hb + 1, blocks)
    h_prev = lax.rem(hb + blocks - 1, blocks)
    has_prev = me > 0
    has_next = me < groups - 1

    barrier = pltpu.get_barrier_semaphore()

    def greet(d):
        pl.semaphore_signal(
            barrier, inc=1, device_id=(lax.rem(me + d, groups), hb), device_id_type=MESH
        )

    if groups <= 8:
        for d in range(1, groups):
            greet(d)
    else:
        pl.loop(1, groups)(greet)
    for other in (h_prev, h_next):
        pl.semaphore_signal(barrier, inc=1, device_id=(me, other), device_id_type=MESH)

    pairs = (
        (weight_h, weight), (offy_h, offy), (offs_h, offs), (xy_h, xy), (hs_h, hs), (count_h, count),
        (value_h, value), (avoid_h, avoid),
    )
    loads = [pltpu.make_async_copy(a, b, in_sem.at[i]) for i, (a, b) in enumerate(pairs)]
    for load in loads:
        load.start()
    for load in loads[:6]:
        load.wait()

    owners = lax.broadcasted_iota(jnp.int32, (groups, groups), 0)
    lanes = lax.broadcasted_iota(jnp.int32, (groups, groups), 1)
    live = jnp.sum(
        jnp.where(owners == lanes, jnp.broadcast_to(count[...], (groups, groups)), 0).astype(jnp.float32),
        axis=1, keepdims=True,
    )
    slot = lax.broadcasted_iota(jnp.int32, (groups, slots), 1).astype(jnp.float32)
    w = jnp.where(slot < live, weight[...], 0.0)
    oy = offy[...]
    os = offs[...]
    state = hs[...]
    head = lax.div(state, speeds)
    pay[:, 0, :] = w * (1.0 - oy)
    pay[:, 1, :] = w * oy
    pay[:, 2, :] = 1.0 - os
    pay[:, 3, :] = os
    pay[:, 4, :] = (head * (cells * lines) + xy[...]).astype(jnp.float32)
    pay[:, 5, :] = (state - head * speeds).astype(jnp.float32)
    pay[:, 6, :] = jnp.zeros((groups, slots), jnp.float32)
    pay[:, 7, :] = jnp.zeros((groups, slots), jnp.float32)

    loads[6].wait()
    pl.semaphore_wait(barrier, groups - 1 + 2)

    def h_copy(side):
        return pltpu.make_async_remote_copy(
            value.at[0 if side == 0 else heads - 1], hhalo.at[1 - side],
            h_send.at[side], h_recv.at[1 - side],
            device_id=(me, h_prev if side == 0 else h_next), device_id_type=MESH,
        )

    def x_copy(side):
        return pltpu.make_async_remote_copy(
            value.at[:, 0 if side == 0 else cells - 1], xhalo.at[1 - side],
            x_send.at[side], x_recv.at[1 - side],
            device_id=(me - 1 if side == 0 else me + 1, hb), device_id_type=MESH,
        )

    def pay_copy(d):
        peer = lax.rem(me + d, groups)
        return pltpu.make_async_remote_copy(
            pay.at[peer], got.at[d], pay_send.at[d], pay_recv.at[d],
            device_id=(peer, hb), device_id_type=MESH,
        )

    for side in range(2):
        h_copy(side).start()
    for side, has in ((0, has_prev), (1, has_next)):
        @pl.when(has)
        def _():
            x_copy(side).start()

    if groups <= 8:
        for d in range(groups - 1, 0, -1):
            pay_copy(d).start()
    else:
        pl.loop(1, groups)(lambda d: pay_copy(d).start())
    mine = pltpu.make_async_copy(pay.at[me], got.at[0], self_sem)
    mine.start()
    loads[7].wait()

    for side, has in ((0, has_prev), (1, has_next)):
        @pl.when(jnp.logical_not(has))
        def _():
            xhalo[side] = value[:, 0 if side == 0 else cells - 1]

    total = heads * blocks
    angles = [np.float32(2.0 * math.pi / total) * np.float32(k) for k in range(total)]
    cosines = [float(np.cos(a)) for a in angles]
    sines = [float(np.sin(a)) for a in angles]
    speed = SLOWEST + SPEED_RANGE * lax.broadcasted_iota(jnp.int32, (1, speeds), 1).astype(
        jnp.float32
    ) / (speeds - 1)
    cx = [pick(cosines, hb * heads + h) * speed for h in range(heads)]
    cy = [pick(sines, hb * heads + h) * speed for h in range(heads)]
    grid = [(h, x) for h in range(heads) for x in range(cells)]
    v = {(h, x): value[h, x] for h, x in grid}
    part, s_slope = {}, {}
    for h, x in grid:
        here = v[h, x]
        up, down = upper(here, 0), lower(here, 0)
        term = cy[h] * (up - down) * 0.5 - (up - 2.0 * here + down) * 0.5
        up, down = upper(here, 1), lower(here, 1)
        slope = 0.5 * (up - down)
        size = smooth_abs(slope)
        s_slope[h, x] = slope / size
        part[h, x] = term + ACCELERATION * size - ACCELERATION * 0.5 * (up - 2.0 * here + down)

    for side in range(2):
        h_copy(side).wait_recv()
    for side, has in ((0, has_prev), (1, has_next)):
        @pl.when(has)
        def _():
            x_copy(1 - side).wait_recv()
    for x in range(cells):
        v[-1, x] = hhalo[0, x]
        v[heads, x] = hhalo[1, x]
    for h in range(heads):
        v[h, -1] = xhalo[0, h]
        v[h, cells] = xhalo[1, h]

    share, h_slope, above = {}, {}, {}
    for h, x in grid:
        here = v[h, x]
        up, down = v[h + 1, x], v[h - 1, x]
        slope = 0.5 * (up - down)
        size = smooth_abs(slope)
        h_slope[h, x] = slope / size
        turning = TURN_RATE * size - TURN_RATE * 0.5 * (up - 2.0 * here + down)
        up, down = v[h, x + 1], v[h, x - 1]
        across = cx[h] * (up - down) * 0.5 - (up - 2.0 * here + down) * 0.5
        relaxed = here - TIME_STEP * (across + part[h, x] + turning)
        floor = avoid[h, x]
        excess = SHARPNESS * (relaxed - floor)
        small = jnp.exp(-jnp.abs(excess))
        share[h, x] = jnp.where(excess >= 0.0, 1.0, small) / (1.0 + small)
        above[h, x] = (excess, small)

    rows = heads * cells * lines
    row_id = lax.broadcasted_iota(jnp.int32, (rows, slots), 0).astype(jnp.float32)
    speed_id = lax.broadcasted_iota(jnp.int32, (speeds, slots), 0).astype(jnp.float32)

    def operands(d):
        one = got[d]
        cell = jnp.broadcast_to(one[4:5], (rows, slots))
        left = jnp.where(row_id == cell, one[0:1], jnp.where(row_id == cell + 1.0, one[1:2], 0.0))
        cell = jnp.broadcast_to(one[5:6], (speeds, slots))
        right = jnp.where(
            speed_id == cell, one[2:3], jnp.where(speed_id == cell + 1.0, one[3:4], 0.0)
        )
        return left, right

    def product(left, right):
        return lax.dot_general(
            left, right, (((1,), (1,)), ((), ())),
            precision=lax.Precision.HIGHEST, preferred_element_type=jnp.float32,
        )

    mine.wait()
    if groups <= 8:
        for d in range(1, groups):
            pay_copy(d).wait_recv()
        both = [operands(d) for d in range(groups)]
        deposit = product(
            jnp.concatenate([b[0] for b in both], 1), jnp.concatenate([b[1] for b in both], 1)
        )
    else:
        pl.loop(1, groups)(lambda d: pay_copy(d).wait_recv())
        deposit = lax.fori_loop(
            0, groups, lambda d, so_far: so_far + product(*operands(d)),
            jnp.zeros((rows, speeds), jnp.float32),
        )

    c, adj = {}, {}
    for n, (h, x) in enumerate(grid):
        adjoint = deposit[n * lines : (n + 1) * lines]
        c[h, x] = adjoint * share[h, x]
        carried[h, x] = c[h, x]
        adj[h, x] = adjoint
    def cx_copy(side):
        return pltpu.make_async_remote_copy(
            carried.at[:, 0 if side == 0 else cells - 1], cxhalo.at[1 - side],
            cx_send.at[side], cx_recv.at[1 - side],
            device_id=(me - 1 if side == 0 else me + 1, hb), device_id_type=MESH,
        )

    for side, has in ((0, has_prev), (1, has_next)):
        @pl.when(has)
        def _():
            cx_copy(side).start()

        @pl.when(jnp.logical_not(has))
        def _():
            cxhalo[side] = jnp.zeros_like(cxhalo[side])
    ahead, back = {}, {}
    for h, x in grid:
        pull = (0.5 * TURN_RATE) * c[h, x] * h_slope[h, x]
        keep = (0.5 * TURN_RATE) * c[h, x]
        ahead[h, x] = pull - keep
        back[h, x] = -pull - keep
    for x in range(cells):
        turned[0, x] = back[0, x]
        turned[1, x] = ahead[heads - 1, x]

    def ch_copy(side):
        return pltpu.make_async_remote_copy(
            turned.at[side], chhalo.at[1 - side], ch_send.at[side], ch_recv.at[1 - side],
            device_id=(me, h_prev if side == 0 else h_next), device_id_type=MESH,
        )

    for side in range(2):
        ch_copy(side).start()

    local = {}
    for h, x in grid:
        excess, small = above[h, x]
        next_o[h, x] = avoid[h, x] + (jnp.maximum(excess, 0.0) + jnp.log1p(small)) / SHARPNESS
        agrad_o[h, x] = adj[h, x] * (jnp.where(excess >= 0.0, small, 1.0) / (1.0 + small))
        here = c[h, x]
        grad = spread((0.5 * cy[h] - 0.5) * here, (-0.5 * cy[h] - 0.5) * here, 0)
        pull = (0.5 * ACCELERATION) * here * s_slope[h, x]
        keep = (0.5 * ACCELERATION) * here
        grad = grad + spread(pull - keep, -pull - keep, 1)
        local[h, x] = grad + (2.0 + TURN_RATE + ACCELERATION) * here

    for side in range(2):
        ch_copy(side).wait_recv()
    for side, has in ((0, has_prev), (1, has_next)):
        @pl.when(has)
        def _():
            cx_copy(1 - side).wait_recv()
    for h, x in grid:
        grad = local[h, x]
        grad = grad + (ahead[h - 1, x] if h > 0 else chhalo[0, x])
        grad = grad + (back[h + 1, x] if h < heads - 1 else chhalo[1, x])
        low, high = 0.5 * cx[h] - 0.5, -0.5 * cx[h] - 0.5
        if x > 0:
            grad = grad + low * c[h, x - 1]
        else:
            grad = grad + jnp.where(has_prev, low * cxhalo[0, h], high * c[h, x])
        if x < cells - 1:
            grad = grad + high * c[h, x + 1]
        else:
            grad = grad + jnp.where(has_next, high * cxhalo[1, h], low * c[h, x])
        vgrad_o[h, x] = c[h, x] - TIME_STEP * grad

    for side in range(2):
        h_copy(side).wait_send()
        ch_copy(side).wait_send()
    for side, has in ((0, has_prev), (1, has_next)):
        @pl.when(has)
        def _():
            x_copy(side).wait_send()
            cx_copy(side).wait_send()
    if groups <= 8:
        for d in range(1, groups):
            pay_copy(d).wait_send()
    else:
        pl.loop(1, groups)(lambda d: pay_copy(d).wait_send())


def near_kernel(
    groups, blocks,
    value_h, avoid_h, weight_h, offy_h, offs_h, xy_h, hs_h, count_h,
    next_o, vgrad_o, agrad_o,
    fields, sample, cell, count, pay, got, packed, halo,
    in_sem, pay_send, near_send, pay_recv, halo_send, halo_recv,
):
    _, heads, cells, lines, speeds = fields.shape
    value, avoid = fields.at[0], fields.at[1]
    slots = sample.shape[2]
    me = lax.axis_index("gx")
    hb = lax.axis_index("ha")
    h_next = lax.rem(hb + 1, blocks)
    h_prev = lax.rem(hb + blocks - 1, blocks)
    h_side = (h_prev, h_next)
    has_prev = me > 0
    has_next = me < groups - 1
    has_x = (has_prev, has_next)

    barrier = pltpu.get_barrier_semaphore()

    def greet(j, h):
        pl.semaphore_signal(barrier, inc=1, device_id=(j, h), device_id_type=MESH)

    for j in range(groups):
        @pl.when(me != j)
        def _():
            greet(j, hb)
        for h in h_side:
            greet(j, h)

    loads = [
        pltpu.make_async_copy(a, b, in_sem.at[i])
        for a, b, i in (
            (weight_h, sample.at[0], 0), (offy_h, sample.at[1], 0), (offs_h, sample.at[2], 0),
            (xy_h, cell.at[0], 0), (hs_h, cell.at[1], 0), (count_h, count, 1),
            (value_h, value, 2), (avoid_h, avoid, 2),
        )
    ]
    for load in loads:
        load.start()
    loaded = [pltpu.make_async_copy(r, r, in_sem.at[i]) for r, i in ((sample, 0), (count, 1), (fields, 2))]

    pay[0] = jnp.zeros(pay.shape[1:], jnp.float32)
    pay[groups + 1] = jnp.zeros(pay.shape[1:], jnp.float32)

    def copy(src, dst, send_sem, recv_sem, j, h):
        return pltpu.make_async_remote_copy(
            src, dst, send_sem, recv_sem, device_id=(j, h), device_id_type=MESH
        )

    def x_slot(side):
        return 4 + side * 4

    def h_halo(side):
        at = 2 * (1 - side)
        copy(packed, halo.at[at : at + 2], halo_send, halo_recv, me, h_side[side]).start()

    def x_halo(side):
        at = x_slot(1 - side)
        j = me - 1 if side == 0 else me + 1
        copy(packed, halo.at[at : at + 2], halo_send, halo_recv, j, hb).start()
        for h in range(2):
            copy(packed.at[0], halo.at[at + 3 - h], halo_send, halo_recv, j, h_side[h]).start()

    def send(j):
        @pl.when(me != j)
        def _():
            copy(pay.at[j : j + 3], got.at[me, 0:3], pay_send, pay_recv.at[me], j, hb).start()
            for side in range(2):
                copy(
                    pay.at[j + 1], got.at[me, 4 - side], pay_send, pay_recv.at[me], j, h_side[side]
                ).start()

    loaded[0].wait()
    loaded[1].wait()
    owners = lax.broadcasted_iota(jnp.int32, (groups, groups), 0)
    lanes = lax.broadcasted_iota(jnp.int32, (groups, groups), 1)
    live = jnp.sum(
        jnp.where(owners == lanes, jnp.broadcast_to(count[...], (groups, groups)), 0).astype(jnp.float32),
        axis=1, keepdims=True,
    )
    slot = lax.broadcasted_iota(jnp.int32, (groups, slots), 1).astype(jnp.float32)
    w = jnp.where(slot < live, sample[0], 0.0)
    oy = sample[1]
    state = cell[1]
    head = lax.div(state, speeds)
    row = head * (cells * lines) + cell[0]
    pay[1 : groups + 1, 0, :] = w * (1.0 - oy)
    pay[1 : groups + 1, 1, :] = w * oy
    pay[1 : groups + 1, 2, :] = sample[2]
    pay[1 : groups + 1, 3, :] = (row * speeds + (state - head * speeds)).astype(jnp.float32)
    loaded[2].wait()
    grid = [(h, x) for h in range(heads) for x in range(cells)]
    for i in range(2):
        packed[i] = jnp.concatenate([fields[i, h, x] for h, x in grid], 1)

    pl.semaphore_wait(barrier, 3 * groups - 1)
    send(0)
    for side in range(2):
        h_halo(side)
    for side in range(2):
        pl.when(has_x[side])(functools.partial(x_halo, side))
    for side in range(2):
        copy(
            pay.at[me + 1], got.at[me, 4 - side], near_send, pay_recv.at[me], me, h_side[side]
        ).start()
    for j in range(1, groups):
        send(j)

    width = heads * cells * speeds
    half, quarter = width // 2, width // 4
    lane = lax.broadcasted_iota(jnp.int32, (1, width), 1)
    place = lax.div(lane, quarter)
    within = lax.rem(lane, quarter)
    even = lax.rem(place, 2) == 0
    left_half = place < 2
    total = heads * blocks
    angles = [np.float32(2.0 * math.pi / total) * np.float32(k) for k in range(total)]
    cosines = [float(np.cos(a)) for a in angles]
    sines = [float(np.sin(a)) for a in angles]
    speed = SLOWEST + SPEED_RANGE * within.astype(jnp.float32) / (speeds - 1)
    turn = [lax.rem(hb * heads + h + total, total) for h in range(-1, heads + 1)]
    cos_of = [pick(cosines, t) for t in turn]
    sin_of = [pick(sines, t) for t in turn]
    cx_own, cy_own = (jnp.where(left_half, a[1], a[2]) * speed for a in (cos_of, sin_of))
    cx_out, cy_out = (jnp.where(left_half, a[0], a[3]) * speed for a in (cos_of, sin_of))

    def shift(a, by):
        return pltpu.roll(a, by % width, 1)

    def forward(here, floor, cx, cy, h_up, h_down, x_up, x_down):
        up, down = upper(here, 0), lower(here, 0)
        rate = cy * (up - down) * 0.5 - (up - 2.0 * here + down) * 0.5
        up = jnp.where(within == quarter - 1, here, shift(here, -1))
        down = jnp.where(within == 0, here, shift(here, 1))
        slope = 0.5 * (up - down)
        size = smooth_abs(slope)
        s_slope = slope / size
        rate = rate + ACCELERATION * size - ACCELERATION * 0.5 * (up - 2.0 * here + down)
        slope = 0.5 * (h_up - h_down)
        size = smooth_abs(slope)
        h_slope = slope / size
        rate = rate + TURN_RATE * size - TURN_RATE * 0.5 * (h_up - 2.0 * here + h_down)
        rate = rate + cx * (x_up - x_down) * 0.5 - (x_up - 2.0 * here + x_down) * 0.5
        excess = SHARPNESS * (here - TIME_STEP * rate - floor)
        small = jnp.exp(-jnp.abs(excess))
        share = jnp.where(excess >= 0.0, 1.0, small) / (1.0 + small)
        pull = (0.5 * TURN_RATE) * share * h_slope
        keep = (0.5 * TURN_RATE) * share
        return excess, small, share, s_slope, pull - keep, -pull - keep

    def all_halos(sending):
        def wait(n):
            view = halo.at[0:n]
            c = copy(view, view, halo_send, halo_recv, me, h_next)
            c.wait_send() if sending else c.wait_recv()

        @pl.when(has_prev & has_next)
        def _():
            wait(12)

        @pl.when(jnp.logical_not(has_prev & has_next))
        def _():
            wait(8)

    def unpack(a):
        return {(h, x): a[:, n * speeds : (n + 1) * speeds] for n, (h, x) in enumerate(grid)}

    all_halos(False)
    own, floor = packed[0], packed[1]
    hp, hp_floor, hn, hn_floor = (halo[i] for i in range(4))
    xp, xp_floor, pp, pn, xn, xn_floor, np_, nn = (halo[i] for i in range(4, 12))
    edge_h = shift(jnp.where(left_half, hn, hp), half)
    edge_x = jnp.where(even, shift(xp, -quarter), shift(xn, quarter))
    up_x = jnp.where(even, shift(own, -quarter), jnp.where(has_next, edge_x, own))
    down_x = jnp.where(even, jnp.where(has_prev, edge_x, own), shift(own, quarter))
    excess, small, share, s_slope, ahead, back = forward(
        own, floor, cx_own, cy_own,
        shift(jnp.where(left_half, hn, own), half), shift(jnp.where(left_half, own, hp), half),
        up_x, down_x,
    )
    next_v = unpack(floor + (jnp.maximum(excess, 0.0) + jnp.log1p(small)) / SHARPNESS)
    for h, x in grid:
        next_o[h, x] = next_v[h, x]
    rest = unpack(jnp.where(excess >= 0.0, small, 1.0) / (1.0 + small))
    share, s_slope, ahead, back = (unpack(a) for a in (share, s_slope, ahead, back))

    up_x = shift(jnp.where(even, jnp.where(place == 2, np_, nn), edge_h), -quarter)
    down_x = shift(jnp.where(even, edge_h, jnp.where(place == 3, pp, pn)), quarter)
    out = forward(
        edge_h, shift(jnp.where(left_half, hn_floor, hp_floor), half), cx_out, cy_out,
        jnp.where(left_half, own, hn), jnp.where(left_half, hp, own),
        jnp.where(even | has_next, up_x, edge_h), jnp.where(even & jnp.logical_not(has_prev), edge_h, down_x),
    )
    out = unpack(jnp.where(left_half, out[4], out[5]))
    for x in range(cells):
        ahead[-1, x], back[heads, x] = out[0, x], out[1, x]

    turned = shift(edge_x, half)
    up_h = jnp.where(left_half, turned, jnp.where(even, shift(pn, quarter), shift(nn, -quarter)))
    down_h = jnp.where(left_half, jnp.where(even, shift(pp, quarter), shift(np_, -quarter)), turned)
    out = forward(
        edge_x, jnp.where(even, shift(xp_floor, -quarter), shift(xn_floor, quarter)), cx_own, cy_own,
        up_h, down_h, jnp.where(even, own, xn), jnp.where(even, xp, own),
    )
    out = unpack(out[2])
    for h in range(heads):
        share[h, -1], share[h, cells] = out[h, 0], out[h, 1]
    speed = SLOWEST + SPEED_RANGE * lax.broadcasted_iota(jnp.int32, (1, speeds), 1).astype(
        jnp.float32
    ) / (speeds - 1)
    cx = [cos_of[h + 1] * speed for h in range(heads)]
    cy = [sin_of[h + 1] * speed for h in range(heads)]

    span = cells * lines
    inside = lax.broadcasted_iota(jnp.int32, (heads * span, slots), 0)
    edge = lax.broadcasted_iota(jnp.int32, (heads * lines, slots), 0)
    edge = lax.div(edge, lines) * span + lax.rem(edge, lines)
    side_rows = lax.broadcasted_iota(jnp.int32, (span, slots), 0)
    ids = [
        i.astype(jnp.float32)
        for i in (edge + (cells - 1) * lines, inside, edge, side_rows + (heads - 1) * span, side_rows)
    ]
    speed_id = lax.broadcasted_iota(jnp.int32, (speeds, slots), 0).astype(jnp.float32)

    def deposit(one, row_id):
        weight0, weight1, up_s, code = one[0:1], one[1:2], one[2:3], one[3:4]
        row = jnp.floor(code * (1.0 / speeds))
        cell = code - row * speeds
        down_s = 1.0 - up_s
        here, above_it = row_id == row, row_id == row + 1.0
        left = jnp.concatenate(
            [
                jnp.where(here, weight0 * f, jnp.where(above_it, weight1 * f, 0.0))
                for f in (down_s, up_s)
            ],
            1,
        )
        high = left.astype(jnp.bfloat16)
        low = (left - high.astype(jnp.float32)).astype(jnp.bfloat16)
        right = jnp.concatenate(
            [jnp.where(speed_id == c, 1.0, 0.0) for c in (cell, cell + 1.0)], 1
        ).astype(jnp.bfloat16)
        dims = (((1,), (1,)), ((), ()))
        return lax.dot_general(
            high, right, dims, preferred_element_type=jnp.float32
        ) + lax.dot_general(low, right, dims, preferred_element_type=jnp.float32)

    def payload(g, lo, n):
        view = got.at[g, lo : lo + n]
        return copy(view, view, pay_send, pay_recv.at[g], me, h_next)

    def collect(g, sums):
        payload(g, 0, 5).wait_recv()
        return tuple(s + deposit(got[g, i], ids[i]) for i, s in enumerate(sums))

    payload(me, 3, 2).wait_recv()
    sums = tuple(
        deposit(pay[me + i] if i < 3 else got[me, i], ids[i]) for i in range(5)
    )
    sums = lax.fori_loop(0, me, collect, sums)
    sums = lax.fori_loop(me + 1, groups, collect, sums)

    adj, c = {}, {}
    for n, (h, x) in enumerate(grid):
        adj[h, x] = sums[1][n * lines : (n + 1) * lines]
        c[h, x] = adj[h, x] * share[h, x]
    for h in range(heads):
        c[h, -1] = sums[0][h * lines : (h + 1) * lines] * share[h, -1]
        c[h, cells] = sums[2][h * lines : (h + 1) * lines] * share[h, cells]
    for x in range(cells):
        adj[-1, x] = sums[3][x * lines : (x + 1) * lines]
        adj[heads, x] = sums[4][x * lines : (x + 1) * lines]

    for h, x in grid:
        agrad_o[h, x] = adj[h, x] * rest[h, x]
        here = c[h, x]
        grad = spread((0.5 * cy[h] - 0.5) * here, (-0.5 * cy[h] - 0.5) * here, 0)
        pull = (0.5 * ACCELERATION) * here * s_slope[h, x]
        keep = (0.5 * ACCELERATION) * here
        grad = grad + spread(pull - keep, -pull - keep, 1)
        grad = grad + (2.0 + TURN_RATE + ACCELERATION) * here
        grad = grad + adj[h - 1, x] * ahead[h - 1, x] + adj[h + 1, x] * back[h + 1, x]
        low, high = 0.5 * cx[h] - 0.5, -0.5 * cx[h] - 0.5
        if x > 0:
            grad = grad + low * c[h, x - 1]
        else:
            grad = grad + jnp.where(has_prev, low * c[h, -1], high * here)
        if x < cells - 1:
            grad = grad + high * c[h, x + 1]
        else:
            grad = grad + jnp.where(has_next, high * c[h, cells], low * here)
        vgrad_o[h, x] = here - TIME_STEP * grad

    all_halos(True)
    view = got.at[0, 0:2]
    copy(view, view, near_send, pay_recv.at[0], me, h_next).wait_send()
    view = got.at[0 : groups - 1]
    copy(view, view, pay_send, pay_recv.at[0], me, h_next).wait_send()


def write_out(next_v, vgrad_v, agrad_v, next_o, vgrad_o, agrad_o, sem):
    copies = [
        pltpu.make_async_copy(a, b, sem.at[i])
        for i, (a, b) in enumerate(((next_v, next_o), (vgrad_v, vgrad_o), (agrad_v, agrad_o)))
    ]
    for copy in copies:
        copy.start()
    for copy in copies:
        copy.wait()


def on_device(groups, blocks, value, avoid, weight, offy, offs, xy, hs, count):
    slots = weight.shape[3]
    value = jnp.transpose(value, (0, 2, 3, 1))
    avoid = jnp.transpose(avoid, (0, 2, 3, 1))
    weight, offy, offs, xy, hs = (a.reshape(groups, slots) for a in (weight, offy, offs, xy, hs))
    count = count.reshape(1, groups)
    heads, cells, lines, speeds = value.shape
    f32 = jnp.float32
    dma = pltpu.SemaphoreType.DMA
    field = pltpu.VMEM(value.shape, f32)
    x_pair = pltpu.VMEM((2, heads, lines, speeds), f32)
    h_pair = pltpu.VMEM((2, cells, lines, speeds), f32)
    near = 1 < groups <= 8 and blocks > 2 and heads == cells == 2 and 4 * speeds == slots == 128
    sample = pltpu.VMEM((groups, slots), f32)
    index = pltpu.VMEM((groups, slots), jnp.int32)
    counts = pltpu.VMEM((1, groups), jnp.int32)
    if near:
        scratch = [
            pltpu.VMEM((2, *value.shape), f32),
            pltpu.VMEM((5, groups, slots), f32), pltpu.VMEM((2, groups, slots), jnp.int32), counts,
            pltpu.VMEM((groups + 2, 4, slots), f32), pltpu.VMEM((groups, 5, 4, slots), f32),
            pltpu.VMEM((2, lines, slots), f32), pltpu.VMEM((12, lines, slots), f32),
            dma((3,)), dma, dma, dma((groups,)), dma, dma,
        ]
    else:
        scratch = [
            field, field, sample, sample, sample, index, index, counts,
            pltpu.VMEM((groups, ROWS, slots), f32), pltpu.VMEM((groups, ROWS, slots), f32),
            x_pair, h_pair, field, h_pair, x_pair, h_pair,
            dma((8,)), dma((groups,)), dma((groups,)), *[dma((2,))] * 8, dma,
        ]
    outs = pl.pallas_call(
        functools.partial(near_kernel if near else kernel, groups, blocks),
        out_shape=[pltpu.VMEM(value.shape, f32)] * 3,
        in_specs=[pl.BlockSpec(memory_space=pltpu.HBM)] * 8,
        out_specs=[pl.BlockSpec(memory_space=pltpu.VMEM)] * 3,
        scratch_shapes=scratch,
        compiler_params=pltpu.CompilerParams(collective_id=0, has_side_effects=True),
        name="step",
    )(value, avoid, weight, offy, offs, xy, hs, count)
    outs = pl.pallas_call(
        write_out,
        out_shape=[jax.ShapeDtypeStruct(value.shape, f32)] * 3,
        in_specs=[pl.BlockSpec(memory_space=pl.ANY)] * 3,
        out_specs=[pl.BlockSpec(memory_space=pl.ANY)] * 3,
        scratch_shapes=[dma((3,))],
        compiler_params=pltpu.CompilerParams(vmem_limit_bytes=1 << 20),
        name="write_out",
    )(*outs)
    return tuple(jnp.transpose(o, (0, 3, 1, 2)) for o in outs)


def solution(mesh):
    field = P("ha", None, "gx", None)
    sample = P("gx", "ha", None, None)
    return jax.shard_map(
        functools.partial(on_device, mesh.shape["gx"], mesh.shape["ha"]),
        mesh=mesh,
        in_specs=(field, field, sample, sample, sample, sample, sample, P("gx", "ha", None)),
        out_specs=(field, field, field),
        check_vma=False,
    )
```

```python
import functools
import math

import jax
import jax.numpy as jnp
import numpy as np
from jax import lax
from jax.experimental import pallas as pl
from jax.experimental.pallas import tpu as pltpu
from jax.sharding import PartitionSpec as P

TIME_STEP = 0.3
SHARPNESS = 2.0
SOFTENING = 0.1
TURN_RATE = 0.5
ACCELERATION = 0.3
SLOWEST = 0.2
SPEED_RANGE = 0.8
ROWS = 8
MESH = pl.DeviceIdType.MESH


def smooth_abs(slope):
    return jnp.sqrt(slope * slope + SOFTENING * SOFTENING)


def upper(plane, axis):
    n = plane.shape[axis]
    return jnp.concatenate(
        [lax.slice_in_dim(plane, 1, n, axis=axis), lax.slice_in_dim(plane, n - 1, n, axis=axis)], axis
    )


def lower(plane, axis):
    n = plane.shape[axis]
    return jnp.concatenate(
        [lax.slice_in_dim(plane, 0, 1, axis=axis), lax.slice_in_dim(plane, 0, n - 1, axis=axis)], axis
    )


def spread(up, down, axis):
    n = up.shape[axis]
    from_lower = jnp.concatenate(
        [lax.slice_in_dim(down, 0, 1, axis=axis), lax.slice_in_dim(up, 0, n - 1, axis=axis)], axis
    )
    from_upper = jnp.concatenate(
        [lax.slice_in_dim(down, 1, n, axis=axis), lax.slice_in_dim(up, n - 1, n, axis=axis)], axis
    )
    return from_lower + from_upper


def pick(table, index):
    chosen = jnp.float32(table[0])
    for i in range(1, len(table)):
        chosen = jnp.where(index == i, jnp.float32(table[i]), chosen)
    return chosen


def kernel(
    groups, blocks,
    value_h, avoid_h, weight_h, offy_h, offs_h, xy_h, hs_h, count_h,
    next_o, vgrad_o, agrad_o,
    value, avoid, weight, offy, offs, xy, hs, count,
    pay, got, xhalo, hhalo, carried, turned, cxhalo, chhalo,
    in_sem, pay_send, pay_recv, x_send, x_recv, h_send, h_recv,
    cx_send, cx_recv, ch_send, ch_recv, self_sem,
):
    heads, cells, lines, speeds = value.shape
    slots = weight.shape[1]
    me = lax.axis_index("gx")
    hb = lax.axis_index("ha")
    h_next = lax.rem(hb + 1, blocks)
    h_prev = lax.rem(hb + blocks - 1, blocks)
    has_prev = me > 0
    has_next = me < groups - 1

    barrier = pltpu.get_barrier_semaphore()

    def greet(d):
        pl.semaphore_signal(
            barrier, inc=1, device_id=(lax.rem(me + d, groups), hb), device_id_type=MESH
        )

    if groups <= 8:
        for d in range(1, groups):
            greet(d)
    else:
        pl.loop(1, groups)(greet)
    for other in (h_prev, h_next):
        pl.semaphore_signal(barrier, inc=1, device_id=(me, other), device_id_type=MESH)

    pairs = (
        (weight_h, weight), (offy_h, offy), (offs_h, offs), (xy_h, xy), (hs_h, hs), (count_h, count),
        (value_h, value), (avoid_h, avoid),
    )
    loads = [pltpu.make_async_copy(a, b, in_sem.at[i]) for i, (a, b) in enumerate(pairs)]
    for load in loads:
        load.start()
    for load in loads[:6]:
        load.wait()

    owners = lax.broadcasted_iota(jnp.int32, (groups, groups), 0)
    lanes = lax.broadcasted_iota(jnp.int32, (groups, groups), 1)
    live = jnp.sum(
        jnp.where(owners == lanes, jnp.broadcast_to(count[...], (groups, groups)), 0).astype(jnp.float32),
        axis=1, keepdims=True,
    )
    slot = lax.broadcasted_iota(jnp.int32, (groups, slots), 1).astype(jnp.float32)
    w = jnp.where(slot < live, weight[...], 0.0)
    oy = offy[...]
    os = offs[...]
    state = hs[...]
    head = lax.div(state, speeds)
    pay[:, 0, :] = w * (1.0 - oy)
    pay[:, 1, :] = w * oy
    pay[:, 2, :] = 1.0 - os
    pay[:, 3, :] = os
    pay[:, 4, :] = (head * (cells * lines) + xy[...]).astype(jnp.float32)
    pay[:, 5, :] = (state - head * speeds).astype(jnp.float32)
    pay[:, 6, :] = jnp.zeros((groups, slots), jnp.float32)
    pay[:, 7, :] = jnp.zeros((groups, slots), jnp.float32)

    loads[6].wait()
    pl.semaphore_wait(barrier, groups - 1 + 2)

    def h_copy(side):
        return pltpu.make_async_remote_copy(
            value.at[0 if side == 0 else heads - 1], hhalo.at[1 - side],
            h_send.at[side], h_recv.at[1 - side],
            device_id=(me, h_prev if side == 0 else h_next), device_id_type=MESH,
        )

    def x_copy(side):
        return pltpu.make_async_remote_copy(
            value.at[:, 0 if side == 0 else cells - 1], xhalo.at[1 - side],
            x_send.at[side], x_recv.at[1 - side],
            device_id=(me - 1 if side == 0 else me + 1, hb), device_id_type=MESH,
        )

    def pay_copy(d):
        peer = lax.rem(me + d, groups)
        return pltpu.make_async_remote_copy(
            pay.at[peer], got.at[d], pay_send.at[d], pay_recv.at[d],
            device_id=(peer, hb), device_id_type=MESH,
        )

    for side in range(2):
        h_copy(side).start()
    for side, has in ((0, has_prev), (1, has_next)):
        @pl.when(has)
        def _():
            x_copy(side).start()

    if groups <= 8:
        for d in range(groups - 1, 0, -1):
            pay_copy(d).start()
    else:
        pl.loop(1, groups)(lambda d: pay_copy(d).start())
    mine = pltpu.make_async_copy(pay.at[me], got.at[0], self_sem)
    mine.start()
    loads[7].wait()

    for side, has in ((0, has_prev), (1, has_next)):
        @pl.when(jnp.logical_not(has))
        def _():
            xhalo[side] = value[:, 0 if side == 0 else cells - 1]

    total = heads * blocks
    angles = [np.float32(2.0 * math.pi / total) * np.float32(k) for k in range(total)]
    cosines = [float(np.cos(a)) for a in angles]
    sines = [float(np.sin(a)) for a in angles]
    speed = SLOWEST + SPEED_RANGE * lax.broadcasted_iota(jnp.int32, (1, speeds), 1).astype(
        jnp.float32
    ) / (speeds - 1)
    cx = [pick(cosines, hb * heads + h) * speed for h in range(heads)]
    cy = [pick(sines, hb * heads + h) * speed for h in range(heads)]
    grid = [(h, x) for h in range(heads) for x in range(cells)]
    v = {(h, x): value[h, x] for h, x in grid}
    part, s_slope = {}, {}
    for h, x in grid:
        here = v[h, x]
        up, down = upper(here, 0), lower(here, 0)
        term = cy[h] * (up - down) * 0.5 - (up - 2.0 * here + down) * 0.5
        up, down = upper(here, 1), lower(here, 1)
        slope = 0.5 * (up - down)
        size = smooth_abs(slope)
        s_slope[h, x] = slope / size
        part[h, x] = term + ACCELERATION * size - ACCELERATION * 0.5 * (up - 2.0 * here + down)

    for side in range(2):
        h_copy(side).wait_recv()
    for side, has in ((0, has_prev), (1, has_next)):
        @pl.when(has)
        def _():
            x_copy(1 - side).wait_recv()
    for x in range(cells):
        v[-1, x] = hhalo[0, x]
        v[heads, x] = hhalo[1, x]
    for h in range(heads):
        v[h, -1] = xhalo[0, h]
        v[h, cells] = xhalo[1, h]

    share, h_slope, above = {}, {}, {}
    for h, x in grid:
        here = v[h, x]
        up, down = v[h + 1, x], v[h - 1, x]
        slope = 0.5 * (up - down)
        size = smooth_abs(slope)
        h_slope[h, x] = slope / size
        turning = TURN_RATE * size - TURN_RATE * 0.5 * (up - 2.0 * here + down)
        up, down = v[h, x + 1], v[h, x - 1]
        across = cx[h] * (up - down) * 0.5 - (up - 2.0 * here + down) * 0.5
        relaxed = here - TIME_STEP * (across + part[h, x] + turning)
        floor = avoid[h, x]
        excess = SHARPNESS * (relaxed - floor)
        small = jnp.exp(-jnp.abs(excess))
        share[h, x] = jnp.where(excess >= 0.0, 1.0, small) / (1.0 + small)
        above[h, x] = (excess, small)

    rows = heads * cells * lines
    row_id = lax.broadcasted_iota(jnp.int32, (rows, slots), 0).astype(jnp.float32)
    speed_id = lax.broadcasted_iota(jnp.int32, (speeds, slots), 0).astype(jnp.float32)

    def operands(d):
        one = got[d]
        cell = jnp.broadcast_to(one[4:5], (rows, slots))
        left = jnp.where(row_id == cell, one[0:1], jnp.where(row_id == cell + 1.0, one[1:2], 0.0))
        cell = jnp.broadcast_to(one[5:6], (speeds, slots))
        right = jnp.where(
            speed_id == cell, one[2:3], jnp.where(speed_id == cell + 1.0, one[3:4], 0.0)
        )
        return left, right

    def product(left, right):
        return lax.dot_general(
            left, right, (((1,), (1,)), ((), ())),
            precision=lax.Precision.HIGHEST, preferred_element_type=jnp.float32,
        )

    mine.wait()
    if groups <= 8:
        for d in range(1, groups):
            pay_copy(d).wait_recv()
        both = [operands(d) for d in range(groups)]
        deposit = product(
            jnp.concatenate([b[0] for b in both], 1), jnp.concatenate([b[1] for b in both], 1)
        )
    else:
        pl.loop(1, groups)(lambda d: pay_copy(d).wait_recv())
        deposit = lax.fori_loop(
            0, groups, lambda d, so_far: so_far + product(*operands(d)),
            jnp.zeros((rows, speeds), jnp.float32),
        )

    c, adj = {}, {}
    for n, (h, x) in enumerate(grid):
        adjoint = deposit[n * lines : (n + 1) * lines]
        c[h, x] = adjoint * share[h, x]
        carried[h, x] = c[h, x]
        adj[h, x] = adjoint
    def cx_copy(side):
        return pltpu.make_async_remote_copy(
            carried.at[:, 0 if side == 0 else cells - 1], cxhalo.at[1 - side],
            cx_send.at[side], cx_recv.at[1 - side],
            device_id=(me - 1 if side == 0 else me + 1, hb), device_id_type=MESH,
        )

    for side, has in ((0, has_prev), (1, has_next)):
        @pl.when(has)
        def _():
            cx_copy(side).start()

        @pl.when(jnp.logical_not(has))
        def _():
            cxhalo[side] = jnp.zeros_like(cxhalo[side])
    ahead, back = {}, {}
    for h, x in grid:
        pull = (0.5 * TURN_RATE) * c[h, x] * h_slope[h, x]
        keep = (0.5 * TURN_RATE) * c[h, x]
        ahead[h, x] = pull - keep
        back[h, x] = -pull - keep
    for x in range(cells):
        turned[0, x] = back[0, x]
        turned[1, x] = ahead[heads - 1, x]

    def ch_copy(side):
        return pltpu.make_async_remote_copy(
            turned.at[side], chhalo.at[1 - side], ch_send.at[side], ch_recv.at[1 - side],
            device_id=(me, h_prev if side == 0 else h_next), device_id_type=MESH,
        )

    for side in range(2):
        ch_copy(side).start()

    local = {}
    for h, x in grid:
        excess, small = above[h, x]
        next_o[h, x] = avoid[h, x] + (jnp.maximum(excess, 0.0) + jnp.log1p(small)) / SHARPNESS
        agrad_o[h, x] = adj[h, x] * (jnp.where(excess >= 0.0, small, 1.0) / (1.0 + small))
        here = c[h, x]
        grad = spread((0.5 * cy[h] - 0.5) * here, (-0.5 * cy[h] - 0.5) * here, 0)
        pull = (0.5 * ACCELERATION) * here * s_slope[h, x]
        keep = (0.5 * ACCELERATION) * here
        grad = grad + spread(pull - keep, -pull - keep, 1)
        local[h, x] = grad + (2.0 + TURN_RATE + ACCELERATION) * here

    for side in range(2):
        ch_copy(side).wait_recv()
    for side, has in ((0, has_prev), (1, has_next)):
        @pl.when(has)
        def _():
            cx_copy(1 - side).wait_recv()
    for h, x in grid:
        grad = local[h, x]
        grad = grad + (ahead[h - 1, x] if h > 0 else chhalo[0, x])
        grad = grad + (back[h + 1, x] if h < heads - 1 else chhalo[1, x])
        low, high = 0.5 * cx[h] - 0.5, -0.5 * cx[h] - 0.5
        if x > 0:
            grad = grad + low * c[h, x - 1]
        else:
            grad = grad + jnp.where(has_prev, low * cxhalo[0, h], high * c[h, x])
        if x < cells - 1:
            grad = grad + high * c[h, x + 1]
        else:
            grad = grad + jnp.where(has_next, high * cxhalo[1, h], low * c[h, x])
        vgrad_o[h, x] = c[h, x] - TIME_STEP * grad

    for side in range(2):
        h_copy(side).wait_send()
        ch_copy(side).wait_send()
    for side, has in ((0, has_prev), (1, has_next)):
        @pl.when(has)
        def _():
            x_copy(side).wait_send()
            cx_copy(side).wait_send()
    if groups <= 8:
        for d in range(1, groups):
            pay_copy(d).wait_send()
    else:
        pl.loop(1, groups)(lambda d: pay_copy(d).wait_send())


def near_kernel(
    groups, blocks,
    value_h, avoid_h, weight_h, offy_h, offs_h, xy_h, hs_h, count_h,
    next_o, vgrad_o, agrad_o,
    fields, sample, cell, count, pay, got, packed, corner, halo,
    in_sem, pay_send, pay_recv, halo_send, halo_recv, row_in, late, late_near,
):
    _, heads, cells, lines, speeds = fields.shape
    value, avoid = fields.at[0], fields.at[1]
    slots = sample.shape[2]
    me = lax.axis_index("gx")
    hb = lax.axis_index("ha")
    h_next = lax.rem(hb + 1, blocks)
    h_prev = lax.rem(hb + blocks - 1, blocks)
    h_side = (h_prev, h_next)
    has_prev = me > 0
    has_next = me < groups - 1
    first = me == 0

    is_even = lax.rem(hb, 2) == 0
    upper_pair = hb >= blocks // 2
    mate_side = 1 - lax.rem(hb, 2)
    far_side = 1 - mate_side
    mate, far = (lax.rem(hb + blocks - 1 + 2 * s, blocks) for s in (mate_side, far_side))
    level = lax.div(me + 1, 2)
    far_before = jnp.where(
        upper_pair, jnp.minimum(2 * level + 3, groups), jnp.maximum(2 * level - 3, 1)
    )
    earlier = 2 * me + jnp.where(is_even, 1, 0) + far_before
    near_from = jnp.clip(me - 1, 1, far_before)
    near_to = jnp.clip(me + 2, 1, far_before)
    near_far = jnp.minimum(me + 2, groups) - jnp.maximum(me - 1, 1) - (near_to - near_from)
    near_later = jnp.where(has_next, 2, 0) + jnp.where(is_even, 0, 1) + near_far

    barrier = pltpu.get_barrier_semaphore()

    def signal(sem, j, h):
        pl.semaphore_signal(sem, inc=1, device_id=(j, h), device_id_type=MESH)

    def rows(lo, hi, body):
        lax.fori_loop(lo, hi, lambda j, carry: (body(j), carry)[1], 0)

    def signal_pair(sem):
        def body(j):
            signal(sem, j, hb)
            signal(sem, j, mate)

        return body

    def signal_far(sem):
        return lambda j: signal(sem, j, far)

    def wait_some(sem, n):
        @pl.when(n > 0)
        def _():
            pl.semaphore_wait(sem, n)

    @pl.when(first)
    def _():
        for j in range(1, groups):
            for h in (hb, h_prev, h_next):
                signal(barrier, j, h)

    @pl.when(has_prev)
    def _():
        for h in (hb, h_prev, h_next):
            signal(barrier, 0, h)
        rows(me + 1, groups, signal_pair(barrier))
        rows(far_before, groups, signal_far(barrier))

        @pl.when(jnp.logical_not(is_even))
        def _():
            signal(barrier, me, mate)

    loads = [
        pltpu.make_async_copy(a, b, in_sem.at[i])
        for a, b, i in (
            (weight_h, sample.at[0], 0), (offy_h, sample.at[1], 0), (offs_h, sample.at[2], 0),
            (xy_h, cell.at[0], 0), (hs_h, cell.at[1], 0), (count_h, count, 1),
            (value_h, value, 2), (avoid_h, avoid, 2),
        )
    ]
    for load in loads:
        load.start()
    loaded = [pltpu.make_async_copy(r, r, in_sem.at[i]) for r, i in ((sample, 0), (count, 1), (fields, 2))]

    pay[0] = jnp.zeros(pay.shape[1:], jnp.float32)
    pay[groups + 1] = jnp.zeros(pay.shape[1:], jnp.float32)

    def copy(src, dst, send_sem, recv_sem, j, h):
        return pltpu.make_async_remote_copy(
            src, dst, send_sem, recv_sem, device_id=(j, h), device_id_type=MESH
        )

    def x_slot(side):
        return 6 + side * 5

    def h_halo(side, h):
        dst = halo.at[pl.ds(3 * (1 - side), 3)]
        copy(packed.at[side], dst, halo_send, halo_recv, me, h).start()

    def x_halo(side):
        at = x_slot(1 - side)
        copy(packed.at[2 + side], halo.at[at : at + 3], halo_send, halo_recv, me - 1 + 2 * side, hb).start()

    def corner_halo(side, h_to, h):
        at = x_slot(1 - side) + 4 - h_to
        copy(corner.at[side, h_to], halo.at[at], halo_send, halo_recv, me - 1 + 2 * side, h).start()

    def send_side(j, side, h):
        copy(pay.at[j + 1], got.at[me * 5 + 4 - side], pay_send, pay_recv.at[me], j, h).start()

    def send_pair(j):
        copy(pay.at[pl.ds(j, 3)], got.at[pl.ds(me * 5, 3)], pay_send, pay_recv.at[me], j, hb).start()
        send_side(j, mate_side, mate)

    def send_far(j):
        send_side(j, far_side, far)

    loaded[0].wait()
    loaded[1].wait()
    owners = lax.broadcasted_iota(jnp.int32, (groups, groups), 0)
    lanes = lax.broadcasted_iota(jnp.int32, (groups, groups), 1)
    live = jnp.sum(
        jnp.where(owners == lanes, jnp.broadcast_to(count[...], (groups, groups)), 0).astype(jnp.float32),
        axis=1, keepdims=True,
    )
    slot = lax.broadcasted_iota(jnp.int32, (groups, slots), 1).astype(jnp.float32)
    w = jnp.where(slot < live, sample[0], 0.0)
    oy = sample[1]
    state = cell[1]
    head = lax.div(state, speeds)
    row = head * (cells * lines) + cell[0]
    pay[1 : groups + 1, 0, :] = w * (1.0 - oy)
    pay[1 : groups + 1, 1, :] = w * oy
    pay[1 : groups + 1, 2, :] = sample[2]
    pay[1 : groups + 1, 3, :] = (row * speeds + (state - head * speeds)).astype(jnp.float32)
    loaded[2].wait()
    grid = [(h, x) for h in range(heads) for x in range(cells)]
    plane = {(i, h, x): fields[i, h, x] for i in range(2) for h, x in grid}
    whole = jnp.concatenate([plane[0, h, x] for h, x in grid], 1)
    mid = lines // 2
    for side, edge in ((0, 0), (1, 1)):
        h_edge, x_edge = edge * (heads - 1), edge * (cells - 1)
        over_h = [plane[1, h_edge, x] for x in range(cells)]
        over_x = [plane[1, h, x_edge] for h in range(heads)]
        h_tile = [p[:mid] for p in over_h] + [p[mid:] for p in over_h]
        x_tile = [q for p in over_x for q in (p[:mid], p[mid:])]
        for to, tile in ((side, h_tile), (2 + side, x_tile)):
            packed[to, 0] = whole[:mid]
            packed[to, 1] = whole[mid:]
            packed[to, 2] = jnp.concatenate(tile, 1)
        for h in range(2):
            p = plane[0, h * (heads - 1), x_edge]
            corner[side, h] = jnp.concatenate([p[:mid], p[mid:]] * 2, 1)

    @pl.when(has_prev)
    def _():
        pl.semaphore_wait(barrier, earlier)
        send_pair(0)
        send_far(0)

        @pl.when(me == 1)
        def _():
            signal(row_in, 0, hb)

        rows(jnp.maximum(me - 1, 1), me, signal_pair(late_near))
        rows(near_from, near_to, signal_far(late_near))

        @pl.when(is_even)
        def _():
            signal(late_near, me, mate)

        rows(1, me - 1, signal_pair(late))
        rows(1, near_from, signal_far(late))
        rows(near_to, far_before, signal_far(late))

        x_halo(0)
        corner_halo(0, mate_side, mate)

        @pl.when(me - 1 < far_before)
        def _():
            corner_halo(0, far_side, far)

        @pl.when(is_even)
        def _():
            h_halo(mate_side, mate)
            send_side(me, mate_side, mate)

        @pl.when(upper_pair)
        def _():
            h_halo(far_side, far)

        @pl.when(has_next & (me + 1 < far_before))
        def _():
            corner_halo(1, far_side, far)

        rows(1, me, send_pair)
        rows(1, far_before, send_far)

        wait_some(late_near, near_later)

        @pl.when(has_next)
        def _():
            x_halo(1)
            corner_halo(1, mate_side, mate)

            @pl.when(me + 1 >= far_before)
            def _():
                corner_halo(1, far_side, far)

        @pl.when(jnp.logical_not(is_even))
        def _():
            h_halo(mate_side, mate)
            send_side(me, mate_side, mate)

        @pl.when(jnp.logical_not(upper_pair))
        def _():
            h_halo(far_side, far)

        @pl.when(me - 1 >= far_before)
        def _():
            corner_halo(0, far_side, far)

        wait_some(late, 3 * groups - 1 - earlier - near_later)
        rows(me + 1, groups, send_pair)
        rows(far_before, groups, send_far)

    @pl.when(first)
    def _():
        pl.semaphore_wait(row_in, 1)
        for side in range(2):
            h_halo(side, h_side[side])
            send_side(0, side, h_side[side])
        pl.semaphore_wait(barrier, 3 * (groups - 1))
        x_halo(1)
        for side in range(2):
            corner_halo(1, side, h_side[side])
        rows(1, groups, send_pair)
        rows(1, groups, send_far)

    width = heads * cells * speeds
    half, quarter = width // 2, width // 4
    lane = lax.broadcasted_iota(jnp.int32, (1, width), 1)
    place = lax.div(lane, quarter)
    within = lax.rem(lane, quarter)
    even = lax.rem(place, 2) == 0
    left_half = place < 2
    total = heads * blocks
    angles = [np.float32(2.0 * math.pi / total) * np.float32(k) for k in range(total)]
    cosines = [float(np.cos(a)) for a in angles]
    sines = [float(np.sin(a)) for a in angles]
    speed = SLOWEST + SPEED_RANGE * within.astype(jnp.float32) / (speeds - 1)
    turn = [lax.rem(hb * heads + h + total, total) for h in range(-1, heads + 1)]
    cos_of = [pick(cosines, t) for t in turn]
    sin_of = [pick(sines, t) for t in turn]
    cx_own, cy_own = (jnp.where(left_half, a[1], a[2]) * speed for a in (cos_of, sin_of))
    cx_out, cy_out = (jnp.where(left_half, a[0], a[3]) * speed for a in (cos_of, sin_of))

    def shift(a, by):
        return pltpu.roll(a, by % width, 1)

    def forward(here, floor, cx, cy, h_up, h_down, x_up, x_down):
        up, down = upper(here, 0), lower(here, 0)
        rate = cy * (up - down) * 0.5 - (up - 2.0 * here + down) * 0.5
        up = jnp.where(within == quarter - 1, here, shift(here, -1))
        down = jnp.where(within == 0, here, shift(here, 1))
        slope = 0.5 * (up - down)
        size = smooth_abs(slope)
        s_slope = slope / size
        rate = rate + ACCELERATION * size - ACCELERATION * 0.5 * (up - 2.0 * here + down)
        slope = 0.5 * (h_up - h_down)
        size = smooth_abs(slope)
        h_slope = slope / size
        rate = rate + TURN_RATE * size - TURN_RATE * 0.5 * (h_up - 2.0 * here + h_down)
        rate = rate + cx * (x_up - x_down) * 0.5 - (x_up - 2.0 * here + x_down) * 0.5
        excess = SHARPNESS * (here - TIME_STEP * rate - floor)
        small = jnp.exp(-jnp.abs(excess))
        share = jnp.where(excess >= 0.0, 1.0, small) / (1.0 + small)
        pull = (0.5 * TURN_RATE) * share * h_slope
        keep = (0.5 * TURN_RATE) * share
        return excess, small, share, s_slope, pull - keep, -pull - keep

    def all_halos(sending):
        def wait(n):
            view = halo.at[0:n]
            c = copy(view, view, halo_send, halo_recv, me, h_next)
            c.wait_send() if sending else c.wait_recv()

        @pl.when(has_prev & has_next)
        def _():
            wait(16)

        @pl.when(jnp.logical_not(has_prev & has_next))
        def _():
            wait(11)

    def unpack(a):
        return {(h, x): a[:, n * speeds : (n + 1) * speeds] for n, (h, x) in enumerate(grid)}

    all_halos(False)
    def tall_pair(top, bottom):
        return jnp.concatenate([top, bottom], 0)

    own = whole
    floor = jnp.concatenate([plane[1, h, x] for h, x in grid], 1)
    hp, hn, xp, xn = (tall_pair(halo[i], halo[i + 1]) for i in (0, 3, 6, 11))
    hp_floor, hn_floor, xp_floor, xn_floor = (halo[i] for i in (2, 5, 8, 13))
    on_even, on_odd = [], []
    for i in (9, 10, 14, 15):
        tile = halo[i]
        other = shift(tile, quarter)
        on_even.append(tall_pair(tile, other))
        on_odd.append(tall_pair(other, tile))
    edge_h = shift(jnp.where(left_half, hn, hp), half)
    edge_x = jnp.where(even, shift(xp, -quarter), shift(xn, quarter))
    up_x = jnp.where(even, shift(own, -quarter), jnp.where(has_next, edge_x, own))
    down_x = jnp.where(even, jnp.where(has_prev, edge_x, own), shift(own, quarter))
    excess, small, share, s_slope, ahead, back = forward(
        own, floor, cx_own, cy_own,
        shift(jnp.where(left_half, hn, own), half), shift(jnp.where(left_half, own, hp), half),
        up_x, down_x,
    )
    next_v = unpack(floor + (jnp.maximum(excess, 0.0) + jnp.log1p(small)) / SHARPNESS)
    for h, x in grid:
        next_o[h, x] = next_v[h, x]
    rest = unpack(jnp.where(excess >= 0.0, small, 1.0) / (1.0 + small))
    share, s_slope, ahead, back = (unpack(a) for a in (share, s_slope, ahead, back))

    up_x = jnp.where(even, shift(edge_h, -quarter), jnp.where(left_half, on_odd[2], on_odd[3]))
    down_x = jnp.where(even, jnp.where(left_half, on_even[0], on_even[1]), shift(edge_h, quarter))
    edge_floor = tall_pair(
        jnp.where(left_half, hp_floor, shift(hn_floor, half)),
        jnp.where(left_half, shift(hp_floor, half), hn_floor),
    )
    out = forward(
        edge_h, edge_floor, cx_out, cy_out,
        jnp.where(left_half, own, hn), jnp.where(left_half, hp, own),
        jnp.where(even | has_next, up_x, edge_h), jnp.where(even & jnp.logical_not(has_prev), edge_h, down_x),
    )
    out = unpack(jnp.where(left_half, out[4], out[5]))
    for x in range(cells):
        ahead[-1, x], back[heads, x] = out[0, x], out[1, x]

    turned = shift(edge_x, half)
    up_h = jnp.where(left_half, turned, jnp.where(even, on_even[1], on_odd[3]))
    down_h = jnp.where(left_half, jnp.where(even, on_even[0], on_odd[2]), turned)
    edge_floor = tall_pair(
        jnp.where(even, xp_floor, shift(xn_floor, quarter)),
        jnp.where(even, shift(xp_floor, -quarter), xn_floor),
    )
    out = forward(
        edge_x, edge_floor, cx_own, cy_own,
        up_h, down_h, jnp.where(even, own, xn), jnp.where(even, xp, own),
    )
    out = unpack(out[2])
    for h in range(heads):
        share[h, -1], share[h, cells] = out[h, 0], out[h, 1]
    speed = SLOWEST + SPEED_RANGE * lax.broadcasted_iota(jnp.int32, (1, speeds), 1).astype(
        jnp.float32
    ) / (speeds - 1)
    cx = [cos_of[h + 1] * speed for h in range(heads)]
    cy = [sin_of[h + 1] * speed for h in range(heads)]

    span = cells * lines
    inside = lax.broadcasted_iota(jnp.int32, (heads * span, slots), 0)
    edge = lax.broadcasted_iota(jnp.int32, (heads * lines, slots), 0)
    edge = lax.div(edge, lines) * span + lax.rem(edge, lines)
    side_rows = lax.broadcasted_iota(jnp.int32, (span, slots), 0)
    ids = [
        i.astype(jnp.float32).astype(jnp.bfloat16)
        for i in (edge + (cells - 1) * lines, inside, edge, side_rows + (heads - 1) * span, side_rows)
    ]
    speed_id = lax.broadcasted_iota(jnp.int32, (speeds, slots), 0).astype(jnp.float32)
    speed_id = speed_id.astype(jnp.bfloat16)

    def tall(row, n):
        part = jnp.broadcast_to(row, (16, slots)).astype(jnp.bfloat16)
        return jnp.concatenate([part] * (n // 16), 0)

    def deposit(one, row_id):
        n = row_id.shape[0]
        weight0, weight1, up_s, code = one[0:1], one[1:2], one[2:3], one[3:4]
        row = jnp.floor(code * (1.0 / speeds))
        cell = code - row * speeds
        here, above_it = row_id == tall(row, n), row_id == tall(row + 1.0, n)
        zero = jnp.zeros(row_id.shape, jnp.bfloat16)
        high, low = [], []
        for f in (1.0 - up_s, up_s):
            a, b = weight0 * f, weight1 * f
            for part in (high, low):
                part.append(jnp.where(here, tall(a, n), jnp.where(above_it, tall(b, n), zero)))
                a, b = (t - t.astype(jnp.bfloat16).astype(jnp.float32) for t in (a, b))
        left = jnp.concatenate([jnp.concatenate(part, 1) for part in (high, low)], 0)
        one_hot = jnp.ones(speed_id.shape, jnp.bfloat16)
        right = jnp.concatenate(
            [
                jnp.where(speed_id == tall(c, speeds), one_hot, jnp.zeros_like(one_hot))
                for c in (cell, cell + 1.0)
            ],
            1,
        )
        both = lax.dot_general(
            left, right, (((1,), (1,)), ((), ())), preferred_element_type=jnp.float32
        )
        return both[:n] + both[n:]

    def payload(g, lo, n):
        view = got.at[pl.ds(g * 5 + lo, n)]
        return copy(view, view, pay_send, pay_recv.at[g], me, h_next)

    def collect(g, sums):
        payload(g, 0, 5).wait_recv()
        return tuple(s + deposit(got[g * 5 + i], ids[i]) for i, s in enumerate(sums))

    sums = tuple(deposit(pay[me + i], ids[i]) for i in range(3)) + tuple(
        jnp.zeros((i.shape[0], speeds), jnp.float32) for i in ids[3:]
    )
    sums = lax.fori_loop(me + 1, groups, collect, sums)
    sums = lax.fori_loop(0, me, collect, sums)
    payload(me, 3, 2).wait_recv()
    sums = sums[:3] + tuple(s + deposit(got[me * 5 + 3 + i], ids[3 + i]) for i, s in enumerate(sums[3:]))

    adj, c = {}, {}
    for n, (h, x) in enumerate(grid):
        adj[h, x] = sums[1][n * lines : (n + 1) * lines]
        c[h, x] = adj[h, x] * share[h, x]
    for h in range(heads):
        c[h, -1] = sums[0][h * lines : (h + 1) * lines] * share[h, -1]
        c[h, cells] = sums[2][h * lines : (h + 1) * lines] * share[h, cells]
    for x in range(cells):
        adj[-1, x] = sums[3][x * lines : (x + 1) * lines]
        adj[heads, x] = sums[4][x * lines : (x + 1) * lines]

    for h, x in grid:
        agrad_o[h, x] = adj[h, x] * rest[h, x]
        here = c[h, x]
        grad = spread((0.5 * cy[h] - 0.5) * here, (-0.5 * cy[h] - 0.5) * here, 0)
        pull = (0.5 * ACCELERATION) * here * s_slope[h, x]
        keep = (0.5 * ACCELERATION) * here
        grad = grad + spread(pull - keep, -pull - keep, 1)
        grad = grad + (2.0 + TURN_RATE + ACCELERATION) * here
        grad = grad + adj[h - 1, x] * ahead[h - 1, x] + adj[h + 1, x] * back[h + 1, x]
        low, high = 0.5 * cx[h] - 0.5, -0.5 * cx[h] - 0.5
        if x > 0:
            grad = grad + low * c[h, x - 1]
        else:
            grad = grad + jnp.where(has_prev, low * c[h, -1], high * here)
        if x < cells - 1:
            grad = grad + high * c[h, x + 1]
        else:
            grad = grad + jnp.where(has_next, high * c[h, cells], low * here)
        vgrad_o[h, x] = here - TIME_STEP * grad

    all_halos(True)
    view = got.at[0 : 5 * groups - 3]
    copy(view, view, pay_send, pay_recv.at[0], me, h_next).wait_send()


def write_out(next_v, vgrad_v, agrad_v, next_o, vgrad_o, agrad_o, sem):
    copies = [
        pltpu.make_async_copy(a, b, sem.at[i])
        for i, (a, b) in enumerate(((next_v, next_o), (vgrad_v, vgrad_o), (agrad_v, agrad_o)))
    ]
    for copy in copies:
        copy.start()
    for copy in copies:
        copy.wait()


def on_device(groups, blocks, value, avoid, weight, offy, offs, xy, hs, count):
    slots = weight.shape[3]
    value = jnp.transpose(value, (0, 2, 3, 1))
    avoid = jnp.transpose(avoid, (0, 2, 3, 1))
    weight, offy, offs, xy, hs = (a.reshape(groups, slots) for a in (weight, offy, offs, xy, hs))
    count = count.reshape(1, groups)
    heads, cells, lines, speeds = value.shape
    f32 = jnp.float32
    dma = pltpu.SemaphoreType.DMA
    field = pltpu.VMEM(value.shape, f32)
    x_pair = pltpu.VMEM((2, heads, lines, speeds), f32)
    h_pair = pltpu.VMEM((2, cells, lines, speeds), f32)
    near = 2 < groups <= 8 and blocks == 4 and heads == cells == 2 and 4 * speeds == slots == 128 and lines == 16
    sample = pltpu.VMEM((groups, slots), f32)
    index = pltpu.VMEM((groups, slots), jnp.int32)
    counts = pltpu.VMEM((1, groups), jnp.int32)
    if near:
        scratch = [
            pltpu.VMEM((2, *value.shape), f32),
            pltpu.VMEM((5, groups, slots), f32), pltpu.VMEM((2, groups, slots), jnp.int32), counts,
            pltpu.VMEM((groups + 2, 4, slots), f32), pltpu.VMEM((5 * groups, 4, slots), f32),
            pltpu.VMEM((4, 3, lines // 2, slots), f32), pltpu.VMEM((2, 2, lines // 2, slots), f32),
            pltpu.VMEM((16, lines // 2, slots), f32),
            dma((3,)), dma, dma((groups,)), dma, dma,
            *[pltpu.SemaphoreType.REGULAR] * 3,
        ]
    else:
        scratch = [
            field, field, sample, sample, sample, index, index, counts,
            pltpu.VMEM((groups, ROWS, slots), f32), pltpu.VMEM((groups, ROWS, slots), f32),
            x_pair, h_pair, field, h_pair, x_pair, h_pair,
            dma((8,)), dma((groups,)), dma((groups,)), *[dma((2,))] * 8, dma,
        ]
    outs = pl.pallas_call(
        functools.partial(near_kernel if near else kernel, groups, blocks),
        out_shape=[pltpu.VMEM(value.shape, f32)] * 3,
        in_specs=[pl.BlockSpec(memory_space=pltpu.HBM)] * 8,
        out_specs=[pl.BlockSpec(memory_space=pltpu.VMEM)] * 3,
        scratch_shapes=scratch,
        compiler_params=pltpu.CompilerParams(collective_id=0, has_side_effects=True),
        name="step",
    )(value, avoid, weight, offy, offs, xy, hs, count)
    outs = pl.pallas_call(
        write_out,
        out_shape=[jax.ShapeDtypeStruct(value.shape, f32)] * 3,
        in_specs=[pl.BlockSpec(memory_space=pl.ANY)] * 3,
        out_specs=[pl.BlockSpec(memory_space=pl.ANY)] * 3,
        scratch_shapes=[dma((3,))],
        compiler_params=pltpu.CompilerParams(vmem_limit_bytes=1 << 20),
        name="write_out",
    )(*outs)
    return tuple(jnp.transpose(o, (0, 3, 1, 2)) for o in outs)


def solution(mesh):
    field = P("ha", None, "gx", None)
    sample = P("gx", "ha", None, None)
    return jax.shard_map(
        functools.partial(on_device, mesh.shape["gx"], mesh.shape["ha"]),
        mesh=mesh,
        in_specs=(field, field, sample, sample, sample, sample, sample, P("gx", "ha", None)),
        out_specs=(field, field, field),
        check_vma=False,
    )
```

```python
import functools
import math

import jax
import jax.numpy as jnp
import numpy as np
from jax import lax
from jax.experimental import pallas as pl
from jax.experimental.pallas import tpu as pltpu
from jax.sharding import PartitionSpec as P

TIME_STEP = 0.3
SHARPNESS = 2.0
SOFTENING = 0.1
TURN_RATE = 0.5
ACCELERATION = 0.3
SLOWEST = 0.2
SPEED_RANGE = 0.8
ROWS = 8
MESH = pl.DeviceIdType.MESH


def smooth_abs(slope):
    return jnp.sqrt(slope * slope + SOFTENING * SOFTENING)


def upper(plane, axis):
    n = plane.shape[axis]
    return jnp.concatenate(
        [lax.slice_in_dim(plane, 1, n, axis=axis), lax.slice_in_dim(plane, n - 1, n, axis=axis)], axis
    )


def lower(plane, axis):
    n = plane.shape[axis]
    return jnp.concatenate(
        [lax.slice_in_dim(plane, 0, 1, axis=axis), lax.slice_in_dim(plane, 0, n - 1, axis=axis)], axis
    )


def spread(up, down, axis):
    n = up.shape[axis]
    from_lower = jnp.concatenate(
        [lax.slice_in_dim(down, 0, 1, axis=axis), lax.slice_in_dim(up, 0, n - 1, axis=axis)], axis
    )
    from_upper = jnp.concatenate(
        [lax.slice_in_dim(down, 1, n, axis=axis), lax.slice_in_dim(up, n - 1, n, axis=axis)], axis
    )
    return from_lower + from_upper


def pick(table, index):
    chosen = jnp.float32(table[0])
    for i in range(1, len(table)):
        chosen = jnp.where(index == i, jnp.float32(table[i]), chosen)
    return chosen


def kernel(
    groups, blocks,
    value_h, avoid_h, weight_h, offy_h, offs_h, xy_h, hs_h, count_h,
    next_o, vgrad_o, agrad_o,
    value, avoid, weight, offy, offs, xy, hs, count,
    pay, got, xhalo, hhalo, carried, turned, cxhalo, chhalo,
    in_sem, pay_send, pay_recv, x_send, x_recv, h_send, h_recv,
    cx_send, cx_recv, ch_send, ch_recv, self_sem,
):
    heads, cells, lines, speeds = value.shape
    slots = weight.shape[1]
    me = lax.axis_index("gx")
    hb = lax.axis_index("ha")
    h_next = lax.rem(hb + 1, blocks)
    h_prev = lax.rem(hb + blocks - 1, blocks)
    has_prev = me > 0
    has_next = me < groups - 1

    barrier = pltpu.get_barrier_semaphore()

    def greet(d):
        pl.semaphore_signal(
            barrier, inc=1, device_id=(lax.rem(me + d, groups), hb), device_id_type=MESH
        )

    if groups <= 8:
        for d in range(1, groups):
            greet(d)
    else:
        pl.loop(1, groups)(greet)
    for other in (h_prev, h_next):
        pl.semaphore_signal(barrier, inc=1, device_id=(me, other), device_id_type=MESH)

    pairs = (
        (weight_h, weight), (offy_h, offy), (offs_h, offs), (xy_h, xy), (hs_h, hs), (count_h, count),
        (value_h, value), (avoid_h, avoid),
    )
    loads = [pltpu.make_async_copy(a, b, in_sem.at[i]) for i, (a, b) in enumerate(pairs)]
    for load in loads:
        load.start()
    for load in loads[:6]:
        load.wait()

    owners = lax.broadcasted_iota(jnp.int32, (groups, groups), 0)
    lanes = lax.broadcasted_iota(jnp.int32, (groups, groups), 1)
    live = jnp.sum(
        jnp.where(owners == lanes, jnp.broadcast_to(count[...], (groups, groups)), 0).astype(jnp.float32),
        axis=1, keepdims=True,
    )
    slot = lax.broadcasted_iota(jnp.int32, (groups, slots), 1).astype(jnp.float32)
    w = jnp.where(slot < live, weight[...], 0.0)
    oy = offy[...]
    os = offs[...]
    state = hs[...]
    head = lax.div(state, speeds)
    pay[:, 0, :] = w * (1.0 - oy)
    pay[:, 1, :] = w * oy
    pay[:, 2, :] = 1.0 - os
    pay[:, 3, :] = os
    pay[:, 4, :] = (head * (cells * lines) + xy[...]).astype(jnp.float32)
    pay[:, 5, :] = (state - head * speeds).astype(jnp.float32)
    pay[:, 6, :] = jnp.zeros((groups, slots), jnp.float32)
    pay[:, 7, :] = jnp.zeros((groups, slots), jnp.float32)

    loads[6].wait()
    pl.semaphore_wait(barrier, groups - 1 + 2)

    def h_copy(side):
        return pltpu.make_async_remote_copy(
            value.at[0 if side == 0 else heads - 1], hhalo.at[1 - side],
            h_send.at[side], h_recv.at[1 - side],
            device_id=(me, h_prev if side == 0 else h_next), device_id_type=MESH,
        )

    def x_copy(side):
        return pltpu.make_async_remote_copy(
            value.at[:, 0 if side == 0 else cells - 1], xhalo.at[1 - side],
            x_send.at[side], x_recv.at[1 - side],
            device_id=(me - 1 if side == 0 else me + 1, hb), device_id_type=MESH,
        )

    def pay_copy(d):
        peer = lax.rem(me + d, groups)
        return pltpu.make_async_remote_copy(
            pay.at[peer], got.at[d], pay_send.at[d], pay_recv.at[d],
            device_id=(peer, hb), device_id_type=MESH,
        )

    for side in range(2):
        h_copy(side).start()
    for side, has in ((0, has_prev), (1, has_next)):
        @pl.when(has)
        def _():
            x_copy(side).start()

    if groups <= 8:
        for d in range(groups - 1, 0, -1):
            pay_copy(d).start()
    else:
        pl.loop(1, groups)(lambda d: pay_copy(d).start())
    mine = pltpu.make_async_copy(pay.at[me], got.at[0], self_sem)
    mine.start()
    loads[7].wait()

    for side, has in ((0, has_prev), (1, has_next)):
        @pl.when(jnp.logical_not(has))
        def _():
            xhalo[side] = value[:, 0 if side == 0 else cells - 1]

    total = heads * blocks
    angles = [np.float32(2.0 * math.pi / total) * np.float32(k) for k in range(total)]
    cosines = [float(np.cos(a)) for a in angles]
    sines = [float(np.sin(a)) for a in angles]
    speed = SLOWEST + SPEED_RANGE * lax.broadcasted_iota(jnp.int32, (1, speeds), 1).astype(
        jnp.float32
    ) / (speeds - 1)
    cx = [pick(cosines, hb * heads + h) * speed for h in range(heads)]
    cy = [pick(sines, hb * heads + h) * speed for h in range(heads)]
    grid = [(h, x) for h in range(heads) for x in range(cells)]
    v = {(h, x): value[h, x] for h, x in grid}
    part, s_slope = {}, {}
    for h, x in grid:
        here = v[h, x]
        up, down = upper(here, 0), lower(here, 0)
        term = cy[h] * (up - down) * 0.5 - (up - 2.0 * here + down) * 0.5
        up, down = upper(here, 1), lower(here, 1)
        slope = 0.5 * (up - down)
        size = smooth_abs(slope)
        s_slope[h, x] = slope / size
        part[h, x] = term + ACCELERATION * size - ACCELERATION * 0.5 * (up - 2.0 * here + down)

    for side in range(2):
        h_copy(side).wait_recv()
    for side, has in ((0, has_prev), (1, has_next)):
        @pl.when(has)
        def _():
            x_copy(1 - side).wait_recv()
    for x in range(cells):
        v[-1, x] = hhalo[0, x]
        v[heads, x] = hhalo[1, x]
    for h in range(heads):
        v[h, -1] = xhalo[0, h]
        v[h, cells] = xhalo[1, h]

    share, h_slope, above = {}, {}, {}
    for h, x in grid:
        here = v[h, x]
        up, down = v[h + 1, x], v[h - 1, x]
        slope = 0.5 * (up - down)
        size = smooth_abs(slope)
        h_slope[h, x] = slope / size
        turning = TURN_RATE * size - TURN_RATE * 0.5 * (up - 2.0 * here + down)
        up, down = v[h, x + 1], v[h, x - 1]
        across = cx[h] * (up - down) * 0.5 - (up - 2.0 * here + down) * 0.5
        relaxed = here - TIME_STEP * (across + part[h, x] + turning)
        floor = avoid[h, x]
        excess = SHARPNESS * (relaxed - floor)
        small = jnp.exp(-jnp.abs(excess))
        share[h, x] = jnp.where(excess >= 0.0, 1.0, small) / (1.0 + small)
        above[h, x] = (excess, small)

    rows = heads * cells * lines
    row_id = lax.broadcasted_iota(jnp.int32, (rows, slots), 0).astype(jnp.float32)
    speed_id = lax.broadcasted_iota(jnp.int32, (speeds, slots), 0).astype(jnp.float32)

    def operands(d):
        one = got[d]
        cell = jnp.broadcast_to(one[4:5], (rows, slots))
        left = jnp.where(row_id == cell, one[0:1], jnp.where(row_id == cell + 1.0, one[1:2], 0.0))
        cell = jnp.broadcast_to(one[5:6], (speeds, slots))
        right = jnp.where(
            speed_id == cell, one[2:3], jnp.where(speed_id == cell + 1.0, one[3:4], 0.0)
        )
        return left, right

    def product(left, right):
        return lax.dot_general(
            left, right, (((1,), (1,)), ((), ())),
            precision=lax.Precision.HIGHEST, preferred_element_type=jnp.float32,
        )

    mine.wait()
    if groups <= 8:
        for d in range(1, groups):
            pay_copy(d).wait_recv()
        both = [operands(d) for d in range(groups)]
        deposit = product(
            jnp.concatenate([b[0] for b in both], 1), jnp.concatenate([b[1] for b in both], 1)
        )
    else:
        pl.loop(1, groups)(lambda d: pay_copy(d).wait_recv())
        deposit = lax.fori_loop(
            0, groups, lambda d, so_far: so_far + product(*operands(d)),
            jnp.zeros((rows, speeds), jnp.float32),
        )

    c, adj = {}, {}
    for n, (h, x) in enumerate(grid):
        adjoint = deposit[n * lines : (n + 1) * lines]
        c[h, x] = adjoint * share[h, x]
        carried[h, x] = c[h, x]
        adj[h, x] = adjoint
    def cx_copy(side):
        return pltpu.make_async_remote_copy(
            carried.at[:, 0 if side == 0 else cells - 1], cxhalo.at[1 - side],
            cx_send.at[side], cx_recv.at[1 - side],
            device_id=(me - 1 if side == 0 else me + 1, hb), device_id_type=MESH,
        )

    for side, has in ((0, has_prev), (1, has_next)):
        @pl.when(has)
        def _():
            cx_copy(side).start()

        @pl.when(jnp.logical_not(has))
        def _():
            cxhalo[side] = jnp.zeros_like(cxhalo[side])
    ahead, back = {}, {}
    for h, x in grid:
        pull = (0.5 * TURN_RATE) * c[h, x] * h_slope[h, x]
        keep = (0.5 * TURN_RATE) * c[h, x]
        ahead[h, x] = pull - keep
        back[h, x] = -pull - keep
    for x in range(cells):
        turned[0, x] = back[0, x]
        turned[1, x] = ahead[heads - 1, x]

    def ch_copy(side):
        return pltpu.make_async_remote_copy(
            turned.at[side], chhalo.at[1 - side], ch_send.at[side], ch_recv.at[1 - side],
            device_id=(me, h_prev if side == 0 else h_next), device_id_type=MESH,
        )

    for side in range(2):
        ch_copy(side).start()

    local = {}
    for h, x in grid:
        excess, small = above[h, x]
        next_o[h, x] = avoid[h, x] + (jnp.maximum(excess, 0.0) + jnp.log1p(small)) / SHARPNESS
        agrad_o[h, x] = adj[h, x] * (jnp.where(excess >= 0.0, small, 1.0) / (1.0 + small))
        here = c[h, x]
        grad = spread((0.5 * cy[h] - 0.5) * here, (-0.5 * cy[h] - 0.5) * here, 0)
        pull = (0.5 * ACCELERATION) * here * s_slope[h, x]
        keep = (0.5 * ACCELERATION) * here
        grad = grad + spread(pull - keep, -pull - keep, 1)
        local[h, x] = grad + (2.0 + TURN_RATE + ACCELERATION) * here

    for side in range(2):
        ch_copy(side).wait_recv()
    for side, has in ((0, has_prev), (1, has_next)):
        @pl.when(has)
        def _():
            cx_copy(1 - side).wait_recv()
    for h, x in grid:
        grad = local[h, x]
        grad = grad + (ahead[h - 1, x] if h > 0 else chhalo[0, x])
        grad = grad + (back[h + 1, x] if h < heads - 1 else chhalo[1, x])
        low, high = 0.5 * cx[h] - 0.5, -0.5 * cx[h] - 0.5
        if x > 0:
            grad = grad + low * c[h, x - 1]
        else:
            grad = grad + jnp.where(has_prev, low * cxhalo[0, h], high * c[h, x])
        if x < cells - 1:
            grad = grad + high * c[h, x + 1]
        else:
            grad = grad + jnp.where(has_next, high * cxhalo[1, h], low * c[h, x])
        vgrad_o[h, x] = c[h, x] - TIME_STEP * grad

    for side in range(2):
        h_copy(side).wait_send()
        ch_copy(side).wait_send()
    for side, has in ((0, has_prev), (1, has_next)):
        @pl.when(has)
        def _():
            x_copy(side).wait_send()
            cx_copy(side).wait_send()
    if groups <= 8:
        for d in range(1, groups):
            pay_copy(d).wait_send()
    else:
        pl.loop(1, groups)(lambda d: pay_copy(d).wait_send())


def near_kernel(
    groups, blocks,
    value_h, avoid_h, weight_h, offy_h, offs_h, xy_h, hs_h, count_h,
    next_o, vgrad_o, agrad_o,
    fields, sample, cell, count, pay, got, packed, corner, halo,
    in_sem, pay_send, pay_recv, halo_send, halo_recv, row_in, late, late_near,
):
    _, heads, cells, lines, speeds = fields.shape
    value, avoid = fields.at[0], fields.at[1]
    slots = sample.shape[2]
    me = lax.axis_index("gx")
    hb = lax.axis_index("ha")
    h_next = lax.rem(hb + 1, blocks)
    h_prev = lax.rem(hb + blocks - 1, blocks)
    h_side = (h_prev, h_next)
    has_prev = me > 0
    has_next = me < groups - 1
    first = me == 0

    is_even = lax.rem(hb, 2) == 0
    upper_pair = hb >= blocks // 2
    mate_side = 1 - lax.rem(hb, 2)
    far_side = 1 - mate_side
    mate, far = (lax.rem(hb + blocks - 1 + 2 * s, blocks) for s in (mate_side, far_side))
    level = lax.div(me + 1, 2)
    mate_before = jnp.where(is_even, jnp.minimum(2 * level + 1, groups), jnp.maximum(2 * level - 1, 1))
    far_before = jnp.where(
        upper_pair,
        jnp.minimum(2 * level + jnp.where(is_even, 3, 1), groups),
        jnp.maximum(2 * level - jnp.where(is_even, 1, 3), 1),
    )
    earlier = me + mate_before + far_before

    def near_rows(before):
        return jnp.clip(me - 1, 1, before), jnp.clip(me + 2, 1, before)

    mate_near, far_near = near_rows(mate_before), near_rows(far_before)
    around = jnp.minimum(me + 2, groups) - jnp.maximum(me - 1, 1)
    near_later = jnp.where(has_next, 1, 0) + 2 * around
    for low, high in (mate_near, far_near):
        near_later = near_later - (high - low)

    barrier = pltpu.get_barrier_semaphore()

    def signal(sem, j, h):
        pl.semaphore_signal(sem, inc=1, device_id=(j, h), device_id_type=MESH)

    def rows(lo, hi, body):
        lax.fori_loop(lo, hi, lambda j, carry: (body(j), carry)[1], 0)

    def signal_at(sem, h):
        return lambda j: signal(sem, j, h)

    def wait_some(sem, n):
        @pl.when(n > 0)
        def _():
            pl.semaphore_wait(sem, n)

    @pl.when(first)
    def _():
        for j in range(groups - 1, 0, -1):
            for h in (far, mate, hb):
                signal(barrier, j, h)

    @pl.when(has_prev)
    def _():
        for before, h in ((far_before, far), (mate_before, mate), (me + 1, hb)):
            rows(before, groups, lambda j: signal(barrier, groups - 1 + before - j, h))
        for h in (far, mate, hb):
            signal(barrier, 0, h)

    loads = [
        pltpu.make_async_copy(a, b, in_sem.at[i])
        for a, b, i in (
            (weight_h, sample.at[0], 0), (offy_h, sample.at[1], 0), (offs_h, sample.at[2], 0),
            (xy_h, cell.at[0], 0), (hs_h, cell.at[1], 0), (count_h, count, 1),
            (value_h, value, 2), (avoid_h, avoid, 2),
        )
    ]
    for load in loads:
        load.start()
    loaded = [pltpu.make_async_copy(r, r, in_sem.at[i]) for r, i in ((sample, 0), (count, 1), (fields, 2))]

    pay[0] = jnp.zeros(pay.shape[1:], jnp.float32)
    pay[groups + 1] = jnp.zeros(pay.shape[1:], jnp.float32)

    def copy(src, dst, send_sem, recv_sem, j, h):
        return pltpu.make_async_remote_copy(
            src, dst, send_sem, recv_sem, device_id=(j, h), device_id_type=MESH
        )

    def x_slot(side):
        return 6 + side * 5

    def h_halo(side, h):
        dst = halo.at[pl.ds(3 * (1 - side), 3)]
        copy(packed.at[side], dst, halo_send, halo_recv, me, h).start()

    def x_halo(side):
        at = x_slot(1 - side)
        copy(packed.at[2 + side], halo.at[at : at + 3], halo_send, halo_recv, me - 1 + 2 * side, hb).start()

    def corner_halo(side, h_to, h):
        at = x_slot(1 - side) + 4 - h_to
        copy(corner.at[side, h_to], halo.at[at], halo_send, halo_recv, me - 1 + 2 * side, h).start()

    def send_side(j, side, h):
        copy(pay.at[j + 1], got.at[me * 5 + 4 - side], pay_send, pay_recv.at[me], j, h).start()

    def send_own(j):
        copy(pay.at[pl.ds(j, 3)], got.at[pl.ds(me * 5, 3)], pay_send, pay_recv.at[me], j, hb).start()

    def send_mate(j):
        send_side(j, mate_side, mate)

    def send_far(j):
        send_side(j, far_side, far)

    loaded[0].wait()
    loaded[1].wait()
    owners = lax.broadcasted_iota(jnp.int32, (groups, groups), 0)
    lanes = lax.broadcasted_iota(jnp.int32, (groups, groups), 1)
    live = jnp.sum(
        jnp.where(owners == lanes, jnp.broadcast_to(count[...], (groups, groups)), 0).astype(jnp.float32),
        axis=1, keepdims=True,
    )
    slot = lax.broadcasted_iota(jnp.int32, (groups, slots), 1).astype(jnp.float32)
    w = jnp.where(slot < live, sample[0], 0.0)
    oy = sample[1]
    state = cell[1]
    head = lax.div(state, speeds)
    row = head * (cells * lines) + cell[0]
    pay[1 : groups + 1, 0, :] = w * (1.0 - oy)
    pay[1 : groups + 1, 1, :] = w * oy
    pay[1 : groups + 1, 2, :] = sample[2]
    pay[1 : groups + 1, 3, :] = (row * speeds + (state - head * speeds)).astype(jnp.float32)
    pltpu.make_async_copy(pay.at[pl.ds(me, 3)], got.at[pl.ds(me * 5, 3)], pay_recv.at[me]).start()
    loaded[2].wait()
    grid = [(h, x) for h in range(heads) for x in range(cells)]
    plane = {(i, h, x): fields[i, h, x] for i in range(2) for h, x in grid}
    whole = jnp.concatenate([plane[0, h, x] for h, x in grid], 1)
    mid = lines // 2
    for side, edge in ((0, 0), (1, 1)):
        h_edge, x_edge = edge * (heads - 1), edge * (cells - 1)
        over_h = [plane[1, h_edge, x] for x in range(cells)]
        over_x = [plane[1, h, x_edge] for h in range(heads)]
        h_tile = [p[:mid] for p in over_h] + [p[mid:] for p in over_h]
        x_tile = [q for p in over_x for q in (p[:mid], p[mid:])]
        for to, tile in ((side, h_tile), (2 + side, x_tile)):
            packed[to, 0] = whole[:mid]
            packed[to, 1] = whole[mid:]
            packed[to, 2] = jnp.concatenate(tile, 1)
        for h in range(2):
            p = plane[0, h * (heads - 1), x_edge]
            corner[side, h] = jnp.concatenate([p[:mid], p[mid:]] * 2, 1)

    @pl.when(has_prev)
    def _():
        pl.semaphore_wait(barrier, earlier)
        @pl.when(me == 1)
        def _():
            signal(row_in, 0, hb)

        rows(1, me - 1, signal_at(late, hb))
        for (low, high), before, h in ((mate_near, mate_before, mate), (far_near, far_before, far)):
            rows(1, low, signal_at(late, h))
            rows(high, before, signal_at(late, h))
        send_own(0)
        send_mate(0)
        send_far(0)
        rows(jnp.maximum(me - 1, 1), me, signal_at(late_near, hb))
        rows(*mate_near, signal_at(late_near, mate))
        rows(*far_near, signal_at(late_near, far))

        x_halo(0)
        others = ((mate_before, mate_side, mate), (far_before, far_side, far))

        def near_halos(comes):
            for before, side, h in others:
                pl.when(comes(me - 1, before))(functools.partial(corner_halo, 0, side, h))
                pl.when(comes(me, before))(functools.partial(h_halo, side, h))
                pl.when(comes(me + 1, before) & has_next)(functools.partial(corner_halo, 1, side, h))

        near_halos(lambda j, before: j < before)
        rows(1, me, send_own)
        rows(1, mate_before, send_mate)
        rows(1, far_before, send_far)

        wait_some(late_near, near_later)
        pl.when(has_next)(functools.partial(x_halo, 1))
        near_halos(lambda j, before: j >= before)
        wait_some(late, 3 * groups - 1 - earlier - near_later)
        rows(me + 1, groups, send_own)
        rows(mate_before, groups, send_mate)
        rows(far_before, groups, send_far)

    @pl.when(first)
    def _():
        pl.semaphore_wait(row_in, 1)
        for side in range(2):
            h_halo(side, h_side[side])
            send_side(0, side, h_side[side])
        pl.semaphore_wait(barrier, 3 * (groups - 1))
        x_halo(1)
        for side in range(2):
            corner_halo(1, side, h_side[side])
        rows(1, groups, send_own)
        rows(1, groups, send_mate)
        rows(1, groups, send_far)

    width = heads * cells * speeds
    half, quarter = width // 2, width // 4
    lane = lax.broadcasted_iota(jnp.int32, (1, width), 1)
    place = lax.div(lane, quarter)
    within = lax.rem(lane, quarter)
    even = lax.rem(place, 2) == 0
    left_half = place < 2
    total = heads * blocks
    angles = [np.float32(2.0 * math.pi / total) * np.float32(k) for k in range(total)]
    cosines = [float(np.cos(a)) for a in angles]
    sines = [float(np.sin(a)) for a in angles]
    speed = SLOWEST + SPEED_RANGE * within.astype(jnp.float32) / (speeds - 1)
    turn = [lax.rem(hb * heads + h + total, total) for h in range(-1, heads + 1)]
    cos_of = [pick(cosines, t) for t in turn]
    sin_of = [pick(sines, t) for t in turn]
    cx_own, cy_own = (jnp.where(left_half, a[1], a[2]) * speed for a in (cos_of, sin_of))
    cx_out, cy_out = (jnp.where(left_half, a[0], a[3]) * speed for a in (cos_of, sin_of))

    def shift(a, by):
        return pltpu.roll(a, by % width, 1)

    def forward(here, floor, cx, cy, h_up, h_down, x_up, x_down):
        up, down = upper(here, 0), lower(here, 0)
        rate = cy * (up - down) * 0.5 - (up - 2.0 * here + down) * 0.5
        up = jnp.where(within == quarter - 1, here, shift(here, -1))
        down = jnp.where(within == 0, here, shift(here, 1))
        slope = 0.5 * (up - down)
        size = smooth_abs(slope)
        s_slope = slope / size
        rate = rate + ACCELERATION * size - ACCELERATION * 0.5 * (up - 2.0 * here + down)
        slope = 0.5 * (h_up - h_down)
        size = smooth_abs(slope)
        h_slope = slope / size
        rate = rate + TURN_RATE * size - TURN_RATE * 0.5 * (h_up - 2.0 * here + h_down)
        rate = rate + cx * (x_up - x_down) * 0.5 - (x_up - 2.0 * here + x_down) * 0.5
        excess = SHARPNESS * (here - TIME_STEP * rate - floor)
        small = jnp.exp(-jnp.abs(excess))
        share = jnp.where(excess >= 0.0, 1.0, small) / (1.0 + small)
        pull = (0.5 * TURN_RATE) * share * h_slope
        keep = (0.5 * TURN_RATE) * share
        return excess, small, share, s_slope, pull - keep, -pull - keep

    def all_halos(sending):
        def wait(n):
            view = halo.at[0:n]
            c = copy(view, view, halo_send, halo_recv, me, h_next)
            c.wait_send() if sending else c.wait_recv()

        @pl.when(has_prev & has_next)
        def _():
            wait(16)

        @pl.when(jnp.logical_not(has_prev & has_next))
        def _():
            wait(11)

    def unpack(a):
        return {(h, x): a[:, n * speeds : (n + 1) * speeds] for n, (h, x) in enumerate(grid)}

    all_halos(False)
    def tall_pair(top, bottom):
        return jnp.concatenate([top, bottom], 0)

    own = whole
    floor = jnp.concatenate([plane[1, h, x] for h, x in grid], 1)
    hp, hn, xp, xn = (tall_pair(halo[i], halo[i + 1]) for i in (0, 3, 6, 11))
    hp_floor, hn_floor, xp_floor, xn_floor = (halo[i] for i in (2, 5, 8, 13))
    on_even, on_odd = [], []
    for i in (9, 10, 14, 15):
        tile = halo[i]
        other = shift(tile, quarter)
        on_even.append(tall_pair(tile, other))
        on_odd.append(tall_pair(other, tile))
    edge_h = shift(jnp.where(left_half, hn, hp), half)
    edge_x = jnp.where(even, shift(xp, -quarter), shift(xn, quarter))
    up_x = jnp.where(even, shift(own, -quarter), jnp.where(has_next, edge_x, own))
    down_x = jnp.where(even, jnp.where(has_prev, edge_x, own), shift(own, quarter))
    excess, small, share, s_slope, ahead, back = forward(
        own, floor, cx_own, cy_own,
        shift(jnp.where(left_half, hn, own), half), shift(jnp.where(left_half, own, hp), half),
        up_x, down_x,
    )
    next_v = unpack(floor + (jnp.maximum(excess, 0.0) + jnp.log1p(small)) / SHARPNESS)
    for h, x in grid:
        next_o[h, x] = next_v[h, x]
    rest = unpack(jnp.where(excess >= 0.0, small, 1.0) / (1.0 + small))
    share, s_slope, ahead, back = (unpack(a) for a in (share, s_slope, ahead, back))

    up_x = jnp.where(even, shift(edge_h, -quarter), jnp.where(left_half, on_odd[2], on_odd[3]))
    down_x = jnp.where(even, jnp.where(left_half, on_even[0], on_even[1]), shift(edge_h, quarter))
    edge_floor = tall_pair(
        jnp.where(left_half, hp_floor, shift(hn_floor, half)),
        jnp.where(left_half, shift(hp_floor, half), hn_floor),
    )
    out = forward(
        edge_h, edge_floor, cx_out, cy_out,
        jnp.where(left_half, own, hn), jnp.where(left_half, hp, own),
        jnp.where(even | has_next, up_x, edge_h), jnp.where(even & jnp.logical_not(has_prev), edge_h, down_x),
    )
    out = unpack(jnp.where(left_half, out[4], out[5]))
    for x in range(cells):
        ahead[-1, x], back[heads, x] = out[0, x], out[1, x]

    turned = shift(edge_x, half)
    up_h = jnp.where(left_half, turned, jnp.where(even, on_even[1], on_odd[3]))
    down_h = jnp.where(left_half, jnp.where(even, on_even[0], on_odd[2]), turned)
    edge_floor = tall_pair(
        jnp.where(even, xp_floor, shift(xn_floor, quarter)),
        jnp.where(even, shift(xp_floor, -quarter), xn_floor),
    )
    out = forward(
        edge_x, edge_floor, cx_own, cy_own,
        up_h, down_h, jnp.where(even, own, xn), jnp.where(even, xp, own),
    )
    out = unpack(out[2])
    for h in range(heads):
        share[h, -1], share[h, cells] = out[h, 0], out[h, 1]
    speed = SLOWEST + SPEED_RANGE * lax.broadcasted_iota(jnp.int32, (1, speeds), 1).astype(
        jnp.float32
    ) / (speeds - 1)
    cx = [cos_of[h + 1] * speed for h in range(heads)]
    cy = [sin_of[h + 1] * speed for h in range(heads)]

    span = cells * lines
    inside = lax.broadcasted_iota(jnp.int32, (heads * span, slots), 0)
    edge = lax.broadcasted_iota(jnp.int32, (heads * lines, slots), 0)
    edge = lax.div(edge, lines) * span + lax.rem(edge, lines)
    side_rows = lax.broadcasted_iota(jnp.int32, (span, slots), 0)
    ids = [
        i.astype(jnp.float32).astype(jnp.bfloat16)
        for i in (edge + (cells - 1) * lines, inside, edge, side_rows + (heads - 1) * span, side_rows)
    ]
    speed_id = lax.broadcasted_iota(jnp.int32, (speeds, slots), 0).astype(jnp.float32)
    speed_id = speed_id.astype(jnp.bfloat16)

    def tall(row, n):
        part = jnp.broadcast_to(row, (16, slots)).astype(jnp.bfloat16)
        return jnp.concatenate([part] * (n // 16), 0)

    def deposit(one, row_id):
        n = row_id.shape[0]
        weight0, weight1, up_s, code = one[0:1], one[1:2], one[2:3], one[3:4]
        row = jnp.floor(code * (1.0 / speeds))
        cell = code - row * speeds
        here, above_it = row_id == tall(row, n), row_id == tall(row + 1.0, n)
        zero = jnp.zeros(row_id.shape, jnp.bfloat16)
        high, low = [], []
        for f in (1.0 - up_s, up_s):
            a, b = weight0 * f, weight1 * f
            for part in (high, low):
                part.append(jnp.where(here, tall(a, n), jnp.where(above_it, tall(b, n), zero)))
                a, b = (t - t.astype(jnp.bfloat16).astype(jnp.float32) for t in (a, b))
        left = jnp.concatenate([jnp.concatenate(part, 1) for part in (high, low)], 0)
        one_hot = jnp.ones(speed_id.shape, jnp.bfloat16)
        right = jnp.concatenate(
            [
                jnp.where(speed_id == tall(c, speeds), one_hot, jnp.zeros_like(one_hot))
                for c in (cell, cell + 1.0)
            ],
            1,
        )
        both = lax.dot_general(
            left, right, (((1,), (1,)), ((), ())), preferred_element_type=jnp.float32
        )
        return both[:n] + both[n:]

    def collect(n, sums):
        sources = [lax.rem(me + 1 + 2 * n + t, groups) for t in range(2)]
        for g in sources:
            view = got.at[pl.ds(g * 5, 5)]
            copy(view, view, pay_send, pay_recv.at[g], me, h_next).wait_recv()
        sums = list(sums)
        for g in sources:
            for i in range(5):
                sums[i] = sums[i] + deposit(got[g * 5 + i], ids[i])
        return tuple(sums)

    sums = tuple(jnp.zeros((i.shape[0], speeds), jnp.float32) for i in ids)
    sums = lax.fori_loop(0, groups // 2, collect, sums)

    adj, c = {}, {}
    for n, (h, x) in enumerate(grid):
        adj[h, x] = sums[1][n * lines : (n + 1) * lines]
        c[h, x] = adj[h, x] * share[h, x]
    for h in range(heads):
        c[h, -1] = sums[0][h * lines : (h + 1) * lines] * share[h, -1]
        c[h, cells] = sums[2][h * lines : (h + 1) * lines] * share[h, cells]
    for x in range(cells):
        adj[-1, x] = sums[3][x * lines : (x + 1) * lines]
        adj[heads, x] = sums[4][x * lines : (x + 1) * lines]

    for h, x in grid:
        agrad_o[h, x] = adj[h, x] * rest[h, x]
        here = c[h, x]
        grad = spread((0.5 * cy[h] - 0.5) * here, (-0.5 * cy[h] - 0.5) * here, 0)
        pull = (0.5 * ACCELERATION) * here * s_slope[h, x]
        keep = (0.5 * ACCELERATION) * here
        grad = grad + spread(pull - keep, -pull - keep, 1)
        grad = grad + (2.0 + TURN_RATE + ACCELERATION) * here
        grad = grad + adj[h - 1, x] * ahead[h - 1, x] + adj[h + 1, x] * back[h + 1, x]
        low, high = 0.5 * cx[h] - 0.5, -0.5 * cx[h] - 0.5
        if x > 0:
            grad = grad + low * c[h, x - 1]
        else:
            grad = grad + jnp.where(has_prev, low * c[h, -1], high * here)
        if x < cells - 1:
            grad = grad + high * c[h, x + 1]
        else:
            grad = grad + jnp.where(has_next, high * c[h, cells], low * here)
        vgrad_o[h, x] = here - TIME_STEP * grad

    all_halos(True)
    view = got.at[0 : 5 * groups - 3]
    copy(view, view, pay_send, pay_recv.at[0], me, h_next).wait_send()


def write_out(next_v, vgrad_v, agrad_v, next_o, vgrad_o, agrad_o, sem):
    copies = [
        pltpu.make_async_copy(a, b, sem.at[i])
        for i, (a, b) in enumerate(((next_v, next_o), (vgrad_v, vgrad_o), (agrad_v, agrad_o)))
    ]
    for copy in copies:
        copy.start()
    for copy in copies:
        copy.wait()


def on_device(groups, blocks, value, avoid, weight, offy, offs, xy, hs, count):
    slots = weight.shape[3]
    value = jnp.transpose(value, (0, 2, 3, 1))
    avoid = jnp.transpose(avoid, (0, 2, 3, 1))
    weight, offy, offs, xy, hs = (a.reshape(groups, slots) for a in (weight, offy, offs, xy, hs))
    count = count.reshape(1, groups)
    heads, cells, lines, speeds = value.shape
    f32 = jnp.float32
    dma = pltpu.SemaphoreType.DMA
    field = pltpu.VMEM(value.shape, f32)
    x_pair = pltpu.VMEM((2, heads, lines, speeds), f32)
    h_pair = pltpu.VMEM((2, cells, lines, speeds), f32)
    near = groups in (4, 8) and blocks == 4 and heads == cells == 2 and 4 * speeds == slots == 128 and lines == 16
    sample = pltpu.VMEM((groups, slots), f32)
    index = pltpu.VMEM((groups, slots), jnp.int32)
    counts = pltpu.VMEM((1, groups), jnp.int32)
    if near:
        scratch = [
            pltpu.VMEM((2, *value.shape), f32),
            pltpu.VMEM((5, groups, slots), f32), pltpu.VMEM((2, groups, slots), jnp.int32), counts,
            pltpu.VMEM((groups + 2, 4, slots), f32), pltpu.VMEM((5 * groups, 4, slots), f32),
            pltpu.VMEM((4, 3, lines // 2, slots), f32), pltpu.VMEM((2, 2, lines // 2, slots), f32),
            pltpu.VMEM((16, lines // 2, slots), f32),
            dma((3,)), dma, dma((groups,)), dma, dma,
            *[pltpu.SemaphoreType.REGULAR] * 3,
        ]
    else:
        scratch = [
            field, field, sample, sample, sample, index, index, counts,
            pltpu.VMEM((groups, ROWS, slots), f32), pltpu.VMEM((groups, ROWS, slots), f32),
            x_pair, h_pair, field, h_pair, x_pair, h_pair,
            dma((8,)), dma((groups,)), dma((groups,)), *[dma((2,))] * 8, dma,
        ]
    outs = pl.pallas_call(
        functools.partial(near_kernel if near else kernel, groups, blocks),
        out_shape=[pltpu.VMEM(value.shape, f32)] * 3,
        in_specs=[pl.BlockSpec(memory_space=pltpu.HBM)] * 8,
        out_specs=[pl.BlockSpec(memory_space=pltpu.VMEM)] * 3,
        scratch_shapes=scratch,
        compiler_params=pltpu.CompilerParams(collective_id=0, has_side_effects=True),
        name="step",
    )(value, avoid, weight, offy, offs, xy, hs, count)
    outs = pl.pallas_call(
        write_out,
        out_shape=[jax.ShapeDtypeStruct(value.shape, f32)] * 3,
        in_specs=[pl.BlockSpec(memory_space=pl.ANY)] * 3,
        out_specs=[pl.BlockSpec(memory_space=pl.ANY)] * 3,
        scratch_shapes=[dma((3,))],
        compiler_params=pltpu.CompilerParams(vmem_limit_bytes=1 << 20),
        name="write_out",
    )(*outs)
    return tuple(jnp.transpose(o, (0, 3, 1, 2)) for o in outs)


def solution(mesh):
    field = P("ha", None, "gx", None)
    sample = P("gx", "ha", None, None)
    return jax.shard_map(
        functools.partial(on_device, mesh.shape["gx"], mesh.shape["ha"]),
        mesh=mesh,
        in_specs=(field, field, sample, sample, sample, sample, sample, P("gx", "ha", None)),
        out_specs=(field, field, field),
        check_vma=False,
    )
```

```python
import functools
import math

import jax
import jax.numpy as jnp
import numpy as np
from jax import lax
from jax.experimental import pallas as pl
from jax.experimental.pallas import tpu as pltpu
from jax.sharding import PartitionSpec as P

TIME_STEP = 0.3
SHARPNESS = 2.0
SOFTENING = 0.1
TURN_RATE = 0.5
ACCELERATION = 0.3
SLOWEST = 0.2
SPEED_RANGE = 0.8
ROWS = 8
MESH = pl.DeviceIdType.MESH


def smooth_abs(slope):
    return jnp.sqrt(slope * slope + SOFTENING * SOFTENING)


def upper(plane, axis):
    n = plane.shape[axis]
    return jnp.concatenate(
        [lax.slice_in_dim(plane, 1, n, axis=axis), lax.slice_in_dim(plane, n - 1, n, axis=axis)], axis
    )


def lower(plane, axis):
    n = plane.shape[axis]
    return jnp.concatenate(
        [lax.slice_in_dim(plane, 0, 1, axis=axis), lax.slice_in_dim(plane, 0, n - 1, axis=axis)], axis
    )


def spread(up, down, axis):
    n = up.shape[axis]
    from_lower = jnp.concatenate(
        [lax.slice_in_dim(down, 0, 1, axis=axis), lax.slice_in_dim(up, 0, n - 1, axis=axis)], axis
    )
    from_upper = jnp.concatenate(
        [lax.slice_in_dim(down, 1, n, axis=axis), lax.slice_in_dim(up, n - 1, n, axis=axis)], axis
    )
    return from_lower + from_upper


def pick(table, index):
    chosen = jnp.float32(table[0])
    for i in range(1, len(table)):
        chosen = jnp.where(index == i, jnp.float32(table[i]), chosen)
    return chosen


def kernel(
    groups, blocks,
    value_h, avoid_h, weight_h, offy_h, offs_h, xy_h, hs_h, count_h,
    next_o, vgrad_o, agrad_o,
    value, avoid, weight, offy, offs, xy, hs, count,
    pay, got, xhalo, hhalo, carried, turned, cxhalo, chhalo,
    in_sem, pay_send, pay_recv, x_send, x_recv, h_send, h_recv,
    cx_send, cx_recv, ch_send, ch_recv, self_sem,
):
    heads, cells, lines, speeds = value.shape
    slots = weight.shape[1]
    me = lax.axis_index("gx")
    hb = lax.axis_index("ha")
    h_next = lax.rem(hb + 1, blocks)
    h_prev = lax.rem(hb + blocks - 1, blocks)
    has_prev = me > 0
    has_next = me < groups - 1

    barrier = pltpu.get_barrier_semaphore()

    def greet(d):
        pl.semaphore_signal(
            barrier, inc=1, device_id=(lax.rem(me + d, groups), hb), device_id_type=MESH
        )

    if groups <= 8:
        for d in range(1, groups):
            greet(d)
    else:
        pl.loop(1, groups)(greet)
    for other in (h_prev, h_next):
        pl.semaphore_signal(barrier, inc=1, device_id=(me, other), device_id_type=MESH)

    pairs = (
        (weight_h, weight), (offy_h, offy), (offs_h, offs), (xy_h, xy), (hs_h, hs), (count_h, count),
        (value_h, value), (avoid_h, avoid),
    )
    loads = [pltpu.make_async_copy(a, b, in_sem.at[i]) for i, (a, b) in enumerate(pairs)]
    for load in loads:
        load.start()
    for load in loads[:6]:
        load.wait()

    owners = lax.broadcasted_iota(jnp.int32, (groups, groups), 0)
    lanes = lax.broadcasted_iota(jnp.int32, (groups, groups), 1)
    live = jnp.sum(
        jnp.where(owners == lanes, jnp.broadcast_to(count[...], (groups, groups)), 0).astype(jnp.float32),
        axis=1, keepdims=True,
    )
    slot = lax.broadcasted_iota(jnp.int32, (groups, slots), 1).astype(jnp.float32)
    w = jnp.where(slot < live, weight[...], 0.0)
    oy = offy[...]
    os = offs[...]
    state = hs[...]
    head = lax.div(state, speeds)
    pay[:, 0, :] = w * (1.0 - oy)
    pay[:, 1, :] = w * oy
    pay[:, 2, :] = 1.0 - os
    pay[:, 3, :] = os
    pay[:, 4, :] = (head * (cells * lines) + xy[...]).astype(jnp.float32)
    pay[:, 5, :] = (state - head * speeds).astype(jnp.float32)
    pay[:, 6, :] = jnp.zeros((groups, slots), jnp.float32)
    pay[:, 7, :] = jnp.zeros((groups, slots), jnp.float32)

    loads[6].wait()
    pl.semaphore_wait(barrier, groups - 1 + 2)

    def h_copy(side):
        return pltpu.make_async_remote_copy(
            value.at[0 if side == 0 else heads - 1], hhalo.at[1 - side],
            h_send.at[side], h_recv.at[1 - side],
            device_id=(me, h_prev if side == 0 else h_next), device_id_type=MESH,
        )

    def x_copy(side):
        return pltpu.make_async_remote_copy(
            value.at[:, 0 if side == 0 else cells - 1], xhalo.at[1 - side],
            x_send.at[side], x_recv.at[1 - side],
            device_id=(me - 1 if side == 0 else me + 1, hb), device_id_type=MESH,
        )

    def pay_copy(d):
        peer = lax.rem(me + d, groups)
        return pltpu.make_async_remote_copy(
            pay.at[peer], got.at[d], pay_send.at[d], pay_recv.at[d],
            device_id=(peer, hb), device_id_type=MESH,
        )

    for side in range(2):
        h_copy(side).start()
    for side, has in ((0, has_prev), (1, has_next)):
        @pl.when(has)
        def _():
            x_copy(side).start()

    if groups <= 8:
        for d in range(groups - 1, 0, -1):
            pay_copy(d).start()
    else:
        pl.loop(1, groups)(lambda d: pay_copy(d).start())
    mine = pltpu.make_async_copy(pay.at[me], got.at[0], self_sem)
    mine.start()
    loads[7].wait()

    for side, has in ((0, has_prev), (1, has_next)):
        @pl.when(jnp.logical_not(has))
        def _():
            xhalo[side] = value[:, 0 if side == 0 else cells - 1]

    total = heads * blocks
    angles = [np.float32(2.0 * math.pi / total) * np.float32(k) for k in range(total)]
    cosines = [float(np.cos(a)) for a in angles]
    sines = [float(np.sin(a)) for a in angles]
    speed = SLOWEST + SPEED_RANGE * lax.broadcasted_iota(jnp.int32, (1, speeds), 1).astype(
        jnp.float32
    ) / (speeds - 1)
    cx = [pick(cosines, hb * heads + h) * speed for h in range(heads)]
    cy = [pick(sines, hb * heads + h) * speed for h in range(heads)]
    grid = [(h, x) for h in range(heads) for x in range(cells)]
    v = {(h, x): value[h, x] for h, x in grid}
    part, s_slope = {}, {}
    for h, x in grid:
        here = v[h, x]
        up, down = upper(here, 0), lower(here, 0)
        term = cy[h] * (up - down) * 0.5 - (up - 2.0 * here + down) * 0.5
        up, down = upper(here, 1), lower(here, 1)
        slope = 0.5 * (up - down)
        size = smooth_abs(slope)
        s_slope[h, x] = slope / size
        part[h, x] = term + ACCELERATION * size - ACCELERATION * 0.5 * (up - 2.0 * here + down)

    for side in range(2):
        h_copy(side).wait_recv()
    for side, has in ((0, has_prev), (1, has_next)):
        @pl.when(has)
        def _():
            x_copy(1 - side).wait_recv()
    for x in range(cells):
        v[-1, x] = hhalo[0, x]
        v[heads, x] = hhalo[1, x]
    for h in range(heads):
        v[h, -1] = xhalo[0, h]
        v[h, cells] = xhalo[1, h]

    share, h_slope, above = {}, {}, {}
    for h, x in grid:
        here = v[h, x]
        up, down = v[h + 1, x], v[h - 1, x]
        slope = 0.5 * (up - down)
        size = smooth_abs(slope)
        h_slope[h, x] = slope / size
        turning = TURN_RATE * size - TURN_RATE * 0.5 * (up - 2.0 * here + down)
        up, down = v[h, x + 1], v[h, x - 1]
        across = cx[h] * (up - down) * 0.5 - (up - 2.0 * here + down) * 0.5
        relaxed = here - TIME_STEP * (across + part[h, x] + turning)
        floor = avoid[h, x]
        excess = SHARPNESS * (relaxed - floor)
        small = jnp.exp(-jnp.abs(excess))
        share[h, x] = jnp.where(excess >= 0.0, 1.0, small) / (1.0 + small)
        above[h, x] = (excess, small)

    rows = heads * cells * lines
    row_id = lax.broadcasted_iota(jnp.int32, (rows, slots), 0).astype(jnp.float32)
    speed_id = lax.broadcasted_iota(jnp.int32, (speeds, slots), 0).astype(jnp.float32)

    def operands(d):
        one = got[d]
        cell = jnp.broadcast_to(one[4:5], (rows, slots))
        left = jnp.where(row_id == cell, one[0:1], jnp.where(row_id == cell + 1.0, one[1:2], 0.0))
        cell = jnp.broadcast_to(one[5:6], (speeds, slots))
        right = jnp.where(
            speed_id == cell, one[2:3], jnp.where(speed_id == cell + 1.0, one[3:4], 0.0)
        )
        return left, right

    def product(left, right):
        return lax.dot_general(
            left, right, (((1,), (1,)), ((), ())),
            precision=lax.Precision.HIGHEST, preferred_element_type=jnp.float32,
        )

    mine.wait()
    if groups <= 8:
        for d in range(1, groups):
            pay_copy(d).wait_recv()
        both = [operands(d) for d in range(groups)]
        deposit = product(
            jnp.concatenate([b[0] for b in both], 1), jnp.concatenate([b[1] for b in both], 1)
        )
    else:
        pl.loop(1, groups)(lambda d: pay_copy(d).wait_recv())
        deposit = lax.fori_loop(
            0, groups, lambda d, so_far: so_far + product(*operands(d)),
            jnp.zeros((rows, speeds), jnp.float32),
        )

    c, adj = {}, {}
    for n, (h, x) in enumerate(grid):
        adjoint = deposit[n * lines : (n + 1) * lines]
        c[h, x] = adjoint * share[h, x]
        carried[h, x] = c[h, x]
        adj[h, x] = adjoint
    def cx_copy(side):
        return pltpu.make_async_remote_copy(
            carried.at[:, 0 if side == 0 else cells - 1], cxhalo.at[1 - side],
            cx_send.at[side], cx_recv.at[1 - side],
            device_id=(me - 1 if side == 0 else me + 1, hb), device_id_type=MESH,
        )

    for side, has in ((0, has_prev), (1, has_next)):
        @pl.when(has)
        def _():
            cx_copy(side).start()

        @pl.when(jnp.logical_not(has))
        def _():
            cxhalo[side] = jnp.zeros_like(cxhalo[side])
    ahead, back = {}, {}
    for h, x in grid:
        pull = (0.5 * TURN_RATE) * c[h, x] * h_slope[h, x]
        keep = (0.5 * TURN_RATE) * c[h, x]
        ahead[h, x] = pull - keep
        back[h, x] = -pull - keep
    for x in range(cells):
        turned[0, x] = back[0, x]
        turned[1, x] = ahead[heads - 1, x]

    def ch_copy(side):
        return pltpu.make_async_remote_copy(
            turned.at[side], chhalo.at[1 - side], ch_send.at[side], ch_recv.at[1 - side],
            device_id=(me, h_prev if side == 0 else h_next), device_id_type=MESH,
        )

    for side in range(2):
        ch_copy(side).start()

    local = {}
    for h, x in grid:
        excess, small = above[h, x]
        next_o[h, x] = avoid[h, x] + (jnp.maximum(excess, 0.0) + jnp.log1p(small)) / SHARPNESS
        agrad_o[h, x] = adj[h, x] * (jnp.where(excess >= 0.0, small, 1.0) / (1.0 + small))
        here = c[h, x]
        grad = spread((0.5 * cy[h] - 0.5) * here, (-0.5 * cy[h] - 0.5) * here, 0)
        pull = (0.5 * ACCELERATION) * here * s_slope[h, x]
        keep = (0.5 * ACCELERATION) * here
        grad = grad + spread(pull - keep, -pull - keep, 1)
        local[h, x] = grad + (2.0 + TURN_RATE + ACCELERATION) * here

    for side in range(2):
        ch_copy(side).wait_recv()
    for side, has in ((0, has_prev), (1, has_next)):
        @pl.when(has)
        def _():
            cx_copy(1 - side).wait_recv()
    for h, x in grid:
        grad = local[h, x]
        grad = grad + (ahead[h - 1, x] if h > 0 else chhalo[0, x])
        grad = grad + (back[h + 1, x] if h < heads - 1 else chhalo[1, x])
        low, high = 0.5 * cx[h] - 0.5, -0.5 * cx[h] - 0.5
        if x > 0:
            grad = grad + low * c[h, x - 1]
        else:
            grad = grad + jnp.where(has_prev, low * cxhalo[0, h], high * c[h, x])
        if x < cells - 1:
            grad = grad + high * c[h, x + 1]
        else:
            grad = grad + jnp.where(has_next, high * cxhalo[1, h], low * c[h, x])
        vgrad_o[h, x] = c[h, x] - TIME_STEP * grad

    for side in range(2):
        h_copy(side).wait_send()
        ch_copy(side).wait_send()
    for side, has in ((0, has_prev), (1, has_next)):
        @pl.when(has)
        def _():
            x_copy(side).wait_send()
            cx_copy(side).wait_send()
    if groups <= 8:
        for d in range(1, groups):
            pay_copy(d).wait_send()
    else:
        pl.loop(1, groups)(lambda d: pay_copy(d).wait_send())


def near_kernel(
    groups, blocks,
    value_h, avoid_h, weight_h, offy_h, offs_h, xy_h, hs_h, count_h,
    next_o, vgrad_o, agrad_o,
    fields, sample, cell, count, pay, got, packed, corner, halo,
    in_sem, pay_send, pay_recv, halo_send, halo_recv, row_in, late, late_near,
):
    _, heads, cells, lines, speeds = fields.shape
    value, avoid = fields.at[0], fields.at[1]
    slots = sample.shape[2]
    me = lax.axis_index("gx")
    hb = lax.axis_index("ha")
    h_next = lax.rem(hb + 1, blocks)
    h_prev = lax.rem(hb + blocks - 1, blocks)
    h_side = (h_prev, h_next)
    has_prev = me > 0
    has_next = me < groups - 1
    base = 2
    in_base = me < base

    is_even = lax.rem(hb, 2) == 0
    upper_pair = hb >= blocks // 2
    mate_side = 1 - lax.rem(hb, 2)
    far_side = 1 - mate_side
    mate, far = (lax.rem(hb + blocks - 1 + 2 * s, blocks) for s in (mate_side, far_side))
    level = lax.div(me + 1, 2)
    mate_before = jnp.where(is_even, jnp.minimum(2 * level + 1, groups), jnp.maximum(2 * level - 1, base))
    far_before = jnp.where(
        upper_pair,
        jnp.minimum(2 * level + jnp.where(is_even, 3, 1), groups),
        jnp.maximum(2 * level - jnp.where(is_even, 1, 3), base),
    )
    earlier = me + mate_before + far_before

    def near_rows(before):
        return jnp.clip(me - 1, base, before), jnp.clip(me + 2, base, before)

    mate_near, far_near = near_rows(mate_before), near_rows(far_before)
    around = jnp.minimum(me + 2, groups) - jnp.maximum(me - 1, base)
    near_later = jnp.where(has_next, 1, 0) + 2 * around
    for low, high in (mate_near, far_near):
        near_later = near_later - (high - low)

    barrier = pltpu.get_barrier_semaphore()

    def signal(sem, j, h):
        pl.semaphore_signal(sem, inc=1, device_id=(j, h), device_id_type=MESH)

    def rows(lo, hi, body):
        lax.fori_loop(lo, hi, lambda j, carry: (body(j), carry)[1], 0)

    def signal_at(sem, h):
        return lambda j: signal(sem, j, h)

    def wait_some(sem, n):
        @pl.when(n > 0)
        def _():
            pl.semaphore_wait(sem, n)

    @pl.when(in_base)
    def _():
        for j in range(groups - 1, base - 1, -1):
            for h in (far, mate, hb):
                signal(barrier, j, h)

    @pl.when(jnp.logical_not(in_base))
    def _():
        for before, h in ((far_before, far), (mate_before, mate), (me + 1, hb)):
            rows(before, groups, lambda j: signal(barrier, groups - 1 + before - j, h))
        for j in range(base):
            for h in (far, mate, hb):
                signal(barrier, j, h)

    loads = [
        pltpu.make_async_copy(a, b, in_sem.at[i])
        for a, b, i in (
            (weight_h, sample.at[0], 0), (offy_h, sample.at[1], 0), (offs_h, sample.at[2], 0),
            (xy_h, cell.at[0], 0), (hs_h, cell.at[1], 0), (count_h, count, 1),
            (value_h, value, 2), (avoid_h, avoid, 2),
        )
    ]
    for load in loads:
        load.start()
    loaded = [pltpu.make_async_copy(r, r, in_sem.at[i]) for r, i in ((sample, 0), (count, 1), (fields, 2))]

    pay[0] = jnp.zeros(pay.shape[1:], jnp.float32)
    pay[groups + 1] = jnp.zeros(pay.shape[1:], jnp.float32)

    def copy(src, dst, send_sem, recv_sem, j, h):
        return pltpu.make_async_remote_copy(
            src, dst, send_sem, recv_sem, device_id=(j, h), device_id_type=MESH
        )

    def x_slot(side):
        return 6 + side * 5

    def h_halo(side, h):
        dst = halo.at[pl.ds(3 * (1 - side), 3)]
        copy(packed.at[side], dst, halo_send, halo_recv, me, h).start()

    def x_halo(side):
        at = x_slot(1 - side)
        copy(packed.at[2 + side], halo.at[at : at + 3], halo_send, halo_recv, me - 1 + 2 * side, hb).start()

    def corner_halo(side, h_to, h):
        at = x_slot(1 - side) + 4 - h_to
        copy(corner.at[side, h_to], halo.at[at], halo_send, halo_recv, me - 1 + 2 * side, h).start()

    def send_side(j, side, h):
        copy(pay.at[j + 1], got.at[me * 5 + 4 - side], pay_send, pay_recv.at[me], j, h).start()

    def send_own(j):
        copy(pay.at[pl.ds(j, 3)], got.at[pl.ds(me * 5, 3)], pay_send, pay_recv.at[me], j, hb).start()

    def send_mate(j):
        send_side(j, mate_side, mate)

    def send_far(j):
        send_side(j, far_side, far)

    def send_all(j):
        send_own(j)
        send_mate(j)
        send_far(j)

    loaded[0].wait()
    loaded[1].wait()
    owners = lax.broadcasted_iota(jnp.int32, (groups, groups), 0)
    lanes = lax.broadcasted_iota(jnp.int32, (groups, groups), 1)
    live = jnp.sum(
        jnp.where(owners == lanes, jnp.broadcast_to(count[...], (groups, groups)), 0).astype(jnp.float32),
        axis=1, keepdims=True,
    )
    slot = lax.broadcasted_iota(jnp.int32, (groups, slots), 1).astype(jnp.float32)
    w = jnp.where(slot < live, sample[0], 0.0)
    oy = sample[1]
    state = cell[1]
    head = lax.div(state, speeds)
    row = head * (cells * lines) + cell[0]
    pay[1 : groups + 1, 0, :] = w * (1.0 - oy)
    pay[1 : groups + 1, 1, :] = w * oy
    pay[1 : groups + 1, 2, :] = sample[2]
    pay[1 : groups + 1, 3, :] = (row * speeds + (state - head * speeds)).astype(jnp.float32)
    pltpu.make_async_copy(pay.at[pl.ds(me, 3)], got.at[pl.ds(me * 5, 3)], pay_recv.at[me]).start()
    loaded[2].wait()
    grid = [(h, x) for h in range(heads) for x in range(cells)]
    plane = {(i, h, x): fields[i, h, x] for i in range(2) for h, x in grid}
    whole = jnp.concatenate([plane[0, h, x] for h, x in grid], 1)
    mid = lines // 2
    for side, edge in ((0, 0), (1, 1)):
        h_edge, x_edge = edge * (heads - 1), edge * (cells - 1)
        over_h = [plane[1, h_edge, x] for x in range(cells)]
        over_x = [plane[1, h, x_edge] for h in range(heads)]
        h_tile = [p[:mid] for p in over_h] + [p[mid:] for p in over_h]
        x_tile = [q for p in over_x for q in (p[:mid], p[mid:])]
        for to, tile in ((side, h_tile), (2 + side, x_tile)):
            packed[to, 0] = whole[:mid]
            packed[to, 1] = whole[mid:]
            packed[to, 2] = jnp.concatenate(tile, 1)
        for h in range(2):
            p = plane[0, h * (heads - 1), x_edge]
            corner[side, h] = jnp.concatenate([p[:mid], p[mid:]] * 2, 1)

    @pl.when(jnp.logical_not(in_base))
    def _():
        pl.semaphore_wait(barrier, earlier)
        @pl.when(me == base)
        def _():
            for j in range(base):
                signal(row_in, j, hb)

        rows(base, me - 1, signal_at(late, hb))
        for (low, high), before, h in ((mate_near, mate_before, mate), (far_near, far_before, far)):
            rows(base, low, signal_at(late, h))
            rows(high, before, signal_at(late, h))
        for j in range(base):
            send_all(j)
        rows(jnp.maximum(me - 1, base), me, signal_at(late_near, hb))
        rows(*mate_near, signal_at(late_near, mate))
        rows(*far_near, signal_at(late_near, far))

        x_halo(0)
        others = ((mate_before, mate_side, mate), (far_before, far_side, far))

        def near_halos(comes):
            for before, side, h in others:
                pl.when(comes(me - 1, before))(functools.partial(corner_halo, 0, side, h))
                pl.when(comes(me, before))(functools.partial(h_halo, side, h))
                pl.when(comes(me + 1, before) & has_next)(functools.partial(corner_halo, 1, side, h))

        near_halos(lambda j, before: j < before)
        rows(base, me, send_own)
        rows(base, mate_before, send_mate)
        rows(base, far_before, send_far)

        wait_some(late_near, near_later)
        pl.when(has_next)(functools.partial(x_halo, 1))
        near_halos(lambda j, before: j >= before)
        wait_some(late, 3 * groups - 1 - earlier - near_later)
        rows(me + 1, groups, send_own)
        rows(mate_before, groups, send_mate)
        rows(far_before, groups, send_far)

    def x_and_corners(side):
        x_halo(side)
        for h in range(2):
            corner_halo(side, h, h_side[h])

    @pl.when(in_base)
    def _():
        pl.semaphore_wait(row_in, 1)
        for side in range(2):
            h_halo(side, h_side[side])
            send_side(me, side, h_side[side])
        for row in range(base):
            @pl.when(me == row)
            def _():
                x_and_corners(1 - row)
                send_all(1 - row)
        pl.semaphore_wait(barrier, 3 * (groups - base))
        pl.when(me == base - 1)(functools.partial(x_and_corners, 1))
        rows(base, groups, send_own)
        rows(base, groups, send_mate)
        rows(base, groups, send_far)

    width = heads * cells * speeds
    half, quarter = width // 2, width // 4
    lane = lax.broadcasted_iota(jnp.int32, (1, width), 1)
    place = lax.div(lane, quarter)
    within = lax.rem(lane, quarter)
    even = lax.rem(place, 2) == 0
    left_half = place < 2
    total = heads * blocks
    angles = [np.float32(2.0 * math.pi / total) * np.float32(k) for k in range(total)]
    cosines = [float(np.cos(a)) for a in angles]
    sines = [float(np.sin(a)) for a in angles]
    speed = SLOWEST + SPEED_RANGE * within.astype(jnp.float32) / (speeds - 1)
    turn = [lax.rem(hb * heads + h + total, total) for h in range(-1, heads + 1)]
    cos_of = [pick(cosines, t) for t in turn]
    sin_of = [pick(sines, t) for t in turn]
    cx_own, cy_own = (jnp.where(left_half, a[1], a[2]) * speed for a in (cos_of, sin_of))
    cx_out, cy_out = (jnp.where(left_half, a[0], a[3]) * speed for a in (cos_of, sin_of))

    def shift(a, by):
        return pltpu.roll(a, by % width, 1)

    def forward(here, floor, cx, cy, h_up, h_down, x_up, x_down):
        up, down = upper(here, 0), lower(here, 0)
        rate = cy * (up - down) * 0.5 - (up - 2.0 * here + down) * 0.5
        up = jnp.where(within == quarter - 1, here, shift(here, -1))
        down = jnp.where(within == 0, here, shift(here, 1))
        slope = 0.5 * (up - down)
        size = smooth_abs(slope)
        s_slope = slope / size
        rate = rate + ACCELERATION * size - ACCELERATION * 0.5 * (up - 2.0 * here + down)
        slope = 0.5 * (h_up - h_down)
        size = smooth_abs(slope)
        h_slope = slope / size
        rate = rate + TURN_RATE * size - TURN_RATE * 0.5 * (h_up - 2.0 * here + h_down)
        rate = rate + cx * (x_up - x_down) * 0.5 - (x_up - 2.0 * here + x_down) * 0.5
        excess = SHARPNESS * (here - TIME_STEP * rate - floor)
        small = jnp.exp(-jnp.abs(excess))
        share = jnp.where(excess >= 0.0, 1.0, small) / (1.0 + small)
        pull = (0.5 * TURN_RATE) * share * h_slope
        keep = (0.5 * TURN_RATE) * share
        return excess, small, share, s_slope, pull - keep, -pull - keep

    def all_halos(sending):
        def wait(n):
            view = halo.at[0:n]
            c = copy(view, view, halo_send, halo_recv, me, h_next)
            c.wait_send() if sending else c.wait_recv()

        @pl.when(has_prev & has_next)
        def _():
            wait(16)

        @pl.when(jnp.logical_not(has_prev & has_next))
        def _():
            wait(11)

    def unpack(a):
        return {(h, x): a[:, n * speeds : (n + 1) * speeds] for n, (h, x) in enumerate(grid)}

    all_halos(False)
    def tall_pair(top, bottom):
        return jnp.concatenate([top, bottom], 0)

    own = whole
    floor = jnp.concatenate([plane[1, h, x] for h, x in grid], 1)
    hp, hn, xp, xn = (tall_pair(halo[i], halo[i + 1]) for i in (0, 3, 6, 11))
    hp_floor, hn_floor, xp_floor, xn_floor = (halo[i] for i in (2, 5, 8, 13))
    on_even, on_odd = [], []
    for i in (9, 10, 14, 15):
        tile = halo[i]
        other = shift(tile, quarter)
        on_even.append(tall_pair(tile, other))
        on_odd.append(tall_pair(other, tile))
    edge_h = shift(jnp.where(left_half, hn, hp), half)
    edge_x = jnp.where(even, shift(xp, -quarter), shift(xn, quarter))
    up_x = jnp.where(even, shift(own, -quarter), jnp.where(has_next, edge_x, own))
    down_x = jnp.where(even, jnp.where(has_prev, edge_x, own), shift(own, quarter))
    excess, small, share, s_slope, ahead, back = forward(
        own, floor, cx_own, cy_own,
        shift(jnp.where(left_half, hn, own), half), shift(jnp.where(left_half, own, hp), half),
        up_x, down_x,
    )
    next_v = unpack(floor + (jnp.maximum(excess, 0.0) + jnp.log1p(small)) / SHARPNESS)
    for h, x in grid:
        next_o[h, x] = next_v[h, x]
    rest = unpack(jnp.where(excess >= 0.0, small, 1.0) / (1.0 + small))
    share, s_slope, ahead, back = (unpack(a) for a in (share, s_slope, ahead, back))

    up_x = jnp.where(even, shift(edge_h, -quarter), jnp.where(left_half, on_odd[2], on_odd[3]))
    down_x = jnp.where(even, jnp.where(left_half, on_even[0], on_even[1]), shift(edge_h, quarter))
    edge_floor = tall_pair(
        jnp.where(left_half, hp_floor, shift(hn_floor, half)),
        jnp.where(left_half, shift(hp_floor, half), hn_floor),
    )
    out = forward(
        edge_h, edge_floor, cx_out, cy_out,
        jnp.where(left_half, own, hn), jnp.where(left_half, hp, own),
        jnp.where(even | has_next, up_x, edge_h), jnp.where(even & jnp.logical_not(has_prev), edge_h, down_x),
    )
    out = unpack(jnp.where(left_half, out[4], out[5]))
    for x in range(cells):
        ahead[-1, x], back[heads, x] = out[0, x], out[1, x]

    turned = shift(edge_x, half)
    up_h = jnp.where(left_half, turned, jnp.where(even, on_even[1], on_odd[3]))
    down_h = jnp.where(left_half, jnp.where(even, on_even[0], on_odd[2]), turned)
    edge_floor = tall_pair(
        jnp.where(even, xp_floor, shift(xn_floor, quarter)),
        jnp.where(even, shift(xp_floor, -quarter), xn_floor),
    )
    out = forward(
        edge_x, edge_floor, cx_own, cy_own,
        up_h, down_h, jnp.where(even, own, xn), jnp.where(even, xp, own),
    )
    out = unpack(out[2])
    for h in range(heads):
        share[h, -1], share[h, cells] = out[h, 0], out[h, 1]
    speed = SLOWEST + SPEED_RANGE * lax.broadcasted_iota(jnp.int32, (1, speeds), 1).astype(
        jnp.float32
    ) / (speeds - 1)
    cx = [cos_of[h + 1] * speed for h in range(heads)]
    cy = [sin_of[h + 1] * speed for h in range(heads)]

    span = cells * lines
    inside = lax.broadcasted_iota(jnp.int32, (heads * span, slots), 0)
    edge = lax.broadcasted_iota(jnp.int32, (heads * lines, slots), 0)
    edge = lax.div(edge, lines) * span + lax.rem(edge, lines)
    side_rows = lax.broadcasted_iota(jnp.int32, (span, slots), 0)
    ids = [
        i.astype(jnp.float32).astype(jnp.bfloat16)
        for i in (edge + (cells - 1) * lines, inside, edge, side_rows + (heads - 1) * span, side_rows)
    ]
    speed_id = lax.broadcasted_iota(jnp.int32, (speeds, slots), 0).astype(jnp.float32)
    speed_id = speed_id.astype(jnp.bfloat16)

    def tall(row, n):
        part = jnp.broadcast_to(row, (16, slots)).astype(jnp.bfloat16)
        return jnp.concatenate([part] * (n // 16), 0)

    def deposit(one, row_id):
        n = row_id.shape[0]
        weight0, weight1, up_s, code = one[0:1], one[1:2], one[2:3], one[3:4]
        row = jnp.floor(code * (1.0 / speeds))
        cell = code - row * speeds
        here, above_it = row_id == tall(row, n), row_id == tall(row + 1.0, n)
        zero = jnp.zeros(row_id.shape, jnp.bfloat16)
        high, low = [], []
        for f in (1.0 - up_s, up_s):
            a, b = weight0 * f, weight1 * f
            for part in (high, low):
                part.append(jnp.where(here, tall(a, n), jnp.where(above_it, tall(b, n), zero)))
                a, b = (t - t.astype(jnp.bfloat16).astype(jnp.float32) for t in (a, b))
        left = jnp.concatenate([jnp.concatenate(part, 1) for part in (high, low)], 0)
        one_hot = jnp.ones(speed_id.shape, jnp.bfloat16)
        right = jnp.concatenate(
            [
                jnp.where(speed_id == tall(c, speeds), one_hot, jnp.zeros_like(one_hot))
                for c in (cell, cell + 1.0)
            ],
            1,
        )
        both = lax.dot_general(
            left, right, (((1,), (1,)), ((), ())), preferred_element_type=jnp.float32
        )
        return both[:n] + both[n:]

    def collect(n, sums):
        sources = [lax.rem(me + 1 + 2 * n + t, groups) for t in range(2)]
        for g in sources:
            view = got.at[pl.ds(g * 5, 5)]
            copy(view, view, pay_send, pay_recv.at[g], me, h_next).wait_recv()
        sums = list(sums)
        for g in sources:
            for i in range(5):
                sums[i] = sums[i] + deposit(got[g * 5 + i], ids[i])
        return tuple(sums)

    sums = tuple(jnp.zeros((i.shape[0], speeds), jnp.float32) for i in ids)
    sums = lax.fori_loop(0, groups // 2, collect, sums)

    adj, c = {}, {}
    for n, (h, x) in enumerate(grid):
        adj[h, x] = sums[1][n * lines : (n + 1) * lines]
        c[h, x] = adj[h, x] * share[h, x]
    for h in range(heads):
        c[h, -1] = sums[0][h * lines : (h + 1) * lines] * share[h, -1]
        c[h, cells] = sums[2][h * lines : (h + 1) * lines] * share[h, cells]
    for x in range(cells):
        adj[-1, x] = sums[3][x * lines : (x + 1) * lines]
        adj[heads, x] = sums[4][x * lines : (x + 1) * lines]

    for h, x in grid:
        agrad_o[h, x] = adj[h, x] * rest[h, x]
        here = c[h, x]
        grad = spread((0.5 * cy[h] - 0.5) * here, (-0.5 * cy[h] - 0.5) * here, 0)
        pull = (0.5 * ACCELERATION) * here * s_slope[h, x]
        keep = (0.5 * ACCELERATION) * here
        grad = grad + spread(pull - keep, -pull - keep, 1)
        grad = grad + (2.0 + TURN_RATE + ACCELERATION) * here
        grad = grad + adj[h - 1, x] * ahead[h - 1, x] + adj[h + 1, x] * back[h + 1, x]
        low, high = 0.5 * cx[h] - 0.5, -0.5 * cx[h] - 0.5
        if x > 0:
            grad = grad + low * c[h, x - 1]
        else:
            grad = grad + jnp.where(has_prev, low * c[h, -1], high * here)
        if x < cells - 1:
            grad = grad + high * c[h, x + 1]
        else:
            grad = grad + jnp.where(has_next, high * c[h, cells], low * here)
        vgrad_o[h, x] = here - TIME_STEP * grad

    all_halos(True)
    view = got.at[0 : 5 * groups - 3]
    copy(view, view, pay_send, pay_recv.at[0], me, h_next).wait_send()


def write_out(next_v, vgrad_v, agrad_v, next_o, vgrad_o, agrad_o, sem):
    copies = [
        pltpu.make_async_copy(a, b, sem.at[i])
        for i, (a, b) in enumerate(((next_v, next_o), (vgrad_v, vgrad_o), (agrad_v, agrad_o)))
    ]
    for copy in copies:
        copy.start()
    for copy in copies:
        copy.wait()


def on_device(groups, blocks, value, avoid, weight, offy, offs, xy, hs, count):
    slots = weight.shape[3]
    value = jnp.transpose(value, (0, 2, 3, 1))
    avoid = jnp.transpose(avoid, (0, 2, 3, 1))
    weight, offy, offs, xy, hs = (a.reshape(groups, slots) for a in (weight, offy, offs, xy, hs))
    count = count.reshape(1, groups)
    heads, cells, lines, speeds = value.shape
    f32 = jnp.float32
    dma = pltpu.SemaphoreType.DMA
    field = pltpu.VMEM(value.shape, f32)
    x_pair = pltpu.VMEM((2, heads, lines, speeds), f32)
    h_pair = pltpu.VMEM((2, cells, lines, speeds), f32)
    near = groups in (4, 8) and blocks == 4 and heads == cells == 2 and 4 * speeds == slots == 128 and lines == 16
    sample = pltpu.VMEM((groups, slots), f32)
    index = pltpu.VMEM((groups, slots), jnp.int32)
    counts = pltpu.VMEM((1, groups), jnp.int32)
    if near:
        scratch = [
            pltpu.VMEM((2, *value.shape), f32),
            pltpu.VMEM((5, groups, slots), f32), pltpu.VMEM((2, groups, slots), jnp.int32), counts,
            pltpu.VMEM((groups + 2, 4, slots), f32), pltpu.VMEM((5 * groups, 4, slots), f32),
            pltpu.VMEM((4, 3, lines // 2, slots), f32), pltpu.VMEM((2, 2, lines // 2, slots), f32),
            pltpu.VMEM((16, lines // 2, slots), f32),
            dma((3,)), dma, dma((groups,)), dma, dma,
            *[pltpu.SemaphoreType.REGULAR] * 3,
        ]
    else:
        scratch = [
            field, field, sample, sample, sample, index, index, counts,
            pltpu.VMEM((groups, ROWS, slots), f32), pltpu.VMEM((groups, ROWS, slots), f32),
            x_pair, h_pair, field, h_pair, x_pair, h_pair,
            dma((8,)), dma((groups,)), dma((groups,)), *[dma((2,))] * 8, dma,
        ]
    outs = pl.pallas_call(
        functools.partial(near_kernel if near else kernel, groups, blocks),
        out_shape=[pltpu.VMEM(value.shape, f32)] * 3,
        in_specs=[pl.BlockSpec(memory_space=pltpu.HBM)] * 8,
        out_specs=[pl.BlockSpec(memory_space=pltpu.VMEM)] * 3,
        scratch_shapes=scratch,
        compiler_params=pltpu.CompilerParams(collective_id=0, has_side_effects=True),
        name="step",
    )(value, avoid, weight, offy, offs, xy, hs, count)
    outs = pl.pallas_call(
        write_out,
        out_shape=[jax.ShapeDtypeStruct(value.shape, f32)] * 3,
        in_specs=[pl.BlockSpec(memory_space=pl.ANY)] * 3,
        out_specs=[pl.BlockSpec(memory_space=pl.ANY)] * 3,
        scratch_shapes=[dma((3,))],
        compiler_params=pltpu.CompilerParams(vmem_limit_bytes=1 << 20),
        name="write_out",
    )(*outs)
    return tuple(jnp.transpose(o, (0, 3, 1, 2)) for o in outs)


def solution(mesh):
    field = P("ha", None, "gx", None)
    sample = P("gx", "ha", None, None)
    return jax.shard_map(
        functools.partial(on_device, mesh.shape["gx"], mesh.shape["ha"]),
        mesh=mesh,
        in_specs=(field, field, sample, sample, sample, sample, sample, P("gx", "ha", None)),
        out_specs=(field, field, field),
        check_vma=False,
    )
```

```python
import functools
import math

import jax
import jax.numpy as jnp
import numpy as np
from jax import lax
from jax.experimental import pallas as pl
from jax.experimental.pallas import tpu as pltpu
from jax.sharding import PartitionSpec as P

TIME_STEP = 0.3
SHARPNESS = 2.0
SOFTENING = 0.1
TURN_RATE = 0.5
ACCELERATION = 0.3
SLOWEST = 0.2
SPEED_RANGE = 0.8
ROWS = 8
MESH = pl.DeviceIdType.MESH


def smooth_abs(slope):
    return jnp.sqrt(slope * slope + SOFTENING * SOFTENING)


def upper(plane, axis):
    n = plane.shape[axis]
    return jnp.concatenate(
        [lax.slice_in_dim(plane, 1, n, axis=axis), lax.slice_in_dim(plane, n - 1, n, axis=axis)], axis
    )


def lower(plane, axis):
    n = plane.shape[axis]
    return jnp.concatenate(
        [lax.slice_in_dim(plane, 0, 1, axis=axis), lax.slice_in_dim(plane, 0, n - 1, axis=axis)], axis
    )


def spread(up, down, axis):
    n = up.shape[axis]
    from_lower = jnp.concatenate(
        [lax.slice_in_dim(down, 0, 1, axis=axis), lax.slice_in_dim(up, 0, n - 1, axis=axis)], axis
    )
    from_upper = jnp.concatenate(
        [lax.slice_in_dim(down, 1, n, axis=axis), lax.slice_in_dim(up, n - 1, n, axis=axis)], axis
    )
    return from_lower + from_upper


def pick(table, index):
    chosen = jnp.float32(table[0])
    for i in range(1, len(table)):
        chosen = jnp.where(index == i, jnp.float32(table[i]), chosen)
    return chosen


def kernel(
    groups, blocks,
    value_h, avoid_h, weight_h, offy_h, offs_h, xy_h, hs_h, count_h,
    next_o, vgrad_o, agrad_o,
    value, avoid, weight, offy, offs, xy, hs, count,
    pay, got, xhalo, hhalo, carried, turned, cxhalo, chhalo,
    in_sem, pay_send, pay_recv, x_send, x_recv, h_send, h_recv,
    cx_send, cx_recv, ch_send, ch_recv, self_sem,
):
    heads, cells, lines, speeds = value.shape
    slots = weight.shape[1]
    me = lax.axis_index("gx")
    hb = lax.axis_index("ha")
    h_next = lax.rem(hb + 1, blocks)
    h_prev = lax.rem(hb + blocks - 1, blocks)
    has_prev = me > 0
    has_next = me < groups - 1

    barrier = pltpu.get_barrier_semaphore()

    def greet(d):
        pl.semaphore_signal(
            barrier, inc=1, device_id=(lax.rem(me + d, groups), hb), device_id_type=MESH
        )

    if groups <= 8:
        for d in range(1, groups):
            greet(d)
    else:
        pl.loop(1, groups)(greet)
    for other in (h_prev, h_next):
        pl.semaphore_signal(barrier, inc=1, device_id=(me, other), device_id_type=MESH)

    pairs = (
        (weight_h, weight), (offy_h, offy), (offs_h, offs), (xy_h, xy), (hs_h, hs), (count_h, count),
        (value_h, value), (avoid_h, avoid),
    )
    loads = [pltpu.make_async_copy(a, b, in_sem.at[i]) for i, (a, b) in enumerate(pairs)]
    for load in loads:
        load.start()
    for load in loads[:6]:
        load.wait()

    owners = lax.broadcasted_iota(jnp.int32, (groups, groups), 0)
    lanes = lax.broadcasted_iota(jnp.int32, (groups, groups), 1)
    live = jnp.sum(
        jnp.where(owners == lanes, jnp.broadcast_to(count[...], (groups, groups)), 0).astype(jnp.float32),
        axis=1, keepdims=True,
    )
    slot = lax.broadcasted_iota(jnp.int32, (groups, slots), 1).astype(jnp.float32)
    w = jnp.where(slot < live, weight[...], 0.0)
    oy = offy[...]
    os = offs[...]
    state = hs[...]
    head = lax.div(state, speeds)
    pay[:, 0, :] = w * (1.0 - oy)
    pay[:, 1, :] = w * oy
    pay[:, 2, :] = 1.0 - os
    pay[:, 3, :] = os
    pay[:, 4, :] = (head * (cells * lines) + xy[...]).astype(jnp.float32)
    pay[:, 5, :] = (state - head * speeds).astype(jnp.float32)
    pay[:, 6, :] = jnp.zeros((groups, slots), jnp.float32)
    pay[:, 7, :] = jnp.zeros((groups, slots), jnp.float32)

    loads[6].wait()
    pl.semaphore_wait(barrier, groups - 1 + 2)

    def h_copy(side):
        return pltpu.make_async_remote_copy(
            value.at[0 if side == 0 else heads - 1], hhalo.at[1 - side],
            h_send.at[side], h_recv.at[1 - side],
            device_id=(me, h_prev if side == 0 else h_next), device_id_type=MESH,
        )

    def x_copy(side):
        return pltpu.make_async_remote_copy(
            value.at[:, 0 if side == 0 else cells - 1], xhalo.at[1 - side],
            x_send.at[side], x_recv.at[1 - side],
            device_id=(me - 1 if side == 0 else me + 1, hb), device_id_type=MESH,
        )

    def pay_copy(d):
        peer = lax.rem(me + d, groups)
        return pltpu.make_async_remote_copy(
            pay.at[peer], got.at[d], pay_send.at[d], pay_recv.at[d],
            device_id=(peer, hb), device_id_type=MESH,
        )

    for side in range(2):
        h_copy(side).start()
    for side, has in ((0, has_prev), (1, has_next)):
        @pl.when(has)
        def _():
            x_copy(side).start()

    if groups <= 8:
        for d in range(groups - 1, 0, -1):
            pay_copy(d).start()
    else:
        pl.loop(1, groups)(lambda d: pay_copy(d).start())
    mine = pltpu.make_async_copy(pay.at[me], got.at[0], self_sem)
    mine.start()
    loads[7].wait()

    for side, has in ((0, has_prev), (1, has_next)):
        @pl.when(jnp.logical_not(has))
        def _():
            xhalo[side] = value[:, 0 if side == 0 else cells - 1]

    total = heads * blocks
    angles = [np.float32(2.0 * math.pi / total) * np.float32(k) for k in range(total)]
    cosines = [float(np.cos(a)) for a in angles]
    sines = [float(np.sin(a)) for a in angles]
    speed = SLOWEST + SPEED_RANGE * lax.broadcasted_iota(jnp.int32, (1, speeds), 1).astype(
        jnp.float32
    ) / (speeds - 1)
    cx = [pick(cosines, hb * heads + h) * speed for h in range(heads)]
    cy = [pick(sines, hb * heads + h) * speed for h in range(heads)]
    grid = [(h, x) for h in range(heads) for x in range(cells)]
    v = {(h, x): value[h, x] for h, x in grid}
    part, s_slope = {}, {}
    for h, x in grid:
        here = v[h, x]
        up, down = upper(here, 0), lower(here, 0)
        term = cy[h] * (up - down) * 0.5 - (up - 2.0 * here + down) * 0.5
        up, down = upper(here, 1), lower(here, 1)
        slope = 0.5 * (up - down)
        size = smooth_abs(slope)
        s_slope[h, x] = slope / size
        part[h, x] = term + ACCELERATION * size - ACCELERATION * 0.5 * (up - 2.0 * here + down)

    for side in range(2):
        h_copy(side).wait_recv()
    for side, has in ((0, has_prev), (1, has_next)):
        @pl.when(has)
        def _():
            x_copy(1 - side).wait_recv()
    for x in range(cells):
        v[-1, x] = hhalo[0, x]
        v[heads, x] = hhalo[1, x]
    for h in range(heads):
        v[h, -1] = xhalo[0, h]
        v[h, cells] = xhalo[1, h]

    share, h_slope, above = {}, {}, {}
    for h, x in grid:
        here = v[h, x]
        up, down = v[h + 1, x], v[h - 1, x]
        slope = 0.5 * (up - down)
        size = smooth_abs(slope)
        h_slope[h, x] = slope / size
        turning = TURN_RATE * size - TURN_RATE * 0.5 * (up - 2.0 * here + down)
        up, down = v[h, x + 1], v[h, x - 1]
        across = cx[h] * (up - down) * 0.5 - (up - 2.0 * here + down) * 0.5
        relaxed = here - TIME_STEP * (across + part[h, x] + turning)
        floor = avoid[h, x]
        excess = SHARPNESS * (relaxed - floor)
        small = jnp.exp(-jnp.abs(excess))
        share[h, x] = jnp.where(excess >= 0.0, 1.0, small) / (1.0 + small)
        above[h, x] = (excess, small)

    rows = heads * cells * lines
    row_id = lax.broadcasted_iota(jnp.int32, (rows, slots), 0).astype(jnp.float32)
    speed_id = lax.broadcasted_iota(jnp.int32, (speeds, slots), 0).astype(jnp.float32)

    def operands(d):
        one = got[d]
        cell = jnp.broadcast_to(one[4:5], (rows, slots))
        left = jnp.where(row_id == cell, one[0:1], jnp.where(row_id == cell + 1.0, one[1:2], 0.0))
        cell = jnp.broadcast_to(one[5:6], (speeds, slots))
        right = jnp.where(
            speed_id == cell, one[2:3], jnp.where(speed_id == cell + 1.0, one[3:4], 0.0)
        )
        return left, right

    def product(left, right):
        return lax.dot_general(
            left, right, (((1,), (1,)), ((), ())),
            precision=lax.Precision.HIGHEST, preferred_element_type=jnp.float32,
        )

    mine.wait()
    if groups <= 8:
        for d in range(1, groups):
            pay_copy(d).wait_recv()
        both = [operands(d) for d in range(groups)]
        deposit = product(
            jnp.concatenate([b[0] for b in both], 1), jnp.concatenate([b[1] for b in both], 1)
        )
    else:
        pl.loop(1, groups)(lambda d: pay_copy(d).wait_recv())
        deposit = lax.fori_loop(
            0, groups, lambda d, so_far: so_far + product(*operands(d)),
            jnp.zeros((rows, speeds), jnp.float32),
        )

    c, adj = {}, {}
    for n, (h, x) in enumerate(grid):
        adjoint = deposit[n * lines : (n + 1) * lines]
        c[h, x] = adjoint * share[h, x]
        carried[h, x] = c[h, x]
        adj[h, x] = adjoint
    def cx_copy(side):
        return pltpu.make_async_remote_copy(
            carried.at[:, 0 if side == 0 else cells - 1], cxhalo.at[1 - side],
            cx_send.at[side], cx_recv.at[1 - side],
            device_id=(me - 1 if side == 0 else me + 1, hb), device_id_type=MESH,
        )

    for side, has in ((0, has_prev), (1, has_next)):
        @pl.when(has)
        def _():
            cx_copy(side).start()

        @pl.when(jnp.logical_not(has))
        def _():
            cxhalo[side] = jnp.zeros_like(cxhalo[side])
    ahead, back = {}, {}
    for h, x in grid:
        pull = (0.5 * TURN_RATE) * c[h, x] * h_slope[h, x]
        keep = (0.5 * TURN_RATE) * c[h, x]
        ahead[h, x] = pull - keep
        back[h, x] = -pull - keep
    for x in range(cells):
        turned[0, x] = back[0, x]
        turned[1, x] = ahead[heads - 1, x]

    def ch_copy(side):
        return pltpu.make_async_remote_copy(
            turned.at[side], chhalo.at[1 - side], ch_send.at[side], ch_recv.at[1 - side],
            device_id=(me, h_prev if side == 0 else h_next), device_id_type=MESH,
        )

    for side in range(2):
        ch_copy(side).start()

    local = {}
    for h, x in grid:
        excess, small = above[h, x]
        next_o[h, x] = avoid[h, x] + (jnp.maximum(excess, 0.0) + jnp.log1p(small)) / SHARPNESS
        agrad_o[h, x] = adj[h, x] * (jnp.where(excess >= 0.0, small, 1.0) / (1.0 + small))
        here = c[h, x]
        grad = spread((0.5 * cy[h] - 0.5) * here, (-0.5 * cy[h] - 0.5) * here, 0)
        pull = (0.5 * ACCELERATION) * here * s_slope[h, x]
        keep = (0.5 * ACCELERATION) * here
        grad = grad + spread(pull - keep, -pull - keep, 1)
        local[h, x] = grad + (2.0 + TURN_RATE + ACCELERATION) * here

    for side in range(2):
        ch_copy(side).wait_recv()
    for side, has in ((0, has_prev), (1, has_next)):
        @pl.when(has)
        def _():
            cx_copy(1 - side).wait_recv()
    for h, x in grid:
        grad = local[h, x]
        grad = grad + (ahead[h - 1, x] if h > 0 else chhalo[0, x])
        grad = grad + (back[h + 1, x] if h < heads - 1 else chhalo[1, x])
        low, high = 0.5 * cx[h] - 0.5, -0.5 * cx[h] - 0.5
        if x > 0:
            grad = grad + low * c[h, x - 1]
        else:
            grad = grad + jnp.where(has_prev, low * cxhalo[0, h], high * c[h, x])
        if x < cells - 1:
            grad = grad + high * c[h, x + 1]
        else:
            grad = grad + jnp.where(has_next, high * cxhalo[1, h], low * c[h, x])
        vgrad_o[h, x] = c[h, x] - TIME_STEP * grad

    for side in range(2):
        h_copy(side).wait_send()
        ch_copy(side).wait_send()
    for side, has in ((0, has_prev), (1, has_next)):
        @pl.when(has)
        def _():
            x_copy(side).wait_send()
            cx_copy(side).wait_send()
    if groups <= 8:
        for d in range(1, groups):
            pay_copy(d).wait_send()
    else:
        pl.loop(1, groups)(lambda d: pay_copy(d).wait_send())


def near_kernel(
    groups, blocks,
    value_h, avoid_h, weight_h, offy_h, offs_h, xy_h, hs_h, count_h,
    next_o, vgrad_o, agrad_o,
    fields, sample, cell, count, pay, got, packed, corner, halo,
    in_sem, pay_send, pay_recv, halo_send, halo_recv, row_in, late, late_near,
):
    _, heads, cells, lines, speeds = fields.shape
    value, avoid = fields.at[0], fields.at[1]
    slots = sample.shape[2]
    me = lax.axis_index("gx")
    hb = lax.axis_index("ha")
    h_next = lax.rem(hb + 1, blocks)
    h_prev = lax.rem(hb + blocks - 1, blocks)
    h_side = (h_prev, h_next)
    has_prev = me > 0
    has_next = me < groups - 1
    base = 2
    in_base = me < base

    is_even = lax.rem(hb, 2) == 0
    upper_pair = hb >= blocks // 2
    mate_side = 1 - lax.rem(hb, 2)
    far_side = 1 - mate_side
    mate, far = (lax.rem(hb + blocks - 1 + 2 * s, blocks) for s in (mate_side, far_side))
    level = lax.div(me + 1, 2)
    mate_before = jnp.where(is_even, jnp.minimum(2 * level + 1, groups), jnp.maximum(2 * level - 1, base))
    far_before = jnp.where(
        upper_pair,
        jnp.minimum(2 * level + jnp.where(is_even, 3, 1), groups),
        jnp.maximum(2 * level - jnp.where(is_even, 1, 3), base),
    )
    earlier = me + mate_before + far_before

    def near_rows(before):
        return jnp.clip(me - 1, base, before), jnp.clip(me + 2, base, before)

    mate_near, far_near = near_rows(mate_before), near_rows(far_before)
    around = jnp.minimum(me + 2, groups) - jnp.maximum(me - 1, base)
    near_later = jnp.where(has_next, 1, 0) + 2 * around
    for low, high in (mate_near, far_near):
        near_later = near_later - (high - low)

    barrier = pltpu.get_barrier_semaphore()

    def signal(sem, j, h):
        pl.semaphore_signal(sem, inc=1, device_id=(j, h), device_id_type=MESH)

    def rows(lo, hi, body):
        lax.fori_loop(lo, hi, lambda j, carry: (body(j), carry)[1], 0)

    def signal_at(sem, h):
        return lambda j: signal(sem, j, h)

    def wait_some(sem, n):
        @pl.when(n > 0)
        def _():
            pl.semaphore_wait(sem, n)

    @pl.when(in_base)
    def _():
        for j in range(groups - 1, base - 1, -1):
            for h in (far, mate, hb):
                signal(barrier, j, h)

    @pl.when(jnp.logical_not(in_base))
    def _():
        for before, h in ((far_before, far), (mate_before, mate), (me + 1, hb)):
            rows(before, groups, lambda j: signal(barrier, groups - 1 + before - j, h))
        for j in range(base):
            for h in (far, mate, hb):
                signal(barrier, j, h)

    loads = [
        pltpu.make_async_copy(a, b, in_sem.at[i])
        for a, b, i in (
            (weight_h, sample.at[0], 0), (offy_h, sample.at[1], 0), (offs_h, sample.at[2], 0),
            (xy_h, cell.at[0], 0), (hs_h, cell.at[1], 0), (count_h, count, 1),
            (value_h, value, 2), (avoid_h, avoid, 2),
        )
    ]
    for load in loads:
        load.start()
    loaded = [pltpu.make_async_copy(r, r, in_sem.at[i]) for r, i in ((sample, 0), (count, 1), (fields, 2))]

    pay[0] = jnp.zeros(pay.shape[1:], jnp.float32)
    pay[groups + 1] = jnp.zeros(pay.shape[1:], jnp.float32)

    def copy(src, dst, send_sem, recv_sem, j, h):
        return pltpu.make_async_remote_copy(
            src, dst, send_sem, recv_sem, device_id=(j, h), device_id_type=MESH
        )

    def x_slot(side):
        return 6 + side * 5

    def h_halo(side, h):
        dst = halo.at[pl.ds(3 * (1 - side), 3)]
        copy(packed.at[side], dst, halo_send, halo_recv, me, h).start()

    def x_halo(side):
        at = x_slot(1 - side)
        copy(packed.at[2 + side], halo.at[at : at + 3], halo_send, halo_recv, me - 1 + 2 * side, hb).start()

    def corner_halo(side, h_to, h):
        at = x_slot(1 - side) + 4 - h_to
        copy(corner.at[side, h_to], halo.at[at], halo_send, halo_recv, me - 1 + 2 * side, h).start()

    def turn_of(j):
        turn = lax.rem(me - j - 1 + 2 * groups, groups)
        return 5 * turn, jnp.where(turn < groups - 1, lax.div(turn, 2), groups // 2)

    def send_side(j, side, h):
        at, sem = turn_of(j)
        copy(pay.at[j + 1], got.at[at + 4 - side], pay_send, pay_recv.at[sem], j, h).start()

    def send_own(j):
        at, sem = turn_of(j)
        copy(pay.at[pl.ds(j, 3)], got.at[pl.ds(at, 3)], pay_send, pay_recv.at[sem], j, hb).start()

    def send_mate(j):
        send_side(j, mate_side, mate)

    def send_far(j):
        send_side(j, far_side, far)

    def send_all(j):
        send_own(j)
        send_mate(j)
        send_far(j)

    loaded[0].wait()
    loaded[1].wait()
    owners = lax.broadcasted_iota(jnp.int32, (groups, groups), 0)
    lanes = lax.broadcasted_iota(jnp.int32, (groups, groups), 1)
    live = jnp.sum(
        jnp.where(owners == lanes, jnp.broadcast_to(count[...], (groups, groups)), 0).astype(jnp.float32),
        axis=1, keepdims=True,
    )
    slot = lax.broadcasted_iota(jnp.int32, (groups, slots), 1).astype(jnp.float32)
    w = jnp.where(slot < live, sample[0], 0.0)
    oy = sample[1]
    state = cell[1]
    head = lax.div(state, speeds)
    row = head * (cells * lines) + cell[0]
    pay[1 : groups + 1, 0, :] = w * (1.0 - oy)
    pay[1 : groups + 1, 1, :] = w * oy
    pay[1 : groups + 1, 2, :] = sample[2]
    pay[1 : groups + 1, 3, :] = (row * speeds + (state - head * speeds)).astype(jnp.float32)
    own_at = 5 * (groups - 1)
    pltpu.make_async_copy(
        pay.at[pl.ds(me, 3)], got.at[own_at : own_at + 3], pay_recv.at[groups // 2]
    ).start()
    loaded[2].wait()
    grid = [(h, x) for h in range(heads) for x in range(cells)]
    plane = {(i, h, x): fields[i, h, x] for i in range(2) for h, x in grid}
    whole = jnp.concatenate([plane[0, h, x] for h, x in grid], 1)
    mid = lines // 2
    for side, edge in ((0, 0), (1, 1)):
        h_edge, x_edge = edge * (heads - 1), edge * (cells - 1)
        over_h = [plane[1, h_edge, x] for x in range(cells)]
        over_x = [plane[1, h, x_edge] for h in range(heads)]
        h_tile = [p[:mid] for p in over_h] + [p[mid:] for p in over_h]
        x_tile = [q for p in over_x for q in (p[:mid], p[mid:])]
        for to, tile in ((side, h_tile), (2 + side, x_tile)):
            packed[to, 0] = whole[:mid]
            packed[to, 1] = whole[mid:]
            packed[to, 2] = jnp.concatenate(tile, 1)
        for h in range(2):
            p = plane[0, h * (heads - 1), x_edge]
            corner[side, h] = jnp.concatenate([p[:mid], p[mid:]] * 2, 1)

    @pl.when(jnp.logical_not(in_base))
    def _():
        pl.semaphore_wait(barrier, earlier)
        @pl.when(me == base)
        def _():
            for j in range(base):
                signal(row_in, j, hb)

        rows(base, me - 1, signal_at(late, hb))
        for (low, high), before, h in ((mate_near, mate_before, mate), (far_near, far_before, far)):
            rows(base, low, signal_at(late, h))
            rows(high, before, signal_at(late, h))
        for j in range(base):
            send_all(j)
        rows(jnp.maximum(me - 1, base), me, signal_at(late_near, hb))
        rows(*mate_near, signal_at(late_near, mate))
        rows(*far_near, signal_at(late_near, far))

        x_halo(0)
        others = ((mate_before, mate_side, mate), (far_before, far_side, far))

        def near_halos(comes):
            for before, side, h in others:
                pl.when(comes(me - 1, before))(functools.partial(corner_halo, 0, side, h))
                pl.when(comes(me, before))(functools.partial(h_halo, side, h))
                pl.when(comes(me + 1, before) & has_next)(functools.partial(corner_halo, 1, side, h))

        near_halos(lambda j, before: j < before)
        rows(base, me, send_own)
        rows(base, mate_before, send_mate)
        rows(base, far_before, send_far)

        wait_some(late_near, near_later)
        pl.when(has_next)(functools.partial(x_halo, 1))
        near_halos(lambda j, before: j >= before)
        wait_some(late, 3 * groups - 1 - earlier - near_later)
        rows(me + 1, groups, send_own)
        rows(mate_before, groups, send_mate)
        rows(far_before, groups, send_far)

    def x_and_corners(side):
        x_halo(side)
        for h in range(2):
            corner_halo(side, h, h_side[h])

    @pl.when(in_base)
    def _():
        pl.semaphore_wait(row_in, 1)
        for side in range(2):
            h_halo(side, h_side[side])
            send_side(me, side, h_side[side])
        for row in range(base):
            @pl.when(me == row)
            def _():
                x_and_corners(1 - row)
                send_all(1 - row)
        pl.semaphore_wait(barrier, 3 * (groups - base))
        pl.when(me == base - 1)(functools.partial(x_and_corners, 1))
        rows(base, groups, send_own)
        rows(base, groups, send_mate)
        rows(base, groups, send_far)

    width = heads * cells * speeds
    half, quarter = width // 2, width // 4
    lane = lax.broadcasted_iota(jnp.int32, (1, width), 1)
    place = lax.div(lane, quarter)
    within = lax.rem(lane, quarter)
    even = lax.rem(place, 2) == 0
    left_half = place < 2
    total = heads * blocks
    angles = [np.float32(2.0 * math.pi / total) * np.float32(k) for k in range(total)]
    cosines = [float(np.cos(a)) for a in angles]
    sines = [float(np.sin(a)) for a in angles]
    speed = SLOWEST + SPEED_RANGE * within.astype(jnp.float32) / (speeds - 1)
    turn = [lax.rem(hb * heads + h + total, total) for h in range(-1, heads + 1)]
    cos_of = [pick(cosines, t) for t in turn]
    sin_of = [pick(sines, t) for t in turn]
    cx_own, cy_own = (jnp.where(left_half, a[1], a[2]) * speed for a in (cos_of, sin_of))
    cx_out, cy_out = (jnp.where(left_half, a[0], a[3]) * speed for a in (cos_of, sin_of))

    def shift(a, by):
        return pltpu.roll(a, by % width, 1)

    def forward(here, floor, cx, cy, h_up, h_down, x_up, x_down):
        up, down = upper(here, 0), lower(here, 0)
        rate = cy * (up - down) * 0.5 - (up - 2.0 * here + down) * 0.5
        up = jnp.where(within == quarter - 1, here, shift(here, -1))
        down = jnp.where(within == 0, here, shift(here, 1))
        slope = 0.5 * (up - down)
        size = smooth_abs(slope)
        s_slope = slope / size
        rate = rate + ACCELERATION * size - ACCELERATION * 0.5 * (up - 2.0 * here + down)
        slope = 0.5 * (h_up - h_down)
        size = smooth_abs(slope)
        h_slope = slope / size
        rate = rate + TURN_RATE * size - TURN_RATE * 0.5 * (h_up - 2.0 * here + h_down)
        rate = rate + cx * (x_up - x_down) * 0.5 - (x_up - 2.0 * here + x_down) * 0.5
        excess = SHARPNESS * (here - TIME_STEP * rate - floor)
        small = jnp.exp(-jnp.abs(excess))
        share = jnp.where(excess >= 0.0, 1.0, small) / (1.0 + small)
        pull = (0.5 * TURN_RATE) * share * h_slope
        keep = (0.5 * TURN_RATE) * share
        return excess, small, share, s_slope, pull - keep, -pull - keep

    def all_halos(sending):
        def wait(n):
            view = halo.at[0:n]
            c = copy(view, view, halo_send, halo_recv, me, h_next)
            c.wait_send() if sending else c.wait_recv()

        @pl.when(has_prev & has_next)
        def _():
            wait(16)

        @pl.when(jnp.logical_not(has_prev & has_next))
        def _():
            wait(11)

    def unpack(a):
        return {(h, x): a[:, n * speeds : (n + 1) * speeds] for n, (h, x) in enumerate(grid)}

    all_halos(False)
    def tall_pair(top, bottom):
        return jnp.concatenate([top, bottom], 0)

    own = whole
    floor = jnp.concatenate([plane[1, h, x] for h, x in grid], 1)
    hp, hn, xp, xn = (tall_pair(halo[i], halo[i + 1]) for i in (0, 3, 6, 11))
    hp_floor, hn_floor, xp_floor, xn_floor = (halo[i] for i in (2, 5, 8, 13))
    on_even, on_odd = [], []
    for i in (9, 10, 14, 15):
        tile = halo[i]
        other = shift(tile, quarter)
        on_even.append(tall_pair(tile, other))
        on_odd.append(tall_pair(other, tile))
    edge_h = shift(jnp.where(left_half, hn, hp), half)
    edge_x = jnp.where(even, shift(xp, -quarter), shift(xn, quarter))
    up_x = jnp.where(even, shift(own, -quarter), jnp.where(has_next, edge_x, own))
    down_x = jnp.where(even, jnp.where(has_prev, edge_x, own), shift(own, quarter))
    excess, small, share, s_slope, ahead, back = forward(
        own, floor, cx_own, cy_own,
        shift(jnp.where(left_half, hn, own), half), shift(jnp.where(left_half, own, hp), half),
        up_x, down_x,
    )
    next_v = unpack(floor + (jnp.maximum(excess, 0.0) + jnp.log1p(small)) / SHARPNESS)
    for h, x in grid:
        next_o[h, x] = next_v[h, x]
    rest = unpack(jnp.where(excess >= 0.0, small, 1.0) / (1.0 + small))
    share, s_slope, ahead, back = (unpack(a) for a in (share, s_slope, ahead, back))

    up_x = jnp.where(even, shift(edge_h, -quarter), jnp.where(left_half, on_odd[2], on_odd[3]))
    down_x = jnp.where(even, jnp.where(left_half, on_even[0], on_even[1]), shift(edge_h, quarter))
    edge_floor = tall_pair(
        jnp.where(left_half, hp_floor, shift(hn_floor, half)),
        jnp.where(left_half, shift(hp_floor, half), hn_floor),
    )
    out = forward(
        edge_h, edge_floor, cx_out, cy_out,
        jnp.where(left_half, own, hn), jnp.where(left_half, hp, own),
        jnp.where(even | has_next, up_x, edge_h), jnp.where(even & jnp.logical_not(has_prev), edge_h, down_x),
    )
    out = unpack(jnp.where(left_half, out[4], out[5]))
    for x in range(cells):
        ahead[-1, x], back[heads, x] = out[0, x], out[1, x]

    turned = shift(edge_x, half)
    up_h = jnp.where(left_half, turned, jnp.where(even, on_even[1], on_odd[3]))
    down_h = jnp.where(left_half, jnp.where(even, on_even[0], on_odd[2]), turned)
    edge_floor = tall_pair(
        jnp.where(even, xp_floor, shift(xn_floor, quarter)),
        jnp.where(even, shift(xp_floor, -quarter), xn_floor),
    )
    out = forward(
        edge_x, edge_floor, cx_own, cy_own,
        up_h, down_h, jnp.where(even, own, xn), jnp.where(even, xp, own),
    )
    out = unpack(out[2])
    for h in range(heads):
        share[h, -1], share[h, cells] = out[h, 0], out[h, 1]
    speed = SLOWEST + SPEED_RANGE * lax.broadcasted_iota(jnp.int32, (1, speeds), 1).astype(
        jnp.float32
    ) / (speeds - 1)
    cx = [cos_of[h + 1] * speed for h in range(heads)]
    cy = [sin_of[h + 1] * speed for h in range(heads)]

    span = cells * lines
    inside = lax.broadcasted_iota(jnp.int32, (heads * span, slots), 0)
    edge = lax.broadcasted_iota(jnp.int32, (heads * lines, slots), 0)
    edge = lax.div(edge, lines) * span + lax.rem(edge, lines)
    side_rows = lax.broadcasted_iota(jnp.int32, (span, slots), 0)
    ids = [
        i.astype(jnp.float32).astype(jnp.bfloat16)
        for i in (edge + (cells - 1) * lines, inside, edge, side_rows + (heads - 1) * span, side_rows)
    ]
    speed_id = lax.broadcasted_iota(jnp.int32, (speeds, slots), 0).astype(jnp.float32)
    speed_id = speed_id.astype(jnp.bfloat16)

    def tall(row, n):
        part = jnp.broadcast_to(row, (16, slots)).astype(jnp.bfloat16)
        return jnp.concatenate([part] * (n // 16), 0)

    def deposit(one, row_id):
        n = row_id.shape[0]
        weight0, weight1, up_s, code = one[0:1], one[1:2], one[2:3], one[3:4]
        row = jnp.floor(code * (1.0 / speeds))
        cell = code - row * speeds
        here, above_it = row_id == tall(row, n), row_id == tall(row + 1.0, n)
        zero = jnp.zeros(row_id.shape, jnp.bfloat16)
        high, low = [], []
        for f in (1.0 - up_s, up_s):
            a, b = weight0 * f, weight1 * f
            for part in (high, low):
                part.append(jnp.where(here, tall(a, n), jnp.where(above_it, tall(b, n), zero)))
                a, b = (t - t.astype(jnp.bfloat16).astype(jnp.float32) for t in (a, b))
        left = jnp.concatenate([jnp.concatenate(part, 1) for part in (high, low)], 0)
        one_hot = jnp.ones(speed_id.shape, jnp.bfloat16)
        right = jnp.concatenate(
            [
                jnp.where(speed_id == tall(c, speeds), one_hot, jnp.zeros_like(one_hot))
                for c in (cell, cell + 1.0)
            ],
            1,
        )
        both = lax.dot_general(
            left, right, (((1,), (1,)), ((), ())), preferred_element_type=jnp.float32
        )
        return both[:n] + both[n:]

    def collect(at, count, sem, sums):
        view = got.at[pl.ds(at, count)]
        copy(view, view, pay_send, pay_recv.at[sem], me, h_next).wait_recv()
        sums = list(sums)
        for i in range(count):
            sums[i % 5] = sums[i % 5] + deposit(got[at + i], ids[i % 5])
        return tuple(sums)

    sums = tuple(jnp.zeros((i.shape[0], speeds), jnp.float32) for i in ids)
    sums = lax.fori_loop(0, groups // 2 - 1, lambda n, so_far: collect(10 * n, 10, n, so_far), sums)
    sums = collect(own_at, 5, groups // 2, sums)
    sums = collect(own_at - 5, 5, groups // 2 - 1, sums)

    adj, c = {}, {}
    for n, (h, x) in enumerate(grid):
        adj[h, x] = sums[1][n * lines : (n + 1) * lines]
        c[h, x] = adj[h, x] * share[h, x]
    for h in range(heads):
        c[h, -1] = sums[0][h * lines : (h + 1) * lines] * share[h, -1]
        c[h, cells] = sums[2][h * lines : (h + 1) * lines] * share[h, cells]
    for x in range(cells):
        adj[-1, x] = sums[3][x * lines : (x + 1) * lines]
        adj[heads, x] = sums[4][x * lines : (x + 1) * lines]

    for h, x in grid:
        agrad_o[h, x] = adj[h, x] * rest[h, x]
        here = c[h, x]
        grad = spread((0.5 * cy[h] - 0.5) * here, (-0.5 * cy[h] - 0.5) * here, 0)
        pull = (0.5 * ACCELERATION) * here * s_slope[h, x]
        keep = (0.5 * ACCELERATION) * here
        grad = grad + spread(pull - keep, -pull - keep, 1)
        grad = grad + (2.0 + TURN_RATE + ACCELERATION) * here
        grad = grad + adj[h - 1, x] * ahead[h - 1, x] + adj[h + 1, x] * back[h + 1, x]
        low, high = 0.5 * cx[h] - 0.5, -0.5 * cx[h] - 0.5
        if x > 0:
            grad = grad + low * c[h, x - 1]
        else:
            grad = grad + jnp.where(has_prev, low * c[h, -1], high * here)
        if x < cells - 1:
            grad = grad + high * c[h, x + 1]
        else:
            grad = grad + jnp.where(has_next, high * c[h, cells], low * here)
        vgrad_o[h, x] = here - TIME_STEP * grad

    all_halos(True)
    view = got.at[0 : 5 * groups - 3]
    copy(view, view, pay_send, pay_recv.at[0], me, h_next).wait_send()


def write_out(next_v, vgrad_v, agrad_v, next_o, vgrad_o, agrad_o, sem):
    copies = [
        pltpu.make_async_copy(a, b, sem.at[i])
        for i, (a, b) in enumerate(((next_v, next_o), (vgrad_v, vgrad_o), (agrad_v, agrad_o)))
    ]
    for copy in copies:
        copy.start()
    for copy in copies:
        copy.wait()


def on_device(groups, blocks, value, avoid, weight, offy, offs, xy, hs, count):
    slots = weight.shape[3]
    value = jnp.transpose(value, (0, 2, 3, 1))
    avoid = jnp.transpose(avoid, (0, 2, 3, 1))
    weight, offy, offs, xy, hs = (a.reshape(groups, slots) for a in (weight, offy, offs, xy, hs))
    count = count.reshape(1, groups)
    heads, cells, lines, speeds = value.shape
    f32 = jnp.float32
    dma = pltpu.SemaphoreType.DMA
    field = pltpu.VMEM(value.shape, f32)
    x_pair = pltpu.VMEM((2, heads, lines, speeds), f32)
    h_pair = pltpu.VMEM((2, cells, lines, speeds), f32)
    near = groups in (4, 8) and blocks == 4 and heads == cells == 2 and 4 * speeds == slots == 128 and lines == 16
    sample = pltpu.VMEM((groups, slots), f32)
    index = pltpu.VMEM((groups, slots), jnp.int32)
    counts = pltpu.VMEM((1, groups), jnp.int32)
    if near:
        scratch = [
            pltpu.VMEM((2, *value.shape), f32),
            pltpu.VMEM((5, groups, slots), f32), pltpu.VMEM((2, groups, slots), jnp.int32), counts,
            pltpu.VMEM((groups + 2, 4, slots), f32), pltpu.VMEM((5 * groups, 4, slots), f32),
            pltpu.VMEM((4, 3, lines // 2, slots), f32), pltpu.VMEM((2, 2, lines // 2, slots), f32),
            pltpu.VMEM((16, lines // 2, slots), f32),
            dma((3,)), dma, dma((groups // 2 + 1,)), dma, dma,
            *[pltpu.SemaphoreType.REGULAR] * 3,
        ]
    else:
        scratch = [
            field, field, sample, sample, sample, index, index, counts,
            pltpu.VMEM((groups, ROWS, slots), f32), pltpu.VMEM((groups, ROWS, slots), f32),
            x_pair, h_pair, field, h_pair, x_pair, h_pair,
            dma((8,)), dma((groups,)), dma((groups,)), *[dma((2,))] * 8, dma,
        ]
    outs = pl.pallas_call(
        functools.partial(near_kernel if near else kernel, groups, blocks),
        out_shape=[pltpu.VMEM(value.shape, f32)] * 3,
        in_specs=[pl.BlockSpec(memory_space=pltpu.HBM)] * 8,
        out_specs=[pl.BlockSpec(memory_space=pltpu.VMEM)] * 3,
        scratch_shapes=scratch,
        compiler_params=pltpu.CompilerParams(collective_id=0, has_side_effects=True),
        name="step",
    )(value, avoid, weight, offy, offs, xy, hs, count)
    outs = pl.pallas_call(
        write_out,
        out_shape=[jax.ShapeDtypeStruct(value.shape, f32)] * 3,
        in_specs=[pl.BlockSpec(memory_space=pl.ANY)] * 3,
        out_specs=[pl.BlockSpec(memory_space=pl.ANY)] * 3,
        scratch_shapes=[dma((3,))],
        compiler_params=pltpu.CompilerParams(vmem_limit_bytes=1 << 20),
        name="write_out",
    )(*outs)
    return tuple(jnp.transpose(o, (0, 3, 1, 2)) for o in outs)


def solution(mesh):
    field = P("ha", None, "gx", None)
    sample = P("gx", "ha", None, None)
    return jax.shard_map(
        functools.partial(on_device, mesh.shape["gx"], mesh.shape["ha"]),
        mesh=mesh,
        in_specs=(field, field, sample, sample, sample, sample, sample, P("gx", "ha", None)),
        out_specs=(field, field, field),
        check_vma=False,
    )
```

```python
import functools
import math

import jax
import jax.numpy as jnp
import numpy as np
from jax import lax
from jax.experimental import pallas as pl
from jax.experimental.pallas import tpu as pltpu
from jax.sharding import PartitionSpec as P

TIME_STEP = 0.3
SHARPNESS = 2.0
SOFTENING = 0.1
TURN_RATE = 0.5
ACCELERATION = 0.3
SLOWEST = 0.2
SPEED_RANGE = 0.8
ROWS = 8
MESH = pl.DeviceIdType.MESH


def smooth_abs(slope):
    return jnp.sqrt(slope * slope + SOFTENING * SOFTENING)


def upper(plane, axis):
    n = plane.shape[axis]
    return jnp.concatenate(
        [lax.slice_in_dim(plane, 1, n, axis=axis), lax.slice_in_dim(plane, n - 1, n, axis=axis)], axis
    )


def lower(plane, axis):
    n = plane.shape[axis]
    return jnp.concatenate(
        [lax.slice_in_dim(plane, 0, 1, axis=axis), lax.slice_in_dim(plane, 0, n - 1, axis=axis)], axis
    )


def spread(up, down, axis):
    n = up.shape[axis]
    from_lower = jnp.concatenate(
        [lax.slice_in_dim(down, 0, 1, axis=axis), lax.slice_in_dim(up, 0, n - 1, axis=axis)], axis
    )
    from_upper = jnp.concatenate(
        [lax.slice_in_dim(down, 1, n, axis=axis), lax.slice_in_dim(up, n - 1, n, axis=axis)], axis
    )
    return from_lower + from_upper


def pick(table, index):
    chosen = jnp.float32(table[0])
    for i in range(1, len(table)):
        chosen = jnp.where(index == i, jnp.float32(table[i]), chosen)
    return chosen


def kernel(
    groups, blocks,
    value_h, avoid_h, weight_h, offy_h, offs_h, xy_h, hs_h, count_h,
    next_o, vgrad_o, agrad_o,
    value, avoid, weight, offy, offs, xy, hs, count,
    pay, got, xhalo, hhalo, carried, turned, cxhalo, chhalo,
    in_sem, pay_send, pay_recv, x_send, x_recv, h_send, h_recv,
    cx_send, cx_recv, ch_send, ch_recv, self_sem,
):
    heads, cells, lines, speeds = value.shape
    slots = weight.shape[1]
    me = lax.axis_index("gx")
    hb = lax.axis_index("ha")
    h_next = lax.rem(hb + 1, blocks)
    h_prev = lax.rem(hb + blocks - 1, blocks)
    has_prev = me > 0
    has_next = me < groups - 1

    barrier = pltpu.get_barrier_semaphore()

    def greet(d):
        pl.semaphore_signal(
            barrier, inc=1, device_id=(lax.rem(me + d, groups), hb), device_id_type=MESH
        )

    if groups <= 8:
        for d in range(1, groups):
            greet(d)
    else:
        pl.loop(1, groups)(greet)
    for other in (h_prev, h_next):
        pl.semaphore_signal(barrier, inc=1, device_id=(me, other), device_id_type=MESH)

    pairs = (
        (weight_h, weight), (offy_h, offy), (offs_h, offs), (xy_h, xy), (hs_h, hs), (count_h, count),
        (value_h, value), (avoid_h, avoid),
    )
    loads = [pltpu.make_async_copy(a, b, in_sem.at[i]) for i, (a, b) in enumerate(pairs)]
    for load in loads:
        load.start()
    for load in loads[:6]:
        load.wait()

    owners = lax.broadcasted_iota(jnp.int32, (groups, groups), 0)
    lanes = lax.broadcasted_iota(jnp.int32, (groups, groups), 1)
    live = jnp.sum(
        jnp.where(owners == lanes, jnp.broadcast_to(count[...], (groups, groups)), 0).astype(jnp.float32),
        axis=1, keepdims=True,
    )
    slot = lax.broadcasted_iota(jnp.int32, (groups, slots), 1).astype(jnp.float32)
    w = jnp.where(slot < live, weight[...], 0.0)
    oy = offy[...]
    os = offs[...]
    state = hs[...]
    head = lax.div(state, speeds)
    pay[:, 0, :] = w * (1.0 - oy)
    pay[:, 1, :] = w * oy
    pay[:, 2, :] = 1.0 - os
    pay[:, 3, :] = os
    pay[:, 4, :] = (head * (cells * lines) + xy[...]).astype(jnp.float32)
    pay[:, 5, :] = (state - head * speeds).astype(jnp.float32)
    pay[:, 6, :] = jnp.zeros((groups, slots), jnp.float32)
    pay[:, 7, :] = jnp.zeros((groups, slots), jnp.float32)

    loads[6].wait()
    pl.semaphore_wait(barrier, groups - 1 + 2)

    def h_copy(side):
        return pltpu.make_async_remote_copy(
            value.at[0 if side == 0 else heads - 1], hhalo.at[1 - side],
            h_send.at[side], h_recv.at[1 - side],
            device_id=(me, h_prev if side == 0 else h_next), device_id_type=MESH,
        )

    def x_copy(side):
        return pltpu.make_async_remote_copy(
            value.at[:, 0 if side == 0 else cells - 1], xhalo.at[1 - side],
            x_send.at[side], x_recv.at[1 - side],
            device_id=(me - 1 if side == 0 else me + 1, hb), device_id_type=MESH,
        )

    def pay_copy(d):
        peer = lax.rem(me + d, groups)
        return pltpu.make_async_remote_copy(
            pay.at[peer], got.at[d], pay_send.at[d], pay_recv.at[d],
            device_id=(peer, hb), device_id_type=MESH,
        )

    for side in range(2):
        h_copy(side).start()
    for side, has in ((0, has_prev), (1, has_next)):
        @pl.when(has)
        def _():
            x_copy(side).start()

    if groups <= 8:
        for d in range(groups - 1, 0, -1):
            pay_copy(d).start()
    else:
        pl.loop(1, groups)(lambda d: pay_copy(d).start())
    mine = pltpu.make_async_copy(pay.at[me], got.at[0], self_sem)
    mine.start()
    loads[7].wait()

    for side, has in ((0, has_prev), (1, has_next)):
        @pl.when(jnp.logical_not(has))
        def _():
            xhalo[side] = value[:, 0 if side == 0 else cells - 1]

    total = heads * blocks
    angles = [np.float32(2.0 * math.pi / total) * np.float32(k) for k in range(total)]
    cosines = [float(np.cos(a)) for a in angles]
    sines = [float(np.sin(a)) for a in angles]
    speed = SLOWEST + SPEED_RANGE * lax.broadcasted_iota(jnp.int32, (1, speeds), 1).astype(
        jnp.float32
    ) / (speeds - 1)
    cx = [pick(cosines, hb * heads + h) * speed for h in range(heads)]
    cy = [pick(sines, hb * heads + h) * speed for h in range(heads)]
    grid = [(h, x) for h in range(heads) for x in range(cells)]
    v = {(h, x): value[h, x] for h, x in grid}
    part, s_slope = {}, {}
    for h, x in grid:
        here = v[h, x]
        up, down = upper(here, 0), lower(here, 0)
        term = cy[h] * (up - down) * 0.5 - (up - 2.0 * here + down) * 0.5
        up, down = upper(here, 1), lower(here, 1)
        slope = 0.5 * (up - down)
        size = smooth_abs(slope)
        s_slope[h, x] = slope / size
        part[h, x] = term + ACCELERATION * size - ACCELERATION * 0.5 * (up - 2.0 * here + down)

    for side in range(2):
        h_copy(side).wait_recv()
    for side, has in ((0, has_prev), (1, has_next)):
        @pl.when(has)
        def _():
            x_copy(1 - side).wait_recv()
    for x in range(cells):
        v[-1, x] = hhalo[0, x]
        v[heads, x] = hhalo[1, x]
    for h in range(heads):
        v[h, -1] = xhalo[0, h]
        v[h, cells] = xhalo[1, h]

    share, h_slope, above = {}, {}, {}
    for h, x in grid:
        here = v[h, x]
        up, down = v[h + 1, x], v[h - 1, x]
        slope = 0.5 * (up - down)
        size = smooth_abs(slope)
        h_slope[h, x] = slope / size
        turning = TURN_RATE * size - TURN_RATE * 0.5 * (up - 2.0 * here + down)
        up, down = v[h, x + 1], v[h, x - 1]
        across = cx[h] * (up - down) * 0.5 - (up - 2.0 * here + down) * 0.5
        relaxed = here - TIME_STEP * (across + part[h, x] + turning)
        floor = avoid[h, x]
        excess = SHARPNESS * (relaxed - floor)
        small = jnp.exp(-jnp.abs(excess))
        share[h, x] = jnp.where(excess >= 0.0, 1.0, small) / (1.0 + small)
        above[h, x] = (excess, small)

    rows = heads * cells * lines
    row_id = lax.broadcasted_iota(jnp.int32, (rows, slots), 0).astype(jnp.float32)
    speed_id = lax.broadcasted_iota(jnp.int32, (speeds, slots), 0).astype(jnp.float32)

    def operands(d):
        one = got[d]
        cell = jnp.broadcast_to(one[4:5], (rows, slots))
        left = jnp.where(row_id == cell, one[0:1], jnp.where(row_id == cell + 1.0, one[1:2], 0.0))
        cell = jnp.broadcast_to(one[5:6], (speeds, slots))
        right = jnp.where(
            speed_id == cell, one[2:3], jnp.where(speed_id == cell + 1.0, one[3:4], 0.0)
        )
        return left, right

    def product(left, right):
        return lax.dot_general(
            left, right, (((1,), (1,)), ((), ())),
            precision=lax.Precision.HIGHEST, preferred_element_type=jnp.float32,
        )

    mine.wait()
    if groups <= 8:
        for d in range(1, groups):
            pay_copy(d).wait_recv()
        both = [operands(d) for d in range(groups)]
        deposit = product(
            jnp.concatenate([b[0] for b in both], 1), jnp.concatenate([b[1] for b in both], 1)
        )
    else:
        pl.loop(1, groups)(lambda d: pay_copy(d).wait_recv())
        deposit = lax.fori_loop(
            0, groups, lambda d, so_far: so_far + product(*operands(d)),
            jnp.zeros((rows, speeds), jnp.float32),
        )

    c, adj = {}, {}
    for n, (h, x) in enumerate(grid):
        adjoint = deposit[n * lines : (n + 1) * lines]
        c[h, x] = adjoint * share[h, x]
        carried[h, x] = c[h, x]
        adj[h, x] = adjoint
    def cx_copy(side):
        return pltpu.make_async_remote_copy(
            carried.at[:, 0 if side == 0 else cells - 1], cxhalo.at[1 - side],
            cx_send.at[side], cx_recv.at[1 - side],
            device_id=(me - 1 if side == 0 else me + 1, hb), device_id_type=MESH,
        )

    for side, has in ((0, has_prev), (1, has_next)):
        @pl.when(has)
        def _():
            cx_copy(side).start()

        @pl.when(jnp.logical_not(has))
        def _():
            cxhalo[side] = jnp.zeros_like(cxhalo[side])
    ahead, back = {}, {}
    for h, x in grid:
        pull = (0.5 * TURN_RATE) * c[h, x] * h_slope[h, x]
        keep = (0.5 * TURN_RATE) * c[h, x]
        ahead[h, x] = pull - keep
        back[h, x] = -pull - keep
    for x in range(cells):
        turned[0, x] = back[0, x]
        turned[1, x] = ahead[heads - 1, x]

    def ch_copy(side):
        return pltpu.make_async_remote_copy(
            turned.at[side], chhalo.at[1 - side], ch_send.at[side], ch_recv.at[1 - side],
            device_id=(me, h_prev if side == 0 else h_next), device_id_type=MESH,
        )

    for side in range(2):
        ch_copy(side).start()

    local = {}
    for h, x in grid:
        excess, small = above[h, x]
        next_o[h, x] = avoid[h, x] + (jnp.maximum(excess, 0.0) + jnp.log1p(small)) / SHARPNESS
        agrad_o[h, x] = adj[h, x] * (jnp.where(excess >= 0.0, small, 1.0) / (1.0 + small))
        here = c[h, x]
        grad = spread((0.5 * cy[h] - 0.5) * here, (-0.5 * cy[h] - 0.5) * here, 0)
        pull = (0.5 * ACCELERATION) * here * s_slope[h, x]
        keep = (0.5 * ACCELERATION) * here
        grad = grad + spread(pull - keep, -pull - keep, 1)
        local[h, x] = grad + (2.0 + TURN_RATE + ACCELERATION) * here

    for side in range(2):
        ch_copy(side).wait_recv()
    for side, has in ((0, has_prev), (1, has_next)):
        @pl.when(has)
        def _():
            cx_copy(1 - side).wait_recv()
    for h, x in grid:
        grad = local[h, x]
        grad = grad + (ahead[h - 1, x] if h > 0 else chhalo[0, x])
        grad = grad + (back[h + 1, x] if h < heads - 1 else chhalo[1, x])
        low, high = 0.5 * cx[h] - 0.5, -0.5 * cx[h] - 0.5
        if x > 0:
            grad = grad + low * c[h, x - 1]
        else:
            grad = grad + jnp.where(has_prev, low * cxhalo[0, h], high * c[h, x])
        if x < cells - 1:
            grad = grad + high * c[h, x + 1]
        else:
            grad = grad + jnp.where(has_next, high * cxhalo[1, h], low * c[h, x])
        vgrad_o[h, x] = c[h, x] - TIME_STEP * grad

    for side in range(2):
        h_copy(side).wait_send()
        ch_copy(side).wait_send()
    for side, has in ((0, has_prev), (1, has_next)):
        @pl.when(has)
        def _():
            x_copy(side).wait_send()
            cx_copy(side).wait_send()
    if groups <= 8:
        for d in range(1, groups):
            pay_copy(d).wait_send()
    else:
        pl.loop(1, groups)(lambda d: pay_copy(d).wait_send())


def near_kernel(
    groups, blocks,
    value_h, avoid_h, weight_h, offy_h, offs_h, xy_h, hs_h, count_h,
    next_o, vgrad_o, agrad_o,
    fields, sample, cell, count, pay, got, packed, corner, halo,
    in_sem, pay_send, pay_recv, halo_send, halo_recv, row_in, late, late_near,
):
    _, heads, cells, lines, speeds = fields.shape
    value, avoid = fields.at[0], fields.at[1]
    slots = sample.shape[2]
    me = lax.axis_index("gx")
    hb = lax.axis_index("ha")
    h_next = lax.rem(hb + 1, blocks)
    h_prev = lax.rem(hb + blocks - 1, blocks)
    h_side = (h_prev, h_next)
    has_prev = me > 0
    has_next = me < groups - 1
    base = 2
    in_base = me < base

    is_even = lax.rem(hb, 2) == 0
    upper_pair = hb >= blocks // 2
    mate_side = 1 - lax.rem(hb, 2)
    far_side = 1 - mate_side
    mate, far = (lax.rem(hb + blocks - 1 + 2 * s, blocks) for s in (mate_side, far_side))
    level = lax.div(me + 1, 2)
    mate_before = jnp.where(is_even, jnp.minimum(2 * level + 1, groups), jnp.maximum(2 * level - 1, base))
    far_before = jnp.where(
        upper_pair,
        jnp.minimum(2 * level + jnp.where(is_even, 3, 1), groups),
        jnp.maximum(2 * level - jnp.where(is_even, 1, 3), base),
    )
    earlier = me + mate_before + far_before

    def near_rows(before):
        return jnp.clip(me - 1, base, before), jnp.clip(me + 2, base, before)

    mate_near, far_near = near_rows(mate_before), near_rows(far_before)
    around = jnp.minimum(me + 2, groups) - jnp.maximum(me - 1, base)
    near_later = jnp.where(has_next, 1, 0) + 2 * around
    for low, high in (mate_near, far_near):
        near_later = near_later - (high - low)

    barrier = pltpu.get_barrier_semaphore()

    def signal(sem, j, h):
        pl.semaphore_signal(sem, inc=1, device_id=(j, h), device_id_type=MESH)

    def rows(lo, hi, body):
        lax.fori_loop(lo, hi, lambda j, carry: (body(j), carry)[1], 0)

    def signal_at(sem, h):
        return lambda j: signal(sem, j, h)

    def wait_some(sem, n):
        @pl.when(n > 0)
        def _():
            pl.semaphore_wait(sem, n)

    @pl.when(in_base)
    def _():
        for j in range(groups - 1, base - 1, -1):
            for h in (far, mate, hb):
                signal(barrier, j, h)

    @pl.when(jnp.logical_not(in_base))
    def _():
        for before, h in ((far_before, far), (mate_before, mate), (me + 1, hb)):
            rows(before, groups, lambda j: signal(barrier, groups - 1 + before - j, h))
        for j in range(base):
            for h in (far, mate, hb):
                signal(barrier, j, h)

    loads = [
        pltpu.make_async_copy(a, b, in_sem.at[i])
        for a, b, i in (
            (weight_h, sample.at[0], 0), (offy_h, sample.at[1], 0), (offs_h, sample.at[2], 0),
            (xy_h, cell.at[0], 0), (hs_h, cell.at[1], 0), (count_h, count, 1),
            (value_h, value, 2), (avoid_h, avoid, 2),
        )
    ]
    for load in loads:
        load.start()
    loaded = [pltpu.make_async_copy(r, r, in_sem.at[i]) for r, i in ((sample, 0), (count, 1), (fields, 2))]

    pay[0] = jnp.zeros(pay.shape[1:], jnp.float32)
    pay[groups + 1] = jnp.zeros(pay.shape[1:], jnp.float32)

    def copy(src, dst, send_sem, recv_sem, j, h):
        return pltpu.make_async_remote_copy(
            src, dst, send_sem, recv_sem, device_id=(j, h), device_id_type=MESH
        )

    def x_slot(side):
        return 6 + side * 5

    def h_halo(side, h):
        dst = halo.at[pl.ds(3 * (1 - side), 3)]
        copy(packed.at[side], dst, halo_send, halo_recv, me, h).start()

    def x_halo(side):
        at = x_slot(1 - side)
        copy(packed.at[2 + side], halo.at[at : at + 3], halo_send, halo_recv, me - 1 + 2 * side, hb).start()

    def corner_halo(side, h_to, h):
        at = x_slot(1 - side) + 4 - h_to
        copy(corner.at[side, h_to], halo.at[at], halo_send, halo_recv, me - 1 + 2 * side, h).start()

    def turn_of(j):
        turn = lax.rem(me - j - 1 + 2 * groups, groups)
        return 5 * turn, jnp.where(turn < groups - 1, lax.div(turn, 2), groups // 2)

    def send_side(j, side, h):
        at, sem = turn_of(j)
        copy(pay.at[j + 1], got.at[at + 4 - side], pay_send, pay_recv.at[sem], j, h).start()

    def send_own(j):
        at, sem = turn_of(j)
        copy(pay.at[pl.ds(j, 3)], got.at[pl.ds(at, 3)], pay_send, pay_recv.at[sem], j, hb).start()

    def send_mate(j):
        send_side(j, mate_side, mate)

    def send_far(j):
        send_side(j, far_side, far)

    def send_all(j):
        send_own(j)
        send_mate(j)
        send_far(j)

    loaded[0].wait()
    loaded[1].wait()
    owners = lax.broadcasted_iota(jnp.int32, (groups, groups), 0)
    lanes = lax.broadcasted_iota(jnp.int32, (groups, groups), 1)
    live = jnp.sum(
        jnp.where(owners == lanes, jnp.broadcast_to(count[...], (groups, groups)), 0).astype(jnp.float32),
        axis=1, keepdims=True,
    )
    slot = lax.broadcasted_iota(jnp.int32, (groups, slots), 1).astype(jnp.float32)
    w = jnp.where(slot < live, sample[0], 0.0)
    oy = sample[1]
    state = cell[1]
    head = lax.div(state, speeds)
    row = head * (cells * lines) + cell[0]
    pay[1 : groups + 1, 0, :] = w * (1.0 - oy)
    pay[1 : groups + 1, 1, :] = w * oy
    pay[1 : groups + 1, 2, :] = sample[2]
    pay[1 : groups + 1, 3, :] = (row * speeds + (state - head * speeds)).astype(jnp.float32)
    own_at = 5 * (groups - 1)
    pltpu.make_async_copy(
        pay.at[pl.ds(me, 3)], got.at[own_at : own_at + 3], pay_recv.at[groups // 2]
    ).start()
    loaded[2].wait()
    grid = [(h, x) for h in range(heads) for x in range(cells)]
    plane = {(i, h, x): fields[i, h, x] for i in range(2) for h, x in grid}
    whole = jnp.concatenate([plane[0, h, x] for h, x in grid], 1)
    mid = lines // 2
    for side, edge in ((0, 0), (1, 1)):
        h_edge, x_edge = edge * (heads - 1), edge * (cells - 1)
        over_h = [plane[1, h_edge, x] for x in range(cells)]
        over_x = [plane[1, h, x_edge] for h in range(heads)]
        h_tile = [p[:mid] for p in over_h] + [p[mid:] for p in over_h]
        x_tile = [q for p in over_x for q in (p[:mid], p[mid:])]
        for to, tile in ((side, h_tile), (2 + side, x_tile)):
            packed[to, 0] = whole[:mid]
            packed[to, 1] = whole[mid:]
            packed[to, 2] = jnp.concatenate(tile, 1)
        for h in range(2):
            p = plane[0, h * (heads - 1), x_edge]
            corner[side, h] = jnp.concatenate([p[:mid], p[mid:]] * 2, 1)

    @pl.when(jnp.logical_not(in_base))
    def _():
        pl.semaphore_wait(barrier, earlier)
        @pl.when(me == base)
        def _():
            for j in range(base):
                signal(row_in, j, hb)

        rows(base, me - 1, signal_at(late, hb))
        for (low, high), before, h in ((mate_near, mate_before, mate), (far_near, far_before, far)):
            rows(base, low, signal_at(late, h))
            rows(high, before, signal_at(late, h))
        for j in range(base):
            send_all(j)
        rows(jnp.maximum(me - 1, base), me, signal_at(late_near, hb))
        rows(*mate_near, signal_at(late_near, mate))
        rows(*far_near, signal_at(late_near, far))

        x_halo(0)
        others = ((mate_before, mate_side, mate), (far_before, far_side, far))

        def near_halos(comes):
            for before, side, h in others:
                pl.when(comes(me - 1, before))(functools.partial(corner_halo, 0, side, h))
                pl.when(comes(me, before))(functools.partial(h_halo, side, h))
                pl.when(comes(me + 1, before) & has_next)(functools.partial(corner_halo, 1, side, h))

        near_halos(lambda j, before: j < before)
        rows(base, me, send_own)
        rows(base, mate_before, send_mate)
        rows(base, far_before, send_far)

        wait_some(late_near, near_later)
        pl.when(has_next)(functools.partial(x_halo, 1))
        near_halos(lambda j, before: j >= before)
        wait_some(late, 3 * groups - 1 - earlier - near_later)
        for before, to in ((me + 1, send_own), (mate_before, send_mate), (far_before, send_far)):
            rows(before, groups, lambda j: to(groups - 1 + before - j))

    def x_and_corners(side):
        x_halo(side)
        for h in range(2):
            corner_halo(side, h, h_side[h])

    @pl.when(in_base)
    def _():
        pl.semaphore_wait(row_in, 1)
        for side in range(2):
            h_halo(side, h_side[side])
            send_side(me, side, h_side[side])
        for row in range(base):
            @pl.when(me == row)
            def _():
                x_and_corners(1 - row)
                send_all(1 - row)
        pl.semaphore_wait(barrier, 3 * (groups - base))
        pl.when(me == base - 1)(functools.partial(x_and_corners, 1))
        rows(base, groups, lambda j: send_all(groups - 1 + base - j))

    width = heads * cells * speeds
    half, quarter = width // 2, width // 4
    lane = lax.broadcasted_iota(jnp.int32, (1, width), 1)
    place = lax.div(lane, quarter)
    within = lax.rem(lane, quarter)
    even = lax.rem(place, 2) == 0
    left_half = place < 2
    total = heads * blocks
    angles = [np.float32(2.0 * math.pi / total) * np.float32(k) for k in range(total)]
    cosines = [float(np.cos(a)) for a in angles]
    sines = [float(np.sin(a)) for a in angles]
    speed = SLOWEST + SPEED_RANGE * within.astype(jnp.float32) / (speeds - 1)
    turn = [lax.rem(hb * heads + h + total, total) for h in range(-1, heads + 1)]
    cos_of = [pick(cosines, t) for t in turn]
    sin_of = [pick(sines, t) for t in turn]
    cx_own, cy_own = (jnp.where(left_half, a[1], a[2]) * speed for a in (cos_of, sin_of))
    cx_out, cy_out = (jnp.where(left_half, a[0], a[3]) * speed for a in (cos_of, sin_of))

    def shift(a, by):
        return pltpu.roll(a, by % width, 1)

    def forward(here, floor, cx, cy, h_up, h_down, x_up, x_down):
        up, down = upper(here, 0), lower(here, 0)
        rate = cy * (up - down) * 0.5 - (up - 2.0 * here + down) * 0.5
        up = jnp.where(within == quarter - 1, here, shift(here, -1))
        down = jnp.where(within == 0, here, shift(here, 1))
        slope = 0.5 * (up - down)
        size = smooth_abs(slope)
        s_slope = slope / size
        rate = rate + ACCELERATION * size - ACCELERATION * 0.5 * (up - 2.0 * here + down)
        slope = 0.5 * (h_up - h_down)
        size = smooth_abs(slope)
        h_slope = slope / size
        rate = rate + TURN_RATE * size - TURN_RATE * 0.5 * (h_up - 2.0 * here + h_down)
        rate = rate + cx * (x_up - x_down) * 0.5 - (x_up - 2.0 * here + x_down) * 0.5
        excess = SHARPNESS * (here - TIME_STEP * rate - floor)
        small = jnp.exp(-jnp.abs(excess))
        share = jnp.where(excess >= 0.0, 1.0, small) / (1.0 + small)
        pull = (0.5 * TURN_RATE) * share * h_slope
        keep = (0.5 * TURN_RATE) * share
        return excess, small, share, s_slope, pull - keep, -pull - keep

    def all_halos(sending):
        def wait(n):
            view = halo.at[0:n]
            c = copy(view, view, halo_send, halo_recv, me, h_next)
            c.wait_send() if sending else c.wait_recv()

        @pl.when(has_prev & has_next)
        def _():
            wait(16)

        @pl.when(jnp.logical_not(has_prev & has_next))
        def _():
            wait(11)

    def unpack(a):
        return {(h, x): a[:, n * speeds : (n + 1) * speeds] for n, (h, x) in enumerate(grid)}

    all_halos(False)
    def tall_pair(top, bottom):
        return jnp.concatenate([top, bottom], 0)

    own = whole
    floor = jnp.concatenate([plane[1, h, x] for h, x in grid], 1)
    hp, hn, xp, xn = (tall_pair(halo[i], halo[i + 1]) for i in (0, 3, 6, 11))
    hp_floor, hn_floor, xp_floor, xn_floor = (halo[i] for i in (2, 5, 8, 13))
    on_even, on_odd = [], []
    for i in (9, 10, 14, 15):
        tile = halo[i]
        other = shift(tile, quarter)
        on_even.append(tall_pair(tile, other))
        on_odd.append(tall_pair(other, tile))
    edge_h = shift(jnp.where(left_half, hn, hp), half)
    edge_x = jnp.where(even, shift(xp, -quarter), shift(xn, quarter))
    up_x = jnp.where(even, shift(own, -quarter), jnp.where(has_next, edge_x, own))
    down_x = jnp.where(even, jnp.where(has_prev, edge_x, own), shift(own, quarter))
    excess, small, share, s_slope, ahead, back = forward(
        own, floor, cx_own, cy_own,
        shift(jnp.where(left_half, hn, own), half), shift(jnp.where(left_half, own, hp), half),
        up_x, down_x,
    )
    next_v = unpack(floor + (jnp.maximum(excess, 0.0) + jnp.log1p(small)) / SHARPNESS)
    for h, x in grid:
        next_o[h, x] = next_v[h, x]
    rest = unpack(jnp.where(excess >= 0.0, small, 1.0) / (1.0 + small))
    share, s_slope, ahead, back = (unpack(a) for a in (share, s_slope, ahead, back))

    up_x = jnp.where(even, shift(edge_h, -quarter), jnp.where(left_half, on_odd[2], on_odd[3]))
    down_x = jnp.where(even, jnp.where(left_half, on_even[0], on_even[1]), shift(edge_h, quarter))
    edge_floor = tall_pair(
        jnp.where(left_half, hp_floor, shift(hn_floor, half)),
        jnp.where(left_half, shift(hp_floor, half), hn_floor),
    )
    out = forward(
        edge_h, edge_floor, cx_out, cy_out,
        jnp.where(left_half, own, hn), jnp.where(left_half, hp, own),
        jnp.where(even | has_next, up_x, edge_h), jnp.where(even & jnp.logical_not(has_prev), edge_h, down_x),
    )
    out = unpack(jnp.where(left_half, out[4], out[5]))
    for x in range(cells):
        ahead[-1, x], back[heads, x] = out[0, x], out[1, x]

    turned = shift(edge_x, half)
    up_h = jnp.where(left_half, turned, jnp.where(even, on_even[1], on_odd[3]))
    down_h = jnp.where(left_half, jnp.where(even, on_even[0], on_odd[2]), turned)
    edge_floor = tall_pair(
        jnp.where(even, xp_floor, shift(xn_floor, quarter)),
        jnp.where(even, shift(xp_floor, -quarter), xn_floor),
    )
    out = forward(
        edge_x, edge_floor, cx_own, cy_own,
        up_h, down_h, jnp.where(even, own, xn), jnp.where(even, xp, own),
    )
    out = unpack(out[2])
    for h in range(heads):
        share[h, -1], share[h, cells] = out[h, 0], out[h, 1]
    speed = SLOWEST + SPEED_RANGE * lax.broadcasted_iota(jnp.int32, (1, speeds), 1).astype(
        jnp.float32
    ) / (speeds - 1)
    cx = [cos_of[h + 1] * speed for h in range(heads)]
    cy = [sin_of[h + 1] * speed for h in range(heads)]

    span = cells * lines
    inside = lax.broadcasted_iota(jnp.int32, (heads * span, slots), 0)
    edge = lax.broadcasted_iota(jnp.int32, (heads * lines, slots), 0)
    edge = lax.div(edge, lines) * span + lax.rem(edge, lines)
    side_rows = lax.broadcasted_iota(jnp.int32, (span, slots), 0)
    ids = [
        i.astype(jnp.float32).astype(jnp.bfloat16)
        for i in (edge + (cells - 1) * lines, inside, edge, side_rows + (heads - 1) * span, side_rows)
    ]
    speed_id = lax.broadcasted_iota(jnp.int32, (speeds, slots), 0).astype(jnp.float32)
    speed_id = speed_id.astype(jnp.bfloat16)

    def tall(row, n):
        part = jnp.broadcast_to(row, (16, slots)).astype(jnp.bfloat16)
        return jnp.concatenate([part] * (n // 16), 0)

    def deposit(one, row_id):
        n = row_id.shape[0]
        weight0, weight1, up_s, code = one[0:1], one[1:2], one[2:3], one[3:4]
        row = jnp.floor(code * (1.0 / speeds))
        cell = code - row * speeds
        here, above_it = row_id == tall(row, n), row_id == tall(row + 1.0, n)
        zero = jnp.zeros(row_id.shape, jnp.bfloat16)
        high, low = [], []
        for f in (1.0 - up_s, up_s):
            a, b = weight0 * f, weight1 * f
            for part in (high, low):
                part.append(jnp.where(here, tall(a, n), jnp.where(above_it, tall(b, n), zero)))
                a, b = (t - t.astype(jnp.bfloat16).astype(jnp.float32) for t in (a, b))
        left = jnp.concatenate([jnp.concatenate(part, 1) for part in (high, low)], 0)
        one_hot = jnp.ones(speed_id.shape, jnp.bfloat16)
        right = jnp.concatenate(
            [
                jnp.where(speed_id == tall(c, speeds), one_hot, jnp.zeros_like(one_hot))
                for c in (cell, cell + 1.0)
            ],
            1,
        )
        both = lax.dot_general(
            left, right, (((1,), (1,)), ((), ())), preferred_element_type=jnp.float32
        )
        return both[:n] + both[n:]

    def collect(at, count, sem, sums):
        view = got.at[pl.ds(at, count)]
        copy(view, view, pay_send, pay_recv.at[sem], me, h_next).wait_recv()
        sums = list(sums)
        for i in range(count):
            sums[i % 5] = sums[i % 5] + deposit(got[at + i], ids[i % 5])
        return tuple(sums)

    sums = tuple(jnp.zeros((i.shape[0], speeds), jnp.float32) for i in ids)
    sums = lax.fori_loop(0, groups // 2 - 1, lambda n, so_far: collect(10 * n, 10, n, so_far), sums)
    sums = collect(own_at, 5, groups // 2, sums)
    sums = collect(own_at - 5, 5, groups // 2 - 1, sums)

    adj, c = {}, {}
    for n, (h, x) in enumerate(grid):
        adj[h, x] = sums[1][n * lines : (n + 1) * lines]
        c[h, x] = adj[h, x] * share[h, x]
    for h in range(heads):
        c[h, -1] = sums[0][h * lines : (h + 1) * lines] * share[h, -1]
        c[h, cells] = sums[2][h * lines : (h + 1) * lines] * share[h, cells]
    for x in range(cells):
        adj[-1, x] = sums[3][x * lines : (x + 1) * lines]
        adj[heads, x] = sums[4][x * lines : (x + 1) * lines]

    for h, x in grid:
        agrad_o[h, x] = adj[h, x] * rest[h, x]
        here = c[h, x]
        grad = spread((0.5 * cy[h] - 0.5) * here, (-0.5 * cy[h] - 0.5) * here, 0)
        pull = (0.5 * ACCELERATION) * here * s_slope[h, x]
        keep = (0.5 * ACCELERATION) * here
        grad = grad + spread(pull - keep, -pull - keep, 1)
        grad = grad + (2.0 + TURN_RATE + ACCELERATION) * here
        grad = grad + adj[h - 1, x] * ahead[h - 1, x] + adj[h + 1, x] * back[h + 1, x]
        low, high = 0.5 * cx[h] - 0.5, -0.5 * cx[h] - 0.5
        if x > 0:
            grad = grad + low * c[h, x - 1]
        else:
            grad = grad + jnp.where(has_prev, low * c[h, -1], high * here)
        if x < cells - 1:
            grad = grad + high * c[h, x + 1]
        else:
            grad = grad + jnp.where(has_next, high * c[h, cells], low * here)
        vgrad_o[h, x] = here - TIME_STEP * grad

    all_halos(True)
    view = got.at[0 : 5 * groups - 3]
    copy(view, view, pay_send, pay_recv.at[0], me, h_next).wait_send()


def write_out(next_v, vgrad_v, agrad_v, next_o, vgrad_o, agrad_o, sem):
    copies = [
        pltpu.make_async_copy(a, b, sem.at[i])
        for i, (a, b) in enumerate(((next_v, next_o), (vgrad_v, vgrad_o), (agrad_v, agrad_o)))
    ]
    for copy in copies:
        copy.start()
    for copy in copies:
        copy.wait()


def on_device(groups, blocks, value, avoid, weight, offy, offs, xy, hs, count):
    slots = weight.shape[3]
    value = jnp.transpose(value, (0, 2, 3, 1))
    avoid = jnp.transpose(avoid, (0, 2, 3, 1))
    weight, offy, offs, xy, hs = (a.reshape(groups, slots) for a in (weight, offy, offs, xy, hs))
    count = count.reshape(1, groups)
    heads, cells, lines, speeds = value.shape
    f32 = jnp.float32
    dma = pltpu.SemaphoreType.DMA
    field = pltpu.VMEM(value.shape, f32)
    x_pair = pltpu.VMEM((2, heads, lines, speeds), f32)
    h_pair = pltpu.VMEM((2, cells, lines, speeds), f32)
    near = groups in (4, 8) and blocks == 4 and heads == cells == 2 and 4 * speeds == slots == 128 and lines == 16
    sample = pltpu.VMEM((groups, slots), f32)
    index = pltpu.VMEM((groups, slots), jnp.int32)
    counts = pltpu.VMEM((1, groups), jnp.int32)
    if near:
        scratch = [
            pltpu.VMEM((2, *value.shape), f32),
            pltpu.VMEM((5, groups, slots), f32), pltpu.VMEM((2, groups, slots), jnp.int32), counts,
            pltpu.VMEM((groups + 2, 4, slots), f32), pltpu.VMEM((5 * groups, 4, slots), f32),
            pltpu.VMEM((4, 3, lines // 2, slots), f32), pltpu.VMEM((2, 2, lines // 2, slots), f32),
            pltpu.VMEM((16, lines // 2, slots), f32),
            dma((3,)), dma, dma((groups // 2 + 1,)), dma, dma,
            *[pltpu.SemaphoreType.REGULAR] * 3,
        ]
    else:
        scratch = [
            field, field, sample, sample, sample, index, index, counts,
            pltpu.VMEM((groups, ROWS, slots), f32), pltpu.VMEM((groups, ROWS, slots), f32),
            x_pair, h_pair, field, h_pair, x_pair, h_pair,
            dma((8,)), dma((groups,)), dma((groups,)), *[dma((2,))] * 8, dma,
        ]
    outs = pl.pallas_call(
        functools.partial(near_kernel if near else kernel, groups, blocks),
        out_shape=[pltpu.VMEM(value.shape, f32)] * 3,
        in_specs=[pl.BlockSpec(memory_space=pltpu.HBM)] * 8,
        out_specs=[pl.BlockSpec(memory_space=pltpu.VMEM)] * 3,
        scratch_shapes=scratch,
        compiler_params=pltpu.CompilerParams(collective_id=0, has_side_effects=True),
        name="step",
    )(value, avoid, weight, offy, offs, xy, hs, count)
    outs = pl.pallas_call(
        write_out,
        out_shape=[jax.ShapeDtypeStruct(value.shape, f32)] * 3,
        in_specs=[pl.BlockSpec(memory_space=pl.ANY)] * 3,
        out_specs=[pl.BlockSpec(memory_space=pl.ANY)] * 3,
        scratch_shapes=[dma((3,))],
        compiler_params=pltpu.CompilerParams(vmem_limit_bytes=1 << 20),
        name="write_out",
    )(*outs)
    return tuple(jnp.transpose(o, (0, 3, 1, 2)) for o in outs)


def solution(mesh):
    field = P("ha", None, "gx", None)
    sample = P("gx", "ha", None, None)
    return jax.shard_map(
        functools.partial(on_device, mesh.shape["gx"], mesh.shape["ha"]),
        mesh=mesh,
        in_specs=(field, field, sample, sample, sample, sample, sample, P("gx", "ha", None)),
        out_specs=(field, field, field),
        check_vma=False,
    )
```

```python
import functools
import math

import jax
import jax.numpy as jnp
import numpy as np
from jax import lax
from jax.experimental import pallas as pl
from jax.experimental.pallas import tpu as pltpu
from jax.sharding import PartitionSpec as P

TIME_STEP = 0.3
SHARPNESS = 2.0
SOFTENING = 0.1
TURN_RATE = 0.5
ACCELERATION = 0.3
SLOWEST = 0.2
SPEED_RANGE = 0.8
ROWS = 8
MESH = pl.DeviceIdType.MESH


def smooth_abs(slope):
    return jnp.sqrt(slope * slope + SOFTENING * SOFTENING)


def upper(plane, axis):
    n = plane.shape[axis]
    return jnp.concatenate(
        [lax.slice_in_dim(plane, 1, n, axis=axis), lax.slice_in_dim(plane, n - 1, n, axis=axis)], axis
    )


def lower(plane, axis):
    n = plane.shape[axis]
    return jnp.concatenate(
        [lax.slice_in_dim(plane, 0, 1, axis=axis), lax.slice_in_dim(plane, 0, n - 1, axis=axis)], axis
    )


def spread(up, down, axis):
    n = up.shape[axis]
    from_lower = jnp.concatenate(
        [lax.slice_in_dim(down, 0, 1, axis=axis), lax.slice_in_dim(up, 0, n - 1, axis=axis)], axis
    )
    from_upper = jnp.concatenate(
        [lax.slice_in_dim(down, 1, n, axis=axis), lax.slice_in_dim(up, n - 1, n, axis=axis)], axis
    )
    return from_lower + from_upper


def pick(table, index):
    chosen = jnp.float32(table[0])
    for i in range(1, len(table)):
        chosen = jnp.where(index == i, jnp.float32(table[i]), chosen)
    return chosen


def kernel(
    groups, blocks,
    value_h, avoid_h, weight_h, offy_h, offs_h, xy_h, hs_h, count_h,
    next_o, vgrad_o, agrad_o,
    value, avoid, weight, offy, offs, xy, hs, count,
    pay, got, xhalo, hhalo, carried, turned, cxhalo, chhalo,
    in_sem, pay_send, pay_recv, x_send, x_recv, h_send, h_recv,
    cx_send, cx_recv, ch_send, ch_recv, self_sem,
):
    heads, cells, lines, speeds = value.shape
    slots = weight.shape[1]
    me = lax.axis_index("gx")
    hb = lax.axis_index("ha")
    h_next = lax.rem(hb + 1, blocks)
    h_prev = lax.rem(hb + blocks - 1, blocks)
    has_prev = me > 0
    has_next = me < groups - 1

    barrier = pltpu.get_barrier_semaphore()

    def greet(d):
        pl.semaphore_signal(
            barrier, inc=1, device_id=(lax.rem(me + d, groups), hb), device_id_type=MESH
        )

    if groups <= 8:
        for d in range(1, groups):
            greet(d)
    else:
        pl.loop(1, groups)(greet)
    for other in (h_prev, h_next):
        pl.semaphore_signal(barrier, inc=1, device_id=(me, other), device_id_type=MESH)

    pairs = (
        (weight_h, weight), (offy_h, offy), (offs_h, offs), (xy_h, xy), (hs_h, hs), (count_h, count),
        (value_h, value), (avoid_h, avoid),
    )
    loads = [pltpu.make_async_copy(a, b, in_sem.at[i]) for i, (a, b) in enumerate(pairs)]
    for load in loads:
        load.start()
    for load in loads[:6]:
        load.wait()

    owners = lax.broadcasted_iota(jnp.int32, (groups, groups), 0)
    lanes = lax.broadcasted_iota(jnp.int32, (groups, groups), 1)
    live = jnp.sum(
        jnp.where(owners == lanes, jnp.broadcast_to(count[...], (groups, groups)), 0).astype(jnp.float32),
        axis=1, keepdims=True,
    )
    slot = lax.broadcasted_iota(jnp.int32, (groups, slots), 1).astype(jnp.float32)
    w = jnp.where(slot < live, weight[...], 0.0)
    oy = offy[...]
    os = offs[...]
    state = hs[...]
    head = lax.div(state, speeds)
    pay[:, 0, :] = w * (1.0 - oy)
    pay[:, 1, :] = w * oy
    pay[:, 2, :] = 1.0 - os
    pay[:, 3, :] = os
    pay[:, 4, :] = (head * (cells * lines) + xy[...]).astype(jnp.float32)
    pay[:, 5, :] = (state - head * speeds).astype(jnp.float32)
    pay[:, 6, :] = jnp.zeros((groups, slots), jnp.float32)
    pay[:, 7, :] = jnp.zeros((groups, slots), jnp.float32)

    loads[6].wait()
    pl.semaphore_wait(barrier, groups - 1 + 2)

    def h_copy(side):
        return pltpu.make_async_remote_copy(
            value.at[0 if side == 0 else heads - 1], hhalo.at[1 - side],
            h_send.at[side], h_recv.at[1 - side],
            device_id=(me, h_prev if side == 0 else h_next), device_id_type=MESH,
        )

    def x_copy(side):
        return pltpu.make_async_remote_copy(
            value.at[:, 0 if side == 0 else cells - 1], xhalo.at[1 - side],
            x_send.at[side], x_recv.at[1 - side],
            device_id=(me - 1 if side == 0 else me + 1, hb), device_id_type=MESH,
        )

    def pay_copy(d):
        peer = lax.rem(me + d, groups)
        return pltpu.make_async_remote_copy(
            pay.at[peer], got.at[d], pay_send.at[d], pay_recv.at[d],
            device_id=(peer, hb), device_id_type=MESH,
        )

    for side in range(2):
        h_copy(side).start()
    for side, has in ((0, has_prev), (1, has_next)):
        @pl.when(has)
        def _():
            x_copy(side).start()

    if groups <= 8:
        for d in range(groups - 1, 0, -1):
            pay_copy(d).start()
    else:
        pl.loop(1, groups)(lambda d: pay_copy(d).start())
    mine = pltpu.make_async_copy(pay.at[me], got.at[0], self_sem)
    mine.start()
    loads[7].wait()

    for side, has in ((0, has_prev), (1, has_next)):
        @pl.when(jnp.logical_not(has))
        def _():
            xhalo[side] = value[:, 0 if side == 0 else cells - 1]

    total = heads * blocks
    angles = [np.float32(2.0 * math.pi / total) * np.float32(k) for k in range(total)]
    cosines = [float(np.cos(a)) for a in angles]
    sines = [float(np.sin(a)) for a in angles]
    speed = SLOWEST + SPEED_RANGE * lax.broadcasted_iota(jnp.int32, (1, speeds), 1).astype(
        jnp.float32
    ) / (speeds - 1)
    cx = [pick(cosines, hb * heads + h) * speed for h in range(heads)]
    cy = [pick(sines, hb * heads + h) * speed for h in range(heads)]
    grid = [(h, x) for h in range(heads) for x in range(cells)]
    v = {(h, x): value[h, x] for h, x in grid}
    part, s_slope = {}, {}
    for h, x in grid:
        here = v[h, x]
        up, down = upper(here, 0), lower(here, 0)
        term = cy[h] * (up - down) * 0.5 - (up - 2.0 * here + down) * 0.5
        up, down = upper(here, 1), lower(here, 1)
        slope = 0.5 * (up - down)
        size = smooth_abs(slope)
        s_slope[h, x] = slope / size
        part[h, x] = term + ACCELERATION * size - ACCELERATION * 0.5 * (up - 2.0 * here + down)

    for side in range(2):
        h_copy(side).wait_recv()
    for side, has in ((0, has_prev), (1, has_next)):
        @pl.when(has)
        def _():
            x_copy(1 - side).wait_recv()
    for x in range(cells):
        v[-1, x] = hhalo[0, x]
        v[heads, x] = hhalo[1, x]
    for h in range(heads):
        v[h, -1] = xhalo[0, h]
        v[h, cells] = xhalo[1, h]

    share, h_slope, above = {}, {}, {}
    for h, x in grid:
        here = v[h, x]
        up, down = v[h + 1, x], v[h - 1, x]
        slope = 0.5 * (up - down)
        size = smooth_abs(slope)
        h_slope[h, x] = slope / size
        turning = TURN_RATE * size - TURN_RATE * 0.5 * (up - 2.0 * here + down)
        up, down = v[h, x + 1], v[h, x - 1]
        across = cx[h] * (up - down) * 0.5 - (up - 2.0 * here + down) * 0.5
        relaxed = here - TIME_STEP * (across + part[h, x] + turning)
        floor = avoid[h, x]
        excess = SHARPNESS * (relaxed - floor)
        small = jnp.exp(-jnp.abs(excess))
        share[h, x] = jnp.where(excess >= 0.0, 1.0, small) / (1.0 + small)
        above[h, x] = (excess, small)

    rows = heads * cells * lines
    row_id = lax.broadcasted_iota(jnp.int32, (rows, slots), 0).astype(jnp.float32)
    speed_id = lax.broadcasted_iota(jnp.int32, (speeds, slots), 0).astype(jnp.float32)

    def operands(d):
        one = got[d]
        cell = jnp.broadcast_to(one[4:5], (rows, slots))
        left = jnp.where(row_id == cell, one[0:1], jnp.where(row_id == cell + 1.0, one[1:2], 0.0))
        cell = jnp.broadcast_to(one[5:6], (speeds, slots))
        right = jnp.where(
            speed_id == cell, one[2:3], jnp.where(speed_id == cell + 1.0, one[3:4], 0.0)
        )
        return left, right

    def product(left, right):
        return lax.dot_general(
            left, right, (((1,), (1,)), ((), ())),
            precision=lax.Precision.HIGHEST, preferred_element_type=jnp.float32,
        )

    mine.wait()
    if groups <= 8:
        for d in range(1, groups):
            pay_copy(d).wait_recv()
        both = [operands(d) for d in range(groups)]
        deposit = product(
            jnp.concatenate([b[0] for b in both], 1), jnp.concatenate([b[1] for b in both], 1)
        )
    else:
        pl.loop(1, groups)(lambda d: pay_copy(d).wait_recv())
        deposit = lax.fori_loop(
            0, groups, lambda d, so_far: so_far + product(*operands(d)),
            jnp.zeros((rows, speeds), jnp.float32),
        )

    c, adj = {}, {}
    for n, (h, x) in enumerate(grid):
        adjoint = deposit[n * lines : (n + 1) * lines]
        c[h, x] = adjoint * share[h, x]
        carried[h, x] = c[h, x]
        adj[h, x] = adjoint
    def cx_copy(side):
        return pltpu.make_async_remote_copy(
            carried.at[:, 0 if side == 0 else cells - 1], cxhalo.at[1 - side],
            cx_send.at[side], cx_recv.at[1 - side],
            device_id=(me - 1 if side == 0 else me + 1, hb), device_id_type=MESH,
        )

    for side, has in ((0, has_prev), (1, has_next)):
        @pl.when(has)
        def _():
            cx_copy(side).start()

        @pl.when(jnp.logical_not(has))
        def _():
            cxhalo[side] = jnp.zeros_like(cxhalo[side])
    ahead, back = {}, {}
    for h, x in grid:
        pull = (0.5 * TURN_RATE) * c[h, x] * h_slope[h, x]
        keep = (0.5 * TURN_RATE) * c[h, x]
        ahead[h, x] = pull - keep
        back[h, x] = -pull - keep
    for x in range(cells):
        turned[0, x] = back[0, x]
        turned[1, x] = ahead[heads - 1, x]

    def ch_copy(side):
        return pltpu.make_async_remote_copy(
            turned.at[side], chhalo.at[1 - side], ch_send.at[side], ch_recv.at[1 - side],
            device_id=(me, h_prev if side == 0 else h_next), device_id_type=MESH,
        )

    for side in range(2):
        ch_copy(side).start()

    local = {}
    for h, x in grid:
        excess, small = above[h, x]
        next_o[h, x] = avoid[h, x] + (jnp.maximum(excess, 0.0) + jnp.log1p(small)) / SHARPNESS
        agrad_o[h, x] = adj[h, x] * (jnp.where(excess >= 0.0, small, 1.0) / (1.0 + small))
        here = c[h, x]
        grad = spread((0.5 * cy[h] - 0.5) * here, (-0.5 * cy[h] - 0.5) * here, 0)
        pull = (0.5 * ACCELERATION) * here * s_slope[h, x]
        keep = (0.5 * ACCELERATION) * here
        grad = grad + spread(pull - keep, -pull - keep, 1)
        local[h, x] = grad + (2.0 + TURN_RATE + ACCELERATION) * here

    for side in range(2):
        ch_copy(side).wait_recv()
    for side, has in ((0, has_prev), (1, has_next)):
        @pl.when(has)
        def _():
            cx_copy(1 - side).wait_recv()
    for h, x in grid:
        grad = local[h, x]
        grad = grad + (ahead[h - 1, x] if h > 0 else chhalo[0, x])
        grad = grad + (back[h + 1, x] if h < heads - 1 else chhalo[1, x])
        low, high = 0.5 * cx[h] - 0.5, -0.5 * cx[h] - 0.5
        if x > 0:
            grad = grad + low * c[h, x - 1]
        else:
            grad = grad + jnp.where(has_prev, low * cxhalo[0, h], high * c[h, x])
        if x < cells - 1:
            grad = grad + high * c[h, x + 1]
        else:
            grad = grad + jnp.where(has_next, high * cxhalo[1, h], low * c[h, x])
        vgrad_o[h, x] = c[h, x] - TIME_STEP * grad

    for side in range(2):
        h_copy(side).wait_send()
        ch_copy(side).wait_send()
    for side, has in ((0, has_prev), (1, has_next)):
        @pl.when(has)
        def _():
            x_copy(side).wait_send()
            cx_copy(side).wait_send()
    if groups <= 8:
        for d in range(1, groups):
            pay_copy(d).wait_send()
    else:
        pl.loop(1, groups)(lambda d: pay_copy(d).wait_send())


def near_kernel(
    groups, blocks,
    value_h, avoid_h, weight_h, offy_h, offs_h, xy_h, hs_h, count_h,
    next_o, vgrad_o, agrad_o,
    fields, sample, cell, count, pay, got, packed, corner, halo,
    in_sem, pay_send, pay_recv, halo_send, halo_recv, row_in, late, late_near,
):
    _, heads, cells, lines, speeds = fields.shape
    value, avoid = fields.at[0], fields.at[1]
    slots = sample.shape[2]
    me = lax.axis_index("gx")
    hb = lax.axis_index("ha")
    h_next = lax.rem(hb + 1, blocks)
    h_prev = lax.rem(hb + blocks - 1, blocks)
    h_side = (h_prev, h_next)
    has_prev = me > 0
    has_next = me < groups - 1
    base = 2
    in_base = me < base

    is_even = lax.rem(hb, 2) == 0
    upper_pair = hb >= blocks // 2
    mate_side = 1 - lax.rem(hb, 2)
    far_side = 1 - mate_side
    mate, far = (lax.rem(hb + blocks - 1 + 2 * s, blocks) for s in (mate_side, far_side))
    level = lax.div(me + 1, 2)
    mate_before = jnp.where(is_even, jnp.minimum(2 * level + 1, groups), jnp.maximum(2 * level - 1, base))
    far_before = jnp.where(
        upper_pair,
        jnp.minimum(2 * level + jnp.where(is_even, 3, 1), groups),
        jnp.maximum(2 * level - jnp.where(is_even, 1, 3), base),
    )
    earlier = me + mate_before + far_before

    def near_rows(before):
        return jnp.clip(me - 1, base, before), jnp.clip(me + 2, base, before)

    mate_near, far_near = near_rows(mate_before), near_rows(far_before)
    around = jnp.minimum(me + 2, groups) - jnp.maximum(me - 1, base)
    near_later = jnp.where(has_next, 1, 0) + 2 * around
    for low, high in (mate_near, far_near):
        near_later = near_later - (high - low)

    barrier = pltpu.get_barrier_semaphore()

    def signal(sem, j, h):
        pl.semaphore_signal(sem, inc=1, device_id=(j, h), device_id_type=MESH)

    def rows(lo, hi, body):
        lax.fori_loop(lo, hi, lambda j, carry: (body(j), carry)[1], 0)

    def signal_at(sem, h):
        return lambda j: signal(sem, j, h)

    def wait_some(sem, n):
        @pl.when(n > 0)
        def _():
            pl.semaphore_wait(sem, n)

    @pl.when(in_base)
    def _():
        for j in range(groups - 1, base - 1, -1):
            for h in (far, mate, hb):
                signal(barrier, j, h)

    @pl.when(jnp.logical_not(in_base))
    def _():
        for before, h in ((far_before, far), (mate_before, mate), (me + 1, hb)):
            rows(before, groups, lambda j: signal(barrier, groups - 1 + before - j, h))
        for j in range(base):
            for h in (far, mate, hb):
                signal(barrier, j, h)

    loads = [
        pltpu.make_async_copy(a, b, in_sem.at[i])
        for a, b, i in (
            (weight_h, sample.at[0], 0), (offy_h, sample.at[1], 0), (offs_h, sample.at[2], 0),
            (xy_h, cell.at[0], 0), (hs_h, cell.at[1], 0), (count_h, count, 1),
            (value_h, value, 2), (avoid_h, avoid, 2),
        )
    ]
    for load in loads:
        load.start()
    loaded = [pltpu.make_async_copy(r, r, in_sem.at[i]) for r, i in ((sample, 0), (count, 1), (fields, 2))]

    pay[0] = jnp.zeros(pay.shape[1:], jnp.float32)
    pay[groups + 1] = jnp.zeros(pay.shape[1:], jnp.float32)

    def copy(src, dst, send_sem, recv_sem, j, h):
        return pltpu.make_async_remote_copy(
            src, dst, send_sem, recv_sem, device_id=(j, h), device_id_type=MESH
        )

    def x_slot(side):
        return 6 + side * 5

    def h_halo(side, h):
        dst = halo.at[pl.ds(3 * (1 - side), 3)]
        copy(packed.at[side], dst, halo_send, halo_recv, me, h).start()

    def x_halo(side):
        at = x_slot(1 - side)
        copy(packed.at[2 + side], halo.at[at : at + 3], halo_send, halo_recv, me - 1 + 2 * side, hb).start()

    def corner_halo(side, h_to, h):
        at = x_slot(1 - side) + 4 - h_to
        copy(corner.at[side, h_to], halo.at[at], halo_send, halo_recv, me - 1 + 2 * side, h).start()

    def turn_of(j):
        turn = lax.rem(me - j - 1 + 2 * groups, groups)
        return 5 * turn, jnp.where(turn < groups - 1, lax.div(turn, 2), groups // 2)

    def send_side(j, side, h):
        at, sem = turn_of(j)
        copy(pay.at[j + 1], got.at[at + 4 - side], pay_send, pay_recv.at[sem], j, h).start()

    def send_own(j):
        at, sem = turn_of(j)
        copy(pay.at[pl.ds(j, 3)], got.at[pl.ds(at, 3)], pay_send, pay_recv.at[sem], j, hb).start()

    def send_mate(j):
        send_side(j, mate_side, mate)

    def send_far(j):
        send_side(j, far_side, far)

    def send_all(j):
        send_far(j)
        send_mate(j)
        send_own(j)

    loaded[0].wait()
    loaded[1].wait()
    owners = lax.broadcasted_iota(jnp.int32, (groups, groups), 0)
    lanes = lax.broadcasted_iota(jnp.int32, (groups, groups), 1)
    live = jnp.sum(
        jnp.where(owners == lanes, jnp.broadcast_to(count[...], (groups, groups)), 0).astype(jnp.float32),
        axis=1, keepdims=True,
    )
    slot = lax.broadcasted_iota(jnp.int32, (groups, slots), 1).astype(jnp.float32)
    w = jnp.where(slot < live, sample[0], 0.0)
    oy = sample[1]
    state = cell[1]
    head = lax.div(state, speeds)
    row = head * (cells * lines) + cell[0]
    pay[1 : groups + 1, 0, :] = w * (1.0 - oy)
    pay[1 : groups + 1, 1, :] = w * oy
    pay[1 : groups + 1, 2, :] = sample[2]
    pay[1 : groups + 1, 3, :] = (row * speeds + (state - head * speeds)).astype(jnp.float32)
    own_at = 5 * (groups - 1)
    pltpu.make_async_copy(
        pay.at[pl.ds(me, 3)], got.at[own_at : own_at + 3], pay_recv.at[groups // 2]
    ).start()
    loaded[2].wait()
    grid = [(h, x) for h in range(heads) for x in range(cells)]
    plane = {(i, h, x): fields[i, h, x] for i in range(2) for h, x in grid}
    whole = jnp.concatenate([plane[0, h, x] for h, x in grid], 1)
    mid = lines // 2
    for side, edge in ((0, 0), (1, 1)):
        h_edge, x_edge = edge * (heads - 1), edge * (cells - 1)
        over_h = [plane[1, h_edge, x] for x in range(cells)]
        over_x = [plane[1, h, x_edge] for h in range(heads)]
        h_tile = [p[:mid] for p in over_h] + [p[mid:] for p in over_h]
        x_tile = [q for p in over_x for q in (p[:mid], p[mid:])]
        for to, tile in ((side, h_tile), (2 + side, x_tile)):
            packed[to, 0] = whole[:mid]
            packed[to, 1] = whole[mid:]
            packed[to, 2] = jnp.concatenate(tile, 1)
        for h in range(2):
            p = plane[0, h * (heads - 1), x_edge]
            corner[side, h] = jnp.concatenate([p[:mid], p[mid:]] * 2, 1)

    @pl.when(jnp.logical_not(in_base))
    def _():
        pl.semaphore_wait(barrier, earlier)
        @pl.when(me == base)
        def _():
            for j in range(base):
                signal(row_in, j, hb)

        rows(base, me - 1, signal_at(late, hb))
        for (low, high), before, h in ((mate_near, mate_before, mate), (far_near, far_before, far)):
            rows(base, low, signal_at(late, h))
            rows(high, before, signal_at(late, h))
        for j in range(base):
            send_all(j)
        rows(jnp.maximum(me - 1, base), me, signal_at(late_near, hb))
        rows(*mate_near, signal_at(late_near, mate))
        rows(*far_near, signal_at(late_near, far))

        x_halo(0)
        others = ((mate_before, mate_side, mate), (far_before, far_side, far))

        def near_halos(comes):
            for before, side, h in others:
                pl.when(comes(me - 1, before))(functools.partial(corner_halo, 0, side, h))
                pl.when(comes(me, before))(functools.partial(h_halo, side, h))
                pl.when(comes(me + 1, before) & has_next)(functools.partial(corner_halo, 1, side, h))

        near_halos(lambda j, before: j < before)
        rows(base, me, send_own)
        rows(base, mate_before, send_mate)
        rows(base, far_before, send_far)

        wait_some(late_near, near_later)
        pl.when(has_next)(functools.partial(x_halo, 1))
        near_halos(lambda j, before: j >= before)
        wait_some(late, 3 * groups - 1 - earlier - near_later)
        for before, to in ((far_before, send_far), (mate_before, send_mate), (me + 1, send_own)):
            rows(before, groups, lambda j: to(groups - 1 + before - j))

    def x_and_corners(side):
        x_halo(side)
        for h in range(2):
            corner_halo(side, h, h_side[h])

    @pl.when(in_base)
    def _():
        pl.semaphore_wait(row_in, 1)
        for side in range(2):
            h_halo(side, h_side[side])
            send_side(me, side, h_side[side])
        for row in range(base):
            @pl.when(me == row)
            def _():
                x_and_corners(1 - row)
                send_all(1 - row)
        pl.semaphore_wait(barrier, 3 * (groups - base))
        pl.when(me == base - 1)(functools.partial(x_and_corners, 1))
        rows(base, groups, lambda j: send_all(groups - 1 + base - j))

    width = heads * cells * speeds
    half, quarter = width // 2, width // 4
    lane = lax.broadcasted_iota(jnp.int32, (1, width), 1)
    place = lax.div(lane, quarter)
    within = lax.rem(lane, quarter)
    even = lax.rem(place, 2) == 0
    left_half = place < 2
    total = heads * blocks
    angles = [np.float32(2.0 * math.pi / total) * np.float32(k) for k in range(total)]
    cosines = [float(np.cos(a)) for a in angles]
    sines = [float(np.sin(a)) for a in angles]
    speed = SLOWEST + SPEED_RANGE * within.astype(jnp.float32) / (speeds - 1)
    turn = [lax.rem(hb * heads + h + total, total) for h in range(-1, heads + 1)]
    cos_of = [pick(cosines, t) for t in turn]
    sin_of = [pick(sines, t) for t in turn]
    cx_own, cy_own = (jnp.where(left_half, a[1], a[2]) * speed for a in (cos_of, sin_of))
    cx_out, cy_out = (jnp.where(left_half, a[0], a[3]) * speed for a in (cos_of, sin_of))

    def shift(a, by):
        return pltpu.roll(a, by % width, 1)

    def forward(here, floor, cx, cy, h_up, h_down, x_up, x_down):
        up, down = upper(here, 0), lower(here, 0)
        rate = cy * (up - down) * 0.5 - (up - 2.0 * here + down) * 0.5
        up = jnp.where(within == quarter - 1, here, shift(here, -1))
        down = jnp.where(within == 0, here, shift(here, 1))
        slope = 0.5 * (up - down)
        size = smooth_abs(slope)
        s_slope = slope / size
        rate = rate + ACCELERATION * size - ACCELERATION * 0.5 * (up - 2.0 * here + down)
        slope = 0.5 * (h_up - h_down)
        size = smooth_abs(slope)
        h_slope = slope / size
        rate = rate + TURN_RATE * size - TURN_RATE * 0.5 * (h_up - 2.0 * here + h_down)
        rate = rate + cx * (x_up - x_down) * 0.5 - (x_up - 2.0 * here + x_down) * 0.5
        excess = SHARPNESS * (here - TIME_STEP * rate - floor)
        small = jnp.exp(-jnp.abs(excess))
        share = jnp.where(excess >= 0.0, 1.0, small) / (1.0 + small)
        pull = (0.5 * TURN_RATE) * share * h_slope
        keep = (0.5 * TURN_RATE) * share
        return excess, small, share, s_slope, pull - keep, -pull - keep

    def all_halos(sending):
        def wait(n):
            view = halo.at[0:n]
            c = copy(view, view, halo_send, halo_recv, me, h_next)
            c.wait_send() if sending else c.wait_recv()

        @pl.when(has_prev & has_next)
        def _():
            wait(16)

        @pl.when(jnp.logical_not(has_prev & has_next))
        def _():
            wait(11)

    def unpack(a):
        return {(h, x): a[:, n * speeds : (n + 1) * speeds] for n, (h, x) in enumerate(grid)}

    all_halos(False)
    def tall_pair(top, bottom):
        return jnp.concatenate([top, bottom], 0)

    own = whole
    floor = jnp.concatenate([plane[1, h, x] for h, x in grid], 1)
    hp, hn, xp, xn = (tall_pair(halo[i], halo[i + 1]) for i in (0, 3, 6, 11))
    hp_floor, hn_floor, xp_floor, xn_floor = (halo[i] for i in (2, 5, 8, 13))
    on_even, on_odd = [], []
    for i in (9, 10, 14, 15):
        tile = halo[i]
        other = shift(tile, quarter)
        on_even.append(tall_pair(tile, other))
        on_odd.append(tall_pair(other, tile))
    edge_h = shift(jnp.where(left_half, hn, hp), half)
    edge_x = jnp.where(even, shift(xp, -quarter), shift(xn, quarter))
    up_x = jnp.where(even, shift(own, -quarter), jnp.where(has_next, edge_x, own))
    down_x = jnp.where(even, jnp.where(has_prev, edge_x, own), shift(own, quarter))
    excess, small, share, s_slope, ahead, back = forward(
        own, floor, cx_own, cy_own,
        shift(jnp.where(left_half, hn, own), half), shift(jnp.where(left_half, own, hp), half),
        up_x, down_x,
    )
    next_v = unpack(floor + (jnp.maximum(excess, 0.0) + jnp.log1p(small)) / SHARPNESS)
    for h, x in grid:
        next_o[h, x] = next_v[h, x]
    rest = unpack(jnp.where(excess >= 0.0, small, 1.0) / (1.0 + small))
    share, s_slope, ahead, back = (unpack(a) for a in (share, s_slope, ahead, back))

    up_x = jnp.where(even, shift(edge_h, -quarter), jnp.where(left_half, on_odd[2], on_odd[3]))
    down_x = jnp.where(even, jnp.where(left_half, on_even[0], on_even[1]), shift(edge_h, quarter))
    edge_floor = tall_pair(
        jnp.where(left_half, hp_floor, shift(hn_floor, half)),
        jnp.where(left_half, shift(hp_floor, half), hn_floor),
    )
    out = forward(
        edge_h, edge_floor, cx_out, cy_out,
        jnp.where(left_half, own, hn), jnp.where(left_half, hp, own),
        jnp.where(even | has_next, up_x, edge_h), jnp.where(even & jnp.logical_not(has_prev), edge_h, down_x),
    )
    out = unpack(jnp.where(left_half, out[4], out[5]))
    for x in range(cells):
        ahead[-1, x], back[heads, x] = out[0, x], out[1, x]

    turned = shift(edge_x, half)
    up_h = jnp.where(left_half, turned, jnp.where(even, on_even[1], on_odd[3]))
    down_h = jnp.where(left_half, jnp.where(even, on_even[0], on_odd[2]), turned)
    edge_floor = tall_pair(
        jnp.where(even, xp_floor, shift(xn_floor, quarter)),
        jnp.where(even, shift(xp_floor, -quarter), xn_floor),
    )
    out = forward(
        edge_x, edge_floor, cx_own, cy_own,
        up_h, down_h, jnp.where(even, own, xn), jnp.where(even, xp, own),
    )
    out = unpack(out[2])
    for h in range(heads):
        share[h, -1], share[h, cells] = out[h, 0], out[h, 1]
    speed = SLOWEST + SPEED_RANGE * lax.broadcasted_iota(jnp.int32, (1, speeds), 1).astype(
        jnp.float32
    ) / (speeds - 1)
    cx = [cos_of[h + 1] * speed for h in range(heads)]
    cy = [sin_of[h + 1] * speed for h in range(heads)]

    span = cells * lines
    inside = lax.broadcasted_iota(jnp.int32, (heads * span, slots), 0)
    edge = lax.broadcasted_iota(jnp.int32, (heads * lines, slots), 0)
    edge = lax.div(edge, lines) * span + lax.rem(edge, lines)
    side_rows = lax.broadcasted_iota(jnp.int32, (span, slots), 0)
    ids = [
        i.astype(jnp.float32).astype(jnp.bfloat16)
        for i in (edge + (cells - 1) * lines, inside, edge, side_rows + (heads - 1) * span, side_rows)
    ]
    speed_id = lax.broadcasted_iota(jnp.int32, (speeds, slots), 0).astype(jnp.float32)
    speed_id = speed_id.astype(jnp.bfloat16)

    def tall(row, n):
        part = jnp.broadcast_to(row, (16, slots)).astype(jnp.bfloat16)
        return jnp.concatenate([part] * (n // 16), 0)

    def deposit(one, row_id):
        n = row_id.shape[0]
        weight0, weight1, up_s, code = one[0:1], one[1:2], one[2:3], one[3:4]
        row = jnp.floor(code * (1.0 / speeds))
        cell = code - row * speeds
        here, above_it = row_id == tall(row, n), row_id == tall(row + 1.0, n)
        zero = jnp.zeros(row_id.shape, jnp.bfloat16)
        high, low = [], []
        for f in (1.0 - up_s, up_s):
            a, b = weight0 * f, weight1 * f
            for part in (high, low):
                part.append(jnp.where(here, tall(a, n), jnp.where(above_it, tall(b, n), zero)))
                a, b = (t - t.astype(jnp.bfloat16).astype(jnp.float32) for t in (a, b))
        left = jnp.concatenate([jnp.concatenate(part, 1) for part in (high, low)], 0)
        one_hot = jnp.ones(speed_id.shape, jnp.bfloat16)
        right = jnp.concatenate(
            [
                jnp.where(speed_id == tall(c, speeds), one_hot, jnp.zeros_like(one_hot))
                for c in (cell, cell + 1.0)
            ],
            1,
        )
        both = lax.dot_general(
            left, right, (((1,), (1,)), ((), ())), preferred_element_type=jnp.float32
        )
        return both[:n] + both[n:]

    def collect(at, count, sem, sums):
        view = got.at[pl.ds(at, count)]
        copy(view, view, pay_send, pay_recv.at[sem], me, h_next).wait_recv()
        sums = list(sums)
        for i in range(count):
            sums[i % 5] = sums[i % 5] + deposit(got[at + i], ids[i % 5])
        return tuple(sums)

    sums = tuple(jnp.zeros((i.shape[0], speeds), jnp.float32) for i in ids)
    sums = lax.fori_loop(0, groups // 2 - 1, lambda n, so_far: collect(10 * n, 10, n, so_far), sums)
    sums = collect(own_at, 5, groups // 2, sums)
    sums = collect(own_at - 5, 5, groups // 2 - 1, sums)

    adj, c = {}, {}
    for n, (h, x) in enumerate(grid):
        adj[h, x] = sums[1][n * lines : (n + 1) * lines]
        c[h, x] = adj[h, x] * share[h, x]
    for h in range(heads):
        c[h, -1] = sums[0][h * lines : (h + 1) * lines] * share[h, -1]
        c[h, cells] = sums[2][h * lines : (h + 1) * lines] * share[h, cells]
    for x in range(cells):
        adj[-1, x] = sums[3][x * lines : (x + 1) * lines]
        adj[heads, x] = sums[4][x * lines : (x + 1) * lines]

    for h, x in grid:
        agrad_o[h, x] = adj[h, x] * rest[h, x]
        here = c[h, x]
        grad = spread((0.5 * cy[h] - 0.5) * here, (-0.5 * cy[h] - 0.5) * here, 0)
        pull = (0.5 * ACCELERATION) * here * s_slope[h, x]
        keep = (0.5 * ACCELERATION) * here
        grad = grad + spread(pull - keep, -pull - keep, 1)
        grad = grad + (2.0 + TURN_RATE + ACCELERATION) * here
        grad = grad + adj[h - 1, x] * ahead[h - 1, x] + adj[h + 1, x] * back[h + 1, x]
        low, high = 0.5 * cx[h] - 0.5, -0.5 * cx[h] - 0.5
        if x > 0:
            grad = grad + low * c[h, x - 1]
        else:
            grad = grad + jnp.where(has_prev, low * c[h, -1], high * here)
        if x < cells - 1:
            grad = grad + high * c[h, x + 1]
        else:
            grad = grad + jnp.where(has_next, high * c[h, cells], low * here)
        vgrad_o[h, x] = here - TIME_STEP * grad

    all_halos(True)
    view = got.at[0 : 5 * groups - 3]
    copy(view, view, pay_send, pay_recv.at[0], me, h_next).wait_send()


def write_out(next_v, vgrad_v, agrad_v, next_o, vgrad_o, agrad_o, sem):
    copies = [
        pltpu.make_async_copy(a, b, sem.at[i])
        for i, (a, b) in enumerate(((next_v, next_o), (vgrad_v, vgrad_o), (agrad_v, agrad_o)))
    ]
    for copy in copies:
        copy.start()
    for copy in copies:
        copy.wait()


def on_device(groups, blocks, value, avoid, weight, offy, offs, xy, hs, count):
    slots = weight.shape[3]
    value = jnp.transpose(value, (0, 2, 3, 1))
    avoid = jnp.transpose(avoid, (0, 2, 3, 1))
    weight, offy, offs, xy, hs = (a.reshape(groups, slots) for a in (weight, offy, offs, xy, hs))
    count = count.reshape(1, groups)
    heads, cells, lines, speeds = value.shape
    f32 = jnp.float32
    dma = pltpu.SemaphoreType.DMA
    field = pltpu.VMEM(value.shape, f32)
    x_pair = pltpu.VMEM((2, heads, lines, speeds), f32)
    h_pair = pltpu.VMEM((2, cells, lines, speeds), f32)
    near = groups in (4, 8) and blocks == 4 and heads == cells == 2 and 4 * speeds == slots == 128 and lines == 16
    sample = pltpu.VMEM((groups, slots), f32)
    index = pltpu.VMEM((groups, slots), jnp.int32)
    counts = pltpu.VMEM((1, groups), jnp.int32)
    if near:
        scratch = [
            pltpu.VMEM((2, *value.shape), f32),
            pltpu.VMEM((5, groups, slots), f32), pltpu.VMEM((2, groups, slots), jnp.int32), counts,
            pltpu.VMEM((groups + 2, 4, slots), f32), pltpu.VMEM((5 * groups, 4, slots), f32),
            pltpu.VMEM((4, 3, lines // 2, slots), f32), pltpu.VMEM((2, 2, lines // 2, slots), f32),
            pltpu.VMEM((16, lines // 2, slots), f32),
            dma((3,)), dma, dma((groups // 2 + 1,)), dma, dma,
            *[pltpu.SemaphoreType.REGULAR] * 3,
        ]
    else:
        scratch = [
            field, field, sample, sample, sample, index, index, counts,
            pltpu.VMEM((groups, ROWS, slots), f32), pltpu.VMEM((groups, ROWS, slots), f32),
            x_pair, h_pair, field, h_pair, x_pair, h_pair,
            dma((8,)), dma((groups,)), dma((groups,)), *[dma((2,))] * 8, dma,
        ]
    outs = pl.pallas_call(
        functools.partial(near_kernel if near else kernel, groups, blocks),
        out_shape=[pltpu.VMEM(value.shape, f32)] * 3,
        in_specs=[pl.BlockSpec(memory_space=pltpu.HBM)] * 8,
        out_specs=[pl.BlockSpec(memory_space=pltpu.VMEM)] * 3,
        scratch_shapes=scratch,
        compiler_params=pltpu.CompilerParams(collective_id=0, has_side_effects=True),
        name="step",
    )(value, avoid, weight, offy, offs, xy, hs, count)
    outs = pl.pallas_call(
        write_out,
        out_shape=[jax.ShapeDtypeStruct(value.shape, f32)] * 3,
        in_specs=[pl.BlockSpec(memory_space=pl.ANY)] * 3,
        out_specs=[pl.BlockSpec(memory_space=pl.ANY)] * 3,
        scratch_shapes=[dma((3,))],
        compiler_params=pltpu.CompilerParams(vmem_limit_bytes=1 << 20),
        name="write_out",
    )(*outs)
    return tuple(jnp.transpose(o, (0, 3, 1, 2)) for o in outs)


def solution(mesh):
    field = P("ha", None, "gx", None)
    sample = P("gx", "ha", None, None)
    return jax.shard_map(
        functools.partial(on_device, mesh.shape["gx"], mesh.shape["ha"]),
        mesh=mesh,
        in_specs=(field, field, sample, sample, sample, sample, sample, P("gx", "ha", None)),
        out_specs=(field, field, field),
        check_vma=False,
    )
```
